32 devices in a mesh: dp: 8 (over z, y), shard: 4 (over x, core).
Axes of the slice: x: 2, y: 2, z: 4, core: 2. Of those that a mesh axis runs over, the one named last changes fastest.
Arguments:
- tokens: bfloat16 [4096, 768], P(('dp', 'shard')), may hold values from -6 to 6
- cotangent: bfloat16 [4096, 768], P(('dp', 'shard')), may hold values from -6 to 6
- seq_ids: int32 [4096], P(('dp', 'shard')), may hold values from -1 to 127, as said below
- params: float32 [3768320], P(('dp', 'shard')), as said below
- first_moment: float32 [3768320], P(('dp', 'shard')), may hold values from -60 to 60
- second_moment: float32 [3768320], P(('dp', 'shard')), may hold values from 1 to 20
- step_count: int32 [1], replicated, may hold values from 1 to 20
Outputs:
- block_out: bfloat16 [4096, 768], P(('dp', 'shard'))
- grad_input: float32 [4096, 768], P(('dp', 'shard'))
- weight_grads: float32 [3768320], P(('dp', 'shard'))
- new_params: float32 [3768320], P(('dp', 'shard'))
- new_first_moment: float32 [3768320], P(('dp', 'shard'))
- new_second_moment: float32 [3768320], P(('dp', 'shard'))
The draws below stay inside these ranges and needn't reach their ends.
Inputs may be any that keep to these rules, and one draw needn't show every extreme that they name: `seq_ids`: numbering restarts on every device's 128 slots: a device's first slot starts a sequence, consecutive equal numbers form one sequence, live slots come first and the remaining ones are -1. A sequence has at most 128 slots; some device holds exactly one such sequence, and some device has every slot live as a sequence of its own. `params`: entries are laid out as in the first step of the statement.
All inputs are finite; a program needn't handle non-finite values.
Results may differ from the reference program's by a relative error of at most 0.01.
Values may be sent and summed in bfloat16 or wider, within the bound.
A program may use at most 128 MiB of HBM per device.

```python
import math
import jax
import jax.numpy as jnp
from jax import lax

D = 768
HEADS = 24
HEAD_DIM = 64
STATE = 128
KERNEL = 4
STRETCH = 128
TOK_DEV = 128
INNER = 1536
CHANNELS = 1792
PRAW = 3765320
PTOTAL = 3768320
TOKENS = 4096


def draw_seq_ids(key, part):
    blocks = TOKENS // TOK_DEV
    key_live, key_full, key_cut = jax.random.split(key, 3)
    live = jax.random.randint(key_live, (blocks,), TOK_DEV // 4, TOK_DEV + 1)
    chosen = jax.random.randint(key_full, (), 0, blocks)
    half_block = (chosen + 1) % blocks
    single_block = (chosen + 2) % blocks
    block_index = jnp.arange(blocks, dtype=jnp.int32)
    live = jnp.where(block_index == half_block, TOK_DEV // 2, live)
    live = jnp.where(block_index == single_block, TOK_DEV, live)
    live = jnp.where(block_index == chosen, TOK_DEV, live)
    spacing = max(TOK_DEV // 3, 2)
    cuts = (jax.random.randint(key_cut, (blocks, TOK_DEV), 0, spacing) == 0).astype(jnp.int32)
    position = jnp.arange(TOK_DEV, dtype=jnp.int32)
    cuts = jnp.where(position[None, :] == 0, 1, cuts)
    cuts = jnp.where((block_index == single_block)[:, None], 1, cuts)
    cuts = jnp.where((block_index == chosen)[:, None] & (position[None, :] > 0), 0, cuts)
    local_ids = jnp.cumsum(cuts, axis=1) - 1
    local_ids = jnp.where(position[None, :] < live[:, None], local_ids, -1)
    return local_ids.reshape(TOKENS).astype(jnp.int32)


def draw_params(key, part):
    keys = jax.random.split(key, 11)
    main_noise = jax.random.normal(keys[1], (D * (INNER + CHANNELS),), jnp.float32)
    dt_noise = jax.random.normal(keys[2], (D * HEADS,), jnp.float32)
    out_noise = jax.random.normal(keys[9], (INNER * D,), jnp.float32)
    gain_in = jax.random.uniform(keys[0], (D,), jnp.float32, 0.5, 1.5)
    w_main = main_noise * D ** (-0.5)
    w_dt = dt_noise * D ** (-0.5)
    conv_w = jax.random.uniform(keys[3], (KERNEL * CHANNELS,), jnp.float32, -0.6, 0.6)
    conv_b = jax.random.uniform(keys[4], (CHANNELS,), jnp.float32, -0.5, 0.5)
    dt_start = jnp.exp(jax.random.uniform(keys[5], (HEADS,), jnp.float32, -6.9077553, -2.3025851))
    dt_bias = jnp.log(jnp.expm1(dt_start))
    a_log = jax.random.uniform(keys[6], (HEADS,), jnp.float32, 0.0, 2.7725887)
    d_skip = jax.random.uniform(keys[7], (HEADS,), jnp.float32, 0.5, 1.5)
    gain_out = jax.random.uniform(keys[8], (INNER,), jnp.float32, 0.5, 1.5)
    w_out = out_noise * INNER ** (-0.5)
    unused = jax.random.normal(keys[10], (PTOTAL - PRAW,), jnp.float32) * 0.02
    return jnp.concatenate([gain_in, w_main, w_dt, conv_w, conv_b, dt_bias, a_log, d_skip, gain_out, w_out, unused])


def level_of(key, extent, cuts, least, largest):
    loudness = 1.0
    for dim, parts in cuts:
        steps = jax.random.uniform(jax.random.fold_in(jax.random.fold_in(key, 6), dim), (parts,), jnp.float32, least / len(cuts), largest / len(cuts))
        loudness = loudness * jnp.repeat(jnp.exp(steps), extent[dim] // parts).reshape((-1,) + (1,) * (len(extent) - 1 - dim))
    return loudness


def centred(rng, extent, scale, reach, cuts=(), kind=jnp.bfloat16):
    factor_of = level_of(rng, extent, cuts, -0.22, 0.18) if cuts else 1.0
    array = jax.random.normal(rng, extent, jnp.float32) * scale * factor_of
    return jnp.minimum(jnp.maximum(array, -reach), reach).astype(kind)


def setup_inputs(seed: int = 0) -> dict:
    streams_of = jax.random.split(jax.random.key(seed), 8)
    tokens = centred(streams_of[0], (TOKENS, D), 1.0, 6.0, ((0, 32),))
    cotangent = centred(streams_of[1], (TOKENS, D), 1.0, 6.0, ((0, 32),))
    seq_ids = draw_seq_ids(jax.random.fold_in(streams_of[7], 71), 0)
    params = draw_params(jax.random.fold_in(streams_of[7], 71), 0)
    first_moment = centred(streams_of[4], (PTOTAL,), 10.0, 60.0, ((0, 32),), jnp.float32)
    second_moment = jnp.clip(jnp.exp(math.log(20.0) - 2.9957323 * jax.random.uniform(streams_of[5], (PTOTAL,), jnp.float32) ** level_of(streams_of[5], (PTOTAL,), ((0, 32),), -0.2, 0.2)), 1.0, 20.0)
    step_count = jax.random.randint(streams_of[6], (1,), 1, 21).astype(jnp.int32)
    return {"tokens": tokens, "cotangent": cotangent, "seq_ids": seq_ids, "params": params, "first_moment": first_moment, "second_moment": second_moment, "step_count": step_count}


EPS = 1e-05
BETA_ONE = 0.9
BETA_TWO = 0.999
ADAM_EPS = 1e-08
LEARN_RATE = 0.01
WEIGHT_DECAY = 0.1

def matmul(left, right):
    return jnp.dot(left, right, preferred_element_type=jnp.float32)

def over_rows(left, right):
    return lax.dot_general(left, right, (((0,), (0,)), ((), ())), preferred_element_type=jnp.float32)

def against(left, right):
    return lax.dot_general(left, right, (((1,), (1,)), ((), ())), preferred_element_type=jnp.float32)

def unpack(flat):
    shapes = [(D,), (D, INNER + CHANNELS), (D, HEADS), (KERNEL, CHANNELS), (CHANNELS,), (HEADS,), (HEADS,), (HEADS,), (INNER,), (INNER, D)]
    pieces = []
    offset = 0
    for shape in shapes:
        length = math.prod(shape)
        pieces.append(flat[offset:offset + length].reshape(shape))
        offset = offset + length
    return pieces

def pack(pieces, total):
    flat = jnp.concatenate([piece.reshape(-1) for piece in pieces])
    return jnp.concatenate([flat, jnp.zeros((total - flat.shape[0],), flat.dtype)])

def norm_in(inputs, gain):
    scale = lax.rsqrt(lax.optimization_barrier(jnp.mean(inputs * inputs, axis=-1, keepdims=True)) + EPS)
    return inputs * scale * gain

def lag_masks(seq_ids):
    padded = jnp.concatenate([jnp.full((KERNEL - 1,), -3, jnp.int32), seq_ids.astype(jnp.int32)])
    masks = []
    for lag in range(1, KERNEL):
        earlier = padded[KERNEL - 1 - lag:KERNEL - 1 - lag + seq_ids.shape[0]]
        masks.append((earlier == seq_ids).astype(jnp.float32)[:, None])
    return masks

def state_space(values, bmat, cmat, steps_dt, rate, seq_ids):
    rows = values.shape[0]
    number = rows // STRETCH
    seg_blocks = seq_ids.astype(jnp.int32).reshape(number, STRETCH)
    before = jnp.concatenate([jnp.full((1,), -3, jnp.int32), seg_blocks[:-1, -1]])
    places = jnp.arange(STRETCH, dtype=jnp.int32)
    lower = places[:, None] >= places[None, :]

    def advance(state, pieces):
        x_block, b_block, c_block, dt_block, seg_block, prior = pieces
        logs = jnp.cumsum(dt_block * rate, axis=0)
        same = lower & (seg_block[:, None] == seg_block[None, :])
        spans = logs.T[:, :, None] - logs.T[:, None, :]
        factor = jnp.exp(jnp.where(same[None], spans, -1e+30))
        scores = jnp.dot(c_block, b_block.T, precision=lax.Precision.HIGHEST)
        mixing = factor * scores[None] * dt_block.T[:, None, :]
        inside = jnp.einsum('htu,uhp->thp', mixing, x_block, precision=lax.Precision.HIGHEST)
        entering = jnp.exp(logs) * (seg_block == prior).astype(logs.dtype)[:, None]
        carried = jnp.einsum('tn,hnp->thp', c_block, state, precision=lax.Precision.HIGHEST) * entering[:, :, None]
        tail_mask = (seg_block == seg_block[-1]).astype(logs.dtype)[:, None]
        towards = jnp.exp(logs[-1][None, :] - logs) * dt_block * tail_mask
        fresh = jnp.einsum('th,tn,thp->hnp', towards, b_block, x_block, precision=lax.Precision.HIGHEST)
        kept = jnp.exp(logs[-1]) * (seg_block[-1] == prior).astype(logs.dtype)
        return (fresh + kept[:, None, None] * state, inside + carried)
    initial = jnp.zeros((HEADS, STATE, HEAD_DIM), values.dtype)
    inputs = (values.reshape(number, STRETCH, HEADS, HEAD_DIM), bmat.reshape(number, STRETCH, STATE), cmat.reshape(number, STRETCH, STATE), steps_dt.reshape(number, STRETCH, HEADS), seg_blocks, before)
    final_state, outputs = lax.scan(advance, initial, inputs)
    return outputs.reshape(rows, HEADS, HEAD_DIM)

def mixer(proj, dt_raw, conv_weight, conv_bias, dt_bias, a_log, d_skip, gain_out, lag_list, seq_ids):
    rows = proj.shape[0]
    gate = proj[:, :INNER]
    conv_in = proj[:, INNER:]
    convolved = conv_bias + conv_weight[KERNEL - 1] * conv_in
    for lag in range(1, KERNEL):
        shifted = jnp.concatenate([jnp.zeros((lag, conv_in.shape[1]), conv_in.dtype), conv_in[:-lag]])
        convolved = convolved + conv_weight[KERNEL - 1 - lag] * shifted * lag_list[lag - 1]
    active = jax.nn.silu(convolved)
    values = active[:, :INNER].reshape(rows, HEADS, HEAD_DIM)
    bmat = active[:, INNER:INNER + STATE]
    cmat = active[:, INNER + STATE:]
    steps_dt = jax.nn.softplus(dt_raw + dt_bias)
    scanned = state_space(values, bmat, cmat, steps_dt, -jnp.exp(a_log), seq_ids)
    scanned = scanned + d_skip[None, :, None] * values
    gated = scanned.reshape(rows, INNER) * jax.nn.silu(gate)
    scale = lax.rsqrt(lax.optimization_barrier(jnp.mean(gated * gated, axis=-1, keepdims=True)) + EPS)
    return gated * scale * gain_out

def block_pass(tokens, cotangent, seq_ids, weights, total):
    gain_in, w_main, w_dt, conv_w, conv_b, dt_bias, a_log, d_skip, gain_out, w_out = weights
    small = [piece.astype(jnp.float32) for piece in (conv_w, conv_b, dt_bias, a_log, d_skip, gain_out)]
    inputs = tokens.astype(jnp.float32)
    normed_full, norm_back = jax.vjp(norm_in, inputs, gain_in.astype(jnp.float32))
    normed = normed_full.astype(jnp.bfloat16)
    proj = matmul(normed, w_main)
    dt_raw = matmul(normed, w_dt)
    masks = lag_masks(seq_ids)
    mixed_full, mixer_back = jax.vjp(partial_mixer(masks, seq_ids), proj, dt_raw, *small)
    hidden = mixed_full.astype(jnp.bfloat16)
    result = (inputs + matmul(hidden, w_out)).astype(jnp.bfloat16)
    live_cot = jnp.where(seq_ids[:, None] >= 0, cotangent, jnp.zeros_like(cotangent))
    grad_w_out = over_rows(hidden, live_cot)
    grad_hidden = against(live_cot, w_out)
    backward = mixer_back(grad_hidden)
    grad_proj = backward[0].astype(jnp.bfloat16)
    grad_dt = backward[1].astype(jnp.bfloat16)
    grad_w_main = over_rows(normed, grad_proj)
    grad_w_dt = over_rows(normed, grad_dt)
    grad_normed = against(grad_proj, w_main) + against(grad_dt, w_dt)
    grad_x, grad_gain = norm_back(grad_normed)
    grad_input = live_cot.astype(jnp.float32) + grad_x
    flat = pack([grad_gain, grad_w_main, grad_w_dt] + list(backward[2:]) + [grad_w_out], total)
    return (result, grad_input, flat)

def partial_mixer(masks, seq_ids):

    def apply_mixer(proj, dt_raw, conv_weight, conv_bias, dt_bias, a_log, d_skip, gain_out):
        return mixer(proj, dt_raw, conv_weight, conv_bias, dt_bias, a_log, d_skip, gain_out, masks, seq_ids)
    return apply_mixer

def adamw(weight, first, second, grad, step_count):
    steps_done = step_count[0].astype(jnp.float32)
    first_new = BETA_ONE * first + (1.0 - BETA_ONE) * grad
    second_new = BETA_TWO * second + (1.0 - BETA_TWO) * grad * grad
    first_hat = first_new / (1.0 - jnp.power(BETA_ONE, steps_done))
    second_hat = second_new / (1.0 - jnp.power(BETA_TWO, steps_done))
    weight_new = weight - LEARN_RATE * (first_hat / (jnp.sqrt(second_hat) + ADAM_EPS) + WEIGHT_DECAY * weight)
    return (weight_new, first_new, second_new)

def reference(tokens, cotangent, seq_ids, params, first_moment, second_moment, step_count):
    weights = unpack(params.astype(jnp.bfloat16))
    blocks = TOKENS // TOK_DEV

    def one_block(summed, pieces):
        token_block, cot_block, seg_block = pieces
        result, grad_input, flat = block_pass(token_block, cot_block, seg_block, weights, PTOTAL)
        return (summed + flat, (result, grad_input))
    start_sum = jnp.zeros((PTOTAL,), jnp.float32)
    summed, (results, grads_in) = lax.scan(one_block, start_sum, (tokens.reshape(blocks, TOK_DEV, D), cotangent.reshape(blocks, TOK_DEV, D), seq_ids.reshape(blocks, TOK_DEV)))
    new_weight, new_first, new_second = adamw(params, first_moment, second_moment, summed, step_count)
    return (results.reshape(TOKENS, D), grads_in.reshape(TOKENS, D), summed, new_weight, new_first, new_second)
```

```python
import functools
import math

import jax
import jax.numpy as jnp
from jax import lax
from jax.experimental import pallas as pl
from jax.experimental.pallas import tpu as pltpu
from jax.sharding import PartitionSpec as P

D = 768
HEADS = 24
HEAD_DIM = 64
STATE = 128
KERNEL = 4
STRETCH = 128
INNER = 1536
CHANNELS = 1792
LANES = 128
CUTS = 8
LAG = 2
SPAN = 256
MESH = pl.DeviceIdType.MESH
PACKED = D + D * (INNER + CHANNELS) + D * HEADS + (KERNEL + 1) * CHANNELS + 3 * HEADS + INNER + INNER * D


EPS = 1e-05
BETA_ONE = 0.9
BETA_TWO = 0.999
ADAM_EPS = 1e-08
LEARN_RATE = 0.01
WEIGHT_DECAY = 0.1


def matmul(left, right):
    return jnp.dot(left, right, preferred_element_type=jnp.float32)


def over_rows(left, right):
    return lax.dot_general(
        left, right, (((0,), (0,)), ((), ())), preferred_element_type=jnp.float32
    )


def against(left, right):
    return lax.dot_general(
        left, right, (((1,), (1,)), ((), ())), preferred_element_type=jnp.float32
    )


ROWS_GAIN = D // LANES
ROWS_MAIN = D * (INNER + CHANNELS) // LANES
START_SMALL = ROWS_GAIN + ROWS_MAIN
START_OUT = (PACKED - INNER * D) // LANES
SHIFT = (PACKED - INNER * D) % LANES
ROWS_OUT = INNER * D // LANES
ROWS_SMALL = START_OUT + 1 - START_SMALL
WIDE = (INNER + CHANNELS) // LANES
THIN = D // LANES


def in_spans(total, body):
    def step(number, carry):
        body(pl.multiple_of(number * SPAN, SPAN), SPAN)
        return carry

    whole = total // SPAN
    lax.fori_loop(0, whole, step, 0)
    if total % SPAN:
        body(whole * SPAN, total - whole * SPAN)


def pack_kernel(gain_ref, small_ref, normed_ref, proj_ref, hidden_ref, cot_ref, out_ref, main, tail):
    main[0:ROWS_GAIN, :] = gain_ref[...]
    main[START_SMALL : START_OUT, :] = small_ref[0 : ROWS_SMALL - 1, :]
    tail[7:8, :] = small_ref[ROWS_SMALL - 1 : ROWS_SMALL, :]
    tail[8 + ROWS_OUT :, :] = jnp.zeros((tail.shape[0] - 8 - ROWS_OUT, LANES), jnp.float32)
    for pair in range(WIDE // 2):
        both = over_rows(normed_ref[...], proj_ref[:, pair * 2 * LANES : (pair + 1) * 2 * LANES])
        for side in range(2):
            main[pl.ds(ROWS_GAIN + 2 * pair + side, D, stride=WIDE), :] = both[
                :, side * LANES : (side + 1) * LANES
            ]
    for pair in range(THIN // 2):
        both = over_rows(hidden_ref[...], cot_ref[:, pair * 2 * LANES : (pair + 1) * 2 * LANES])
        for side in range(2):
            part = pltpu.roll(both[:, side * LANES : (side + 1) * LANES], SHIFT, 1)
            tail[pl.ds(8 + 2 * pair + side, INNER, stride=THIN), :] = part
    edge = START_OUT // 16 * 16

    def cast_main(place, size):
        out_ref[pl.ds(place, size), :] = main[pl.ds(place, size), :].astype(jnp.bfloat16)

    in_spans(edge, cast_main)
    early = lax.broadcasted_iota(jnp.int32, (8, LANES), 1) < SHIFT
    seam = jnp.where(early, tail[7:15, :], tail[8:16, :])
    out_ref[edge : edge + 16, :] = jnp.concatenate([main[edge : edge + 8, :], seam], 0).astype(
        jnp.bfloat16
    )

    def cast_tail(place, size):
        block = tail[pl.ds(place + 16, size), :]
        before = tail[pl.ds(place + 8, size), :]
        joined = jnp.concatenate([before[7:8], block[: size - 1]], 0)
        lanes = lax.broadcasted_iota(jnp.int32, (size, LANES), 1)
        out_ref[pl.ds(edge + 16 + place, size), :] = jnp.where(
            lanes < SHIFT, joined, block
        ).astype(jnp.bfloat16)

    in_spans(out_ref.shape[0] - edge - 16, cast_tail)


def pack_all(gain, small, normed, proj, hidden, cot, rows):
    vmem = pl.BlockSpec(memory_space=pltpu.VMEM)
    return pl.pallas_call(
        pack_kernel,
        out_shape=jax.ShapeDtypeStruct((rows, LANES), jnp.bfloat16),
        in_specs=[vmem] * 6,
        out_specs=vmem,
        scratch_shapes=[
            pltpu.VMEM((START_OUT, LANES), jnp.float32),
            pltpu.VMEM((rows - START_OUT + 16, LANES), jnp.float32),
        ],
        compiler_params=pltpu.CompilerParams(vmem_limit_bytes=48 * 1024 * 1024),
    )(gain, small, normed, proj, hidden, cot)


def in_waves(stages, count):
    for wave in range(count + LAG * (len(stages) - 1)):
        for number, stage in enumerate(stages):
            if 0 <= wave - LAG * number < count:
                stage(wave - LAG * number)


def scatter_kernel(grid, cuts, data, out, send_sem, recv_sem, *refs):
    deep, tall, wide = grid
    dp, shard = lax.axis_index("dp"), lax.axis_index("shard")
    z, y = lax.div(dp, tall), lax.rem(dp, tall)
    x, c = lax.div(shard, 2), lax.rem(shard, 2)

    def place(z, y, x, c):
        return (z * tall + y, x * 2 + c)

    xs = [lax.rem(x + j, wide) for j in range(1, wide)]
    ys = [lax.rem(y + j, tall) for j in range(1, tall)]
    zs = [lax.rem(z + j, deep) for j in range(1, deep)]
    to_x = [place(z, y, p, c) for p in xs]
    to_y = [place(z, p, x, c) for p in ys]
    to_z = [place(p, y, x, c) for p in zs]
    partner = place(z, y, x, 1 - c)
    everyone = [partner] + to_x + to_y + to_z
    barrier = pltpu.get_barrier_semaphore()
    for peer in everyone:
        pl.semaphore_signal(barrier, inc=1, device_id=peer, device_id_type=MESH)
    pl.semaphore_wait(barrier, len(everyone))

    sent = []

    def push(chunk, number, src, dst, peer):
        copy = pltpu.make_async_remote_copy(
            src_ref=src,
            dst_ref=dst,
            send_sem=send_sem.at[chunk, number],
            recv_sem=recv_sem.at[chunk, number],
            device_id=peer,
            device_id_type=MESH,
        )
        copy.start()
        sent.append(copy)
        return copy

    def total(parts):
        value = parts[0].astype(jnp.float32)
        for part in parts[1:]:
            value = value + part.astype(jnp.float32)
        return value

    first_x, first_y, first_z = 1, wide, wide + tall - 1
    chunks = [refs[i * 7 : i * 7 + 7] for i in range(len(cuts))]
    flights = []
    for k, (start, size) in enumerate(cuts):
        src = data.at[:, :, :, 1 - c, start : start + size]
        flights.append([push(k, 0, src, chunks[k][0], partner)])
    def stage_one(k):
        start, size = cuts[k]
        got, acc, got_one = chunks[k][:3]
        for copy in flights[k]:
            copy.wait_recv()

        def add(step, carry):
            zi, rest = lax.div(step, tall * wide), lax.rem(step, tall * wide)
            yi, xi = lax.div(rest, wide), lax.rem(rest, wide)
            mine = data[zi, yi, xi, c, start : start + size, :]
            acc[zi, yi, xi] = total([mine, got[zi, yi, xi]]).astype(jnp.bfloat16)
            return carry

        lax.fori_loop(0, deep * tall * wide, add, 0)
        flights[k] = []
        if k % 2 == 0:
            for j, p in enumerate(xs):
                flights[k].append(push(k, first_x + j, acc.at[:, :, p], got_one.at[j], to_x[j]))
        else:
            for j, p in enumerate(ys):
                flights[k].append(push(k, first_y + j, acc.at[:, p], got_one.at[j], to_y[j]))
    def stage_two(k):
        start, size = cuts[k]
        got, acc, got_one, acc_two, got_two = chunks[k][:5]
        for copy in flights[k]:
            copy.wait_recv()
        other = tall if k % 2 == 0 else wide

        def add(step, carry):
            zi, oi = lax.div(step, other), lax.rem(step, other)
            mine = acc[zi, oi, x] if k % 2 == 0 else acc[zi, y, oi]
            parts = [mine] + [got_one[j, zi, oi] for j in range(got_one.shape[0])]
            acc_two[zi, oi] = total(parts).astype(jnp.bfloat16)
            return carry

        lax.fori_loop(0, deep * other, add, 0)
        flights[k] = []
        if k % 2 == 0:
            for j, p in enumerate(ys):
                flights[k].append(push(k, first_y + j, acc_two.at[:, p], got_two.at[j], to_y[j]))
        else:
            for j, p in enumerate(xs):
                flights[k].append(push(k, first_x + j, acc_two.at[:, p], got_two.at[j], to_x[j]))
    def stage_three(k):
        start, size = cuts[k]
        acc_two, got_two, acc_three, got_three = chunks[k][3:]
        for copy in flights[k]:
            copy.wait_recv()
        mine = y if k % 2 == 0 else x

        def add(zi, carry):
            parts = [acc_two[zi, mine]] + [got_two[j, zi] for j in range(got_two.shape[0])]
            acc_three[zi] = total(parts).astype(jnp.bfloat16)
            return carry

        lax.fori_loop(0, deep, add, 0)
        flights[k] = []
        for j, p in enumerate(zs):
            flights[k].append(push(k, first_z + j, acc_three.at[p], got_three.at[j], to_z[j]))
    def stage_four(k):
        start, size = cuts[k]
        acc_three, got_three = chunks[k][5:]
        for copy in flights[k]:
            copy.wait_recv()
        parts = [acc_three[z]] + [got_three[j] for j in range(deep - 1)]
        out[start : start + size, :] = total(parts)

    in_waves((stage_one, stage_two, stage_three, stage_four), len(cuts))
    for copy in sent:
        copy.wait_send()


def scatter_sum(flat, group_count, wide_count, rows):
    wide = group_count // 2
    tall = wide if wide_count % wide == 0 else 1
    deep = wide_count // tall
    step = -(-rows // (CUTS * 16)) * 16
    cuts = [(start, min(step, rows - start)) for start in range(0, rows, step)]
    scratch = []
    for k, (start, size) in enumerate(cuts):
        lead, other = (wide, tall) if k % 2 == 0 else (tall, wide)
        for shape in (
            (deep, tall, wide),
            (deep, tall, wide),
            (lead - 1, deep, other),
            (deep, other),
            (other - 1, deep),
            (deep,),
            (deep - 1,),
        ):
            scratch.append(pltpu.VMEM((*shape, size, LANES), jnp.bfloat16))
    peers = wide + tall + deep - 2
    sems = pltpu.SemaphoreType.DMA((len(cuts), peers))
    vmem = pl.BlockSpec(memory_space=pltpu.VMEM)
    return pl.pallas_call(
        functools.partial(scatter_kernel, (deep, tall, wide), cuts),
        out_shape=jax.ShapeDtypeStruct((rows, LANES), jnp.float32),
        in_specs=[vmem],
        out_specs=vmem,
        scratch_shapes=[sems, sems] + scratch,
        compiler_params=pltpu.CompilerParams(
            collective_id=0, has_side_effects=True, vmem_limit_bytes=56 * 1024 * 1024
        ),
    )(flat.reshape(deep, tall, wide, 2, rows, LANES))


def gather_kernel(grid, cuts, own, out, send_sem, recv_sem):
    deep, tall, wide = grid
    dp, shard = lax.axis_index("dp"), lax.axis_index("shard")
    z, y = lax.div(dp, tall), lax.rem(dp, tall)
    x, c = lax.div(shard, 2), lax.rem(shard, 2)

    def place(z, y, x, c):
        return (z * tall + y, x * 2 + c)

    to_x = [place(z, y, lax.rem(x + j, wide), c) for j in range(1, wide)]
    to_y = [place(z, lax.rem(y + j, tall), x, c) for j in range(1, tall)]
    to_z = [place(lax.rem(z + j, deep), y, x, c) for j in range(1, deep)]
    partner = place(z, y, x, 1 - c)
    everyone = [partner] + to_x + to_y + to_z
    barrier = pltpu.get_barrier_semaphore()
    for peer in everyone:
        pl.semaphore_signal(barrier, inc=1, device_id=peer, device_id_type=MESH)
    pl.semaphore_wait(barrier, len(everyone))

    sent = []

    def push(chunk, number, src, dst, peers):
        started = []
        for j, peer in enumerate(peers):
            copy = pltpu.make_async_remote_copy(
                src_ref=src,
                dst_ref=dst,
                send_sem=send_sem.at[chunk, number + j],
                recv_sem=recv_sem.at[chunk, number + j],
                device_id=peer,
                device_id_type=MESH,
            )
            copy.start()
            started.append(copy)
        sent.extend(started)
        return started

    first_x, first_y, first_z = 1, wide, wide + tall - 1
    flights = []
    for k, (start, size) in enumerate(cuts):
        rows = pl.ds(start, size)
        flights.append(push(k, first_z, own.at[rows], out.at[z, y, x, c, rows], to_z))
    out[z, y, x, c] = own[...]
    def stage_one(k):
        start, size = cuts[k]
        rows = pl.ds(start, size)
        for copy in flights[k]:
            copy.wait_recv()
        line = out.at[:, y, x, c, rows]
        if k % 2 == 0:
            flights[k] = push(k, first_y, line, line, to_y)
        else:
            flights[k] = push(k, first_x, line, line, to_x)
    def stage_two(k):
        start, size = cuts[k]
        rows = pl.ds(start, size)
        for copy in flights[k]:
            copy.wait_recv()
        if k % 2 == 0:
            sheet = out.at[:, :, x, c, rows]
            flights[k] = push(k, first_x, sheet, sheet, to_x)
        else:
            sheet = out.at[:, y, :, c, rows]
            flights[k] = push(k, first_y, sheet, sheet, to_y)
    def stage_three(k):
        start, size = cuts[k]
        for copy in flights[k]:
            copy.wait_recv()
        cube = out.at[:, :, :, c, pl.ds(start, size)]
        flights[k] = push(k, 0, cube, cube, [partner])
    in_waves((stage_one, stage_two, stage_three), len(cuts))
    for flight in flights:
        for copy in flight:
            copy.wait_recv()
    for copy in sent:
        copy.wait_send()


def gather_rows(own, group_count, wide_count):
    rows = own.shape[0]
    wide = group_count // 2
    tall = wide if wide_count % wide == 0 else 1
    deep = wide_count // tall
    step = -(-rows // (CUTS * 16)) * 16
    cuts = [(start, min(step, rows - start)) for start in range(0, rows, step)]
    sems = pltpu.SemaphoreType.DMA((len(cuts), wide + tall + deep - 2))
    vmem = pl.BlockSpec(memory_space=pltpu.VMEM)
    whole = pl.pallas_call(
        functools.partial(gather_kernel, (deep, tall, wide), cuts),
        out_shape=jax.ShapeDtypeStruct((deep, tall, wide, 2, rows, LANES), jnp.bfloat16),
        in_specs=[vmem],
        out_specs=vmem,
        scratch_shapes=[sems, sems],
        compiler_params=pltpu.CompilerParams(
            collective_id=1, has_side_effects=True, vmem_limit_bytes=32 * 1024 * 1024
        ),
    )(own)
    return whole.reshape(wide_count * group_count * rows, LANES)


def unpack_kernel(rows_ref, main_ref, out_ref, main, tail):
    edge = START_OUT // 16 * 16

    def widen(place, size):
        main[pl.ds(place, size), :] = rows_ref[pl.ds(place, size), :].astype(jnp.float32)

    in_spans(main.shape[0], widen)

    def widen_tail(place, size):
        block = rows_ref[pl.ds(edge + place, size), :].astype(jnp.float32)
        tail[pl.ds(place, size), :] = pltpu.roll(block, LANES - SHIFT, 1)

    in_spans(tail.shape[0], widen_tail)
    for j in range(WIDE):
        main_ref[:, j * LANES : (j + 1) * LANES] = main[
            pl.ds(ROWS_GAIN + j, D, stride=WIDE), :
        ].astype(jnp.bfloat16)
    early = lax.broadcasted_iota(jnp.int32, (INNER, LANES), 1) < LANES - SHIFT
    base = START_OUT - edge
    for j in range(THIN):
        here = tail[pl.ds(base + j, INNER, stride=THIN), :]
        after = tail[pl.ds(base + j + 1, INNER, stride=THIN), :]
        out_ref[:, j * LANES : (j + 1) * LANES] = jnp.where(early, here, after).astype(
            jnp.bfloat16
        )


def unpack(rows):
    w_main, w_out = unpack_wide(rows)
    gain_in = rows[:ROWS_GAIN].reshape(D)
    flat = rows[START_SMALL : START_SMALL + ROWS_SMALL].reshape(-1)
    shapes = [(D, HEADS), (KERNEL, CHANNELS), (CHANNELS,), (HEADS,), (HEADS,), (HEADS,), (INNER,)]
    pieces = []
    offset = 0
    for shape in shapes:
        length = math.prod(shape)
        pieces.append(flat[offset : offset + length].reshape(shape))
        offset = offset + length
    return [gain_in, w_main] + pieces + [w_out]


def unpack_wide(rows):
    vmem = pl.BlockSpec(memory_space=pltpu.VMEM)
    edge = START_OUT // 16 * 16
    return pl.pallas_call(
        unpack_kernel,
        out_shape=(
            jax.ShapeDtypeStruct((D, INNER + CHANNELS), jnp.bfloat16),
            jax.ShapeDtypeStruct((INNER, D), jnp.bfloat16),
        ),
        in_specs=[vmem],
        out_specs=(vmem, vmem),
        scratch_shapes=[
            pltpu.VMEM((-(-START_SMALL // 32) * 32, LANES), jnp.float32),
            pltpu.VMEM(((rows.shape[0] - edge) // 32 * 32, LANES), jnp.float32),
        ],
        compiler_params=pltpu.CompilerParams(vmem_limit_bytes=48 * 1024 * 1024),
    )(rows)


HIGHEST = lax.Precision.HIGHEST
BLOCKS = INNER // LANES
PER = LANES // HEAD_DIM


def exact(left, right):
    return jnp.dot(left, right, preferred_element_type=jnp.float32, precision=HIGHEST)


def row_sum(value):
    return jnp.sum(value, axis=1, keepdims=True)


def col_sum(value):
    return jnp.sum(value, axis=0, keepdims=True)


def mixer_kernel(
    tokens, cot, seq_col, seq_row, gain_in, w_main, w_dt, conv_wb, heads, gain_out, w_out,
    result, grad_input, normed, grad_proj, hidden, live, grad_dt, g_conv, g_heads, g_gain_out, g_gain_in, g_w_dt,
    proj, slope, active, scanned, gated, grad_hidden, factor, mixed, cols, lag_mask,
):
    rows = tokens.shape[0]
    half = jnp.bfloat16
    seq_t = jnp.broadcast_to(seq_col[...], (rows, LANES))
    place_t = lax.broadcasted_iota(jnp.int32, (rows, LANES), 0)
    for lag in range(1, KERNEL):
        same_run = (pltpu.roll(seq_t, lag, 0) == seq_t) & (place_t >= lag)
        lag_mask[lag - 1] = same_run.astype(jnp.float32)
    first = lax.broadcasted_iota(jnp.int32, (rows, rows), 0)
    second = lax.broadcasted_iota(jnp.int32, (rows, rows), 1)
    lower = first >= second
    same = lower & (seq_col[...] == seq_row[...])
    lanes = lax.broadcasted_iota(jnp.int32, (rows, LANES), 1)
    x = tokens[...].astype(jnp.float32)
    scale_in = lax.rsqrt(row_sum(x * x) * (1.0 / D) + EPS)
    normed[...] = (x * scale_in * gain_in[...]).astype(half)
    live[...] = jnp.where(seq_col[...] >= 0, cot[...].astype(jnp.float32), 0.0).astype(half)

    def project(pair):
        both = matmul(normed[...], w_main[:, pair * 2 * LANES : (pair + 1) * 2 * LANES])
        proj[2 * pair] = both[:, :LANES]
        proj[2 * pair + 1] = both[:, LANES:]

    def back_out(pair):
        both = against(live[...], w_out[pair * 2 * LANES : (pair + 1) * 2 * LANES, :])
        grad_hidden[2 * pair] = both[:, :LANES]
        grad_hidden[2 * pair + 1] = both[:, LANES:]

    raw = matmul(normed[...], w_dt[...]) + heads[0:1, 0:LANES]
    steps = jnp.maximum(raw, 0.0) + jnp.log1p(jnp.exp(-jnp.abs(raw)))
    rate = -jnp.exp(heads[1:2, 0:LANES])
    logs = exact(lower.astype(jnp.float32), steps * rate)
    logs_t = logs.T
    steps_t = steps.T

    def convolve(block):
        span = slice(block * LANES, (block + 1) * LANES)
        inside = proj[BLOCKS + block]
        total = conv_wb[KERNEL : KERNEL + 1, span] + conv_wb[KERNEL - 1 : KERNEL, span] * inside
        for lag in range(1, KERNEL):
            tap = conv_wb[KERNEL - 1 - lag : KERNEL - lag, span]
            total = total + tap * (pltpu.roll(inside, lag, 0) * lag_mask[lag - 1])
        gate = jax.nn.sigmoid(total)
        value = total * gate
        active[block] = value
        slope[block] = gate + value * (1.0 - gate)

    project(BLOCKS)
    convolve(BLOCKS)
    convolve(BLOCKS + 1)
    b_mat, c_mat = active[BLOCKS], active[BLOCKS + 1]
    scores = lax.dot_general(
        c_mat, b_mat, (((1,), (1,)), ((), ())), preferred_element_type=jnp.float32, precision=HIGHEST
    )
    squares = jnp.zeros((rows, LANES), jnp.float32)
    cross = jnp.zeros((rows, LANES), jnp.float32)
    for pair in range(BLOCKS // 2):
        project(BLOCKS // 2 + pair)
        project(pair)
        back_out(pair)
        for block in (2 * pair, 2 * pair + 1):
            span = slice(block * LANES, (block + 1) * LANES)
            convolve(block)
            value = active[block]
            parts = []
            for side in range(PER):
                head = PER * block + side
                gap = logs[:, head : head + 1] - logs_t[head : head + 1, :]
                fall = jnp.exp(jnp.where(same, gap, -1e30))
                factor[head] = fall
                mix = ((fall * scores) * steps_t[head : head + 1, :]).astype(half)
                mixed[head] = mix
                parts.append(mix)
            low = value.astype(half)
            zero = jnp.zeros_like(low)
            left = lanes < HEAD_DIM
            stacked = jnp.concatenate(
                [jnp.where(left, low, zero), jnp.where(left, zero, low)], 0
            )
            inside = matmul(jnp.concatenate(parts, 1), stacked)
            total = inside + heads[8:9, span] * value
            gate = proj[block]
            out = total * (gate * jax.nn.sigmoid(gate))
            scanned[block] = total
            gated[block] = out
            squares = squares + out * out
            cross = cross + out * (grad_hidden[block] * gain_out[0:1, span])
    scale = lax.rsqrt(row_sum(squares) * (1.0 / INNER) + EPS)
    pull = row_sum(cross) * (scale * scale * scale) * (1.0 / INNER)
    scale_w = jnp.broadcast_to(scale, (rows, LANES))
    pull_w = jnp.broadcast_to(pull, (rows, LANES))

    def unconvolve(block, grad_active):
        span = slice(block * LANES, (block + 1) * LANES)
        grad = grad_active * slope[block]
        inside = proj[BLOCKS + block]
        total = conv_wb[KERNEL - 1 : KERNEL, span] * grad
        g_conv[KERNEL : KERNEL + 1, span] = col_sum(grad)
        g_conv[KERNEL - 1 : KERNEL, span] = col_sum(grad * inside)
        for lag in range(1, KERNEL):
            tap = conv_wb[KERNEL - 1 - lag : KERNEL - lag, span]
            kept = grad * lag_mask[lag - 1]
            g_conv[KERNEL - 1 - lag : KERNEL - lag, span] = col_sum(kept * pltpu.roll(inside, lag, 0))
            total = total + tap * pltpu.roll(kept, rows - lag, 0)
        grad_proj[:, INNER + block * LANES : INNER + (block + 1) * LANES] = total.astype(half)

    g_conv[KERNEL + 1 :, :] = jnp.zeros((8 - KERNEL - 1, CHANNELS), jnp.float32)
    grad_scores = jnp.zeros((rows, rows), jnp.float32)
    row_part = jnp.zeros((rows, LANES), jnp.float32)
    cols[...] = jnp.zeros((LANES, rows), jnp.float32)
    for block in range(BLOCKS):
        span = slice(block * LANES, (block + 1) * LANES)
        out, total, gate, value = gated[block], scanned[block], proj[block], active[block]
        down = grad_hidden[block]
        unit = out * scale_w
        gain = gain_out[0:1, span]
        hidden[:, span] = (unit * gain).astype(half)
        g_gain_out[0:1, span] = col_sum(down * unit)
        grad_gated = (down * gain) * scale_w - out * pull_w
        sig = jax.nn.sigmoid(gate)
        silu = gate * sig
        grad_total = grad_gated * silu
        grad_proj[:, span] = (grad_gated * total * (sig + silu * (1.0 - sig))).astype(half)
        g_heads[8:9, span] = col_sum(grad_total * value)
        low = grad_total.astype(half)
        zero = jnp.zeros_like(low)
        left = lanes < HEAD_DIM
        values_low = value.astype(half)
        tops = jnp.concatenate([jnp.where(left, low, zero), jnp.where(left, zero, low)], 0)
        grad_mix = against(tops, values_low)
        for side in range(PER):
            head = PER * block + side
            through = grad_mix[side * rows : (side + 1) * rows] * factor[head]
            scored = through * scores
            step = steps_t[head : head + 1, :]
            cols[head : head + 1, :] = col_sum(scored)
            row_part = jnp.where(lanes == head, row_sum(scored * step), row_part)
            grad_scores = grad_scores + through * step
        both = over_rows(jnp.concatenate([mixed[PER * block], mixed[PER * block + 1]], 0), tops)
        unconvolve(block, both + heads[8:9, span] * grad_total)
    low_scores = grad_scores.astype(half)
    unconvolve(BLOCKS + 1, matmul(low_scores, b_mat.astype(half)))
    unconvolve(BLOCKS, over_rows(low_scores, c_mat.astype(half)))
    col_part = cols[...].T
    upper = (first <= second).astype(jnp.float32)
    grad_decay = exact(upper, row_part - col_part * steps)
    grad_steps = col_part + grad_decay * rate
    grad_raw = grad_steps * jax.nn.sigmoid(raw)
    g_heads[0:1, 0:LANES] = col_sum(grad_raw)
    g_heads[1:2, 0:LANES] = col_sum(grad_decay * steps) * rate
    grad_dt[...] = grad_raw.astype(half)
    g_w_dt[...] = over_rows(normed[...], grad_dt[...])
    result[...] = (x + matmul(hidden[...], w_out[...])).astype(half)
    back = against(grad_proj[...], w_main[...]) + against(grad_dt[...], w_dt[...])
    g_gain_in[0:1, :] = col_sum(back * (x * scale_in))
    pulled = back * gain_in[...]
    push = row_sum(pulled * x) * (scale_in * scale_in * scale_in) * (1.0 / D)
    grad_input[...] = live[...].astype(jnp.float32) + (pulled * scale_in - x * push)


def block_pass(tokens, cotangent, seq_ids, weights, total):
    gain_in, w_main, w_dt, conv_w, conv_b, dt_bias, a_log, d_skip, gain_out, w_out = weights
    rows = tokens.shape[0]
    f32 = jnp.float32
    wide = lambda piece: jnp.pad(piece.astype(f32), (0, LANES - HEADS))
    conv_wb = jnp.concatenate([conv_w, conv_b[None], jnp.zeros((3, CHANNELS), conv_w.dtype)]).astype(f32)
    skip = jnp.repeat(d_skip.astype(f32), HEAD_DIM)
    top = jnp.pad(jnp.stack([wide(dt_bias), wide(a_log)]), ((0, 6), (0, INNER - LANES)))
    heads = jnp.concatenate([top, skip[None], jnp.zeros((7, INNER), f32)])
    w_dt_wide = jnp.pad(w_dt, ((0, 0), (0, LANES - HEADS)))
    vmem = pl.BlockSpec(memory_space=pltpu.VMEM)
    shape = jax.ShapeDtypeStruct
    half = jnp.bfloat16
    block = (rows, LANES)
    result, grad_input, normed, grad_proj, hidden, live, _, g_conv, g_heads, g_gain_out, g_gain_in, g_w_dt = pl.pallas_call(
        mixer_kernel,
        out_shape=(
            shape((rows, D), half), shape((rows, D), f32), shape((rows, D), half),
            shape((rows, INNER + CHANNELS), half), shape((rows, INNER), half), shape((rows, D), half),
            shape((rows, LANES), half), shape((8, CHANNELS), f32), shape((16, INNER), f32),
            shape((1, INNER), f32), shape((1, D), f32), shape((D, LANES), f32),
        ),
        in_specs=[vmem] * 11,
        out_specs=(vmem,) * 12,
        scratch_shapes=[
            pltpu.VMEM((WIDE, *block), f32),
            pltpu.VMEM((BLOCKS + 2, *block), f32),
            pltpu.VMEM((BLOCKS + 2, *block), f32),
            pltpu.VMEM((BLOCKS, *block), f32),
            pltpu.VMEM((BLOCKS, *block), f32),
            pltpu.VMEM((BLOCKS, *block), f32),
            pltpu.VMEM((HEADS, rows, rows), f32),
            pltpu.VMEM((HEADS, rows, rows), half),
            pltpu.VMEM((LANES, rows), f32),
            pltpu.VMEM((KERNEL - 1, *block), f32),
        ],
        compiler_params=pltpu.CompilerParams(vmem_limit_bytes=48 * 1024 * 1024),
    )(
        tokens, cotangent, seq_ids[:, None], seq_ids[None, :], gain_in.astype(f32)[None], w_main, w_dt_wide,
        conv_wb, heads, gain_out.astype(f32)[None], w_out,
    )
    skip_grad = g_heads[8].reshape(HEADS, HEAD_DIM).sum(1)
    small_flat = jnp.concatenate([
        g_w_dt[:, :HEADS].reshape(-1), g_conv[: KERNEL + 1].reshape(-1), g_heads[0, :HEADS],
        g_heads[1, :HEADS], skip_grad, g_gain_out[0],
    ])
    small_flat = jnp.pad(small_flat, (0, ROWS_SMALL * LANES - small_flat.shape[0]))
    flat = pack_all(
        g_gain_in.reshape(ROWS_GAIN, LANES), small_flat.reshape(ROWS_SMALL, LANES),
        normed, grad_proj, hidden, live, total // LANES,
    )
    return (result, grad_input, flat)


def adamw(weight, first, second, grad, step_count):
    steps_done = step_count[0].astype(jnp.float32)
    first_new = BETA_ONE * first + (1.0 - BETA_ONE) * grad
    second_new = BETA_TWO * second + (1.0 - BETA_TWO) * grad * grad
    first_hat = first_new / (1.0 - jnp.power(BETA_ONE, steps_done))
    second_hat = second_new / (1.0 - jnp.power(BETA_TWO, steps_done))
    weight_new = weight - LEARN_RATE * (
        first_hat / (jnp.sqrt(second_hat) + ADAM_EPS) + WEIGHT_DECAY * weight
    )
    return (weight_new, first_new, second_new)


def per_device(tokens, cotangent, seq_ids, params, first_moment, second_moment, step_count):
    width = params.shape[0]
    rounded = params.astype(jnp.bfloat16)
    own = rounded.reshape(width // LANES, LANES)
    whole = gather_rows(own, lax.axis_size("shard"), lax.axis_size("dp"))
    weights = unpack(whole)
    result, grad_input, flat = block_pass(tokens, cotangent, seq_ids, weights, whole.size)
    owned = scatter_sum(flat, lax.axis_size("shard"), lax.axis_size("dp"), width // LANES)
    owned = owned.reshape(width)
    new_weight, new_first, new_second = adamw(
        params, first_moment, second_moment, owned, step_count
    )
    return (result, grad_input, owned, new_weight, new_first, new_second)


def solution(mesh):
    return jax.shard_map(
        per_device,
        mesh=mesh,
        in_specs=(
            P(("dp", "shard"), None),
            P(("dp", "shard"), None),
            P(("dp", "shard")),
            P(("dp", "shard")),
            P(("dp", "shard")),
            P(("dp", "shard")),
            P(),
        ),
        out_specs=(
            P(("dp", "shard"), None),
            P(("dp", "shard"), None),
            P(("dp", "shard")),
            P(("dp", "shard")),
            P(("dp", "shard")),
            P(("dp", "shard")),
        ),
        check_vma=False,
    )
```

```python
import functools
import math

import jax
import jax.numpy as jnp
from jax import lax
from jax.experimental import pallas as pl
from jax.experimental.pallas import tpu as pltpu
from jax.sharding import PartitionSpec as P

D = 768
HEADS = 24
HEAD_DIM = 64
STATE = 128
KERNEL = 4
STRETCH = 128
INNER = 1536
CHANNELS = 1792
LANES = 128
CUTS = 4
LAG = 3
AHEAD = 8
SPAN = 256
MESH = pl.DeviceIdType.MESH
PACKED = D + D * (INNER + CHANNELS) + D * HEADS + (KERNEL + 1) * CHANNELS + 3 * HEADS + INNER + INNER * D


EPS = 1e-05
BETA_ONE = 0.9
BETA_TWO = 0.999
ADAM_EPS = 1e-08
LEARN_RATE = 0.01
WEIGHT_DECAY = 0.1


def matmul(left, right):
    return jnp.dot(left, right, preferred_element_type=jnp.float32)


def over_rows(left, right):
    return lax.dot_general(
        left, right, (((0,), (0,)), ((), ())), preferred_element_type=jnp.float32
    )


def against(left, right):
    return lax.dot_general(
        left, right, (((1,), (1,)), ((), ())), preferred_element_type=jnp.float32
    )


ROWS_GAIN = D // LANES
ROWS_MAIN = D * (INNER + CHANNELS) // LANES
START_SMALL = ROWS_GAIN + ROWS_MAIN
START_OUT = (PACKED - INNER * D) // LANES
SHIFT = (PACKED - INNER * D) % LANES
ROWS_OUT = INNER * D // LANES
ROWS_SMALL = START_OUT + 1 - START_SMALL
WIDE = (INNER + CHANNELS) // LANES
THIN = D // LANES


def in_spans(total, body):
    def step(number, carry):
        body(pl.multiple_of(number * SPAN, SPAN), SPAN)
        return carry

    whole = total // SPAN
    lax.fori_loop(0, whole, step, 0)
    if total % SPAN:
        body(whole * SPAN, total - whole * SPAN)


def pack_kernel(gain_ref, small_ref, normed_ref, proj_ref, hidden_ref, cot_ref, out_ref, main, tail):
    main[0:ROWS_GAIN, :] = gain_ref[...]
    main[START_SMALL : START_OUT, :] = small_ref[0 : ROWS_SMALL - 1, :]
    tail[7:8, :] = small_ref[ROWS_SMALL - 1 : ROWS_SMALL, :]
    tail[8 + ROWS_OUT :, :] = jnp.zeros((tail.shape[0] - 8 - ROWS_OUT, LANES), jnp.float32)
    for pair in range(WIDE // 2):
        both = over_rows(normed_ref[...], proj_ref[:, pair * 2 * LANES : (pair + 1) * 2 * LANES])
        for side in range(2):
            main[pl.ds(ROWS_GAIN + 2 * pair + side, D, stride=WIDE), :] = both[
                :, side * LANES : (side + 1) * LANES
            ]
    for pair in range(THIN // 2):
        both = over_rows(hidden_ref[...], cot_ref[:, pair * 2 * LANES : (pair + 1) * 2 * LANES])
        for side in range(2):
            part = pltpu.roll(both[:, side * LANES : (side + 1) * LANES], SHIFT, 1)
            tail[pl.ds(8 + 2 * pair + side, INNER, stride=THIN), :] = part
    edge = START_OUT // 16 * 16

    def cast_main(place, size):
        out_ref[pl.ds(place, size), :] = main[pl.ds(place, size), :].astype(jnp.bfloat16)

    in_spans(edge, cast_main)
    early = lax.broadcasted_iota(jnp.int32, (8, LANES), 1) < SHIFT
    seam = jnp.where(early, tail[7:15, :], tail[8:16, :])
    out_ref[edge : edge + 16, :] = jnp.concatenate([main[edge : edge + 8, :], seam], 0).astype(
        jnp.bfloat16
    )

    def cast_tail(place, size):
        block = tail[pl.ds(place + 16, size), :]
        before = tail[pl.ds(place + 8, size), :]
        joined = jnp.concatenate([before[7:8], block[: size - 1]], 0)
        lanes = lax.broadcasted_iota(jnp.int32, (size, LANES), 1)
        out_ref[pl.ds(edge + 16 + place, size), :] = jnp.where(
            lanes < SHIFT, joined, block
        ).astype(jnp.bfloat16)

    in_spans(out_ref.shape[0] - edge - 16, cast_tail)


def pack_all(gain, small, normed, proj, hidden, cot, rows):
    vmem = pl.BlockSpec(memory_space=pltpu.VMEM)
    return pl.pallas_call(
        pack_kernel,
        out_shape=jax.ShapeDtypeStruct((rows, LANES), jnp.bfloat16),
        in_specs=[vmem] * 6,
        out_specs=vmem,
        scratch_shapes=[
            pltpu.VMEM((START_OUT, LANES), jnp.float32),
            pltpu.VMEM((rows - START_OUT + 16, LANES), jnp.float32),
        ],
        compiler_params=pltpu.CompilerParams(vmem_limit_bytes=48 * 1024 * 1024),
    )(gain, small, normed, proj, hidden, cot)


def flip(place, number, size):
    if size & (size - 1):
        return lax.rem(place + number, size)
    bit = 1
    while bit <= number:
        if number & bit:
            place = place + bit - 2 * bit * lax.rem(lax.div(place, bit), 2)
        bit = 2 * bit
    return place


def unflip(place, number, size):
    return lax.rem(place + size - number, size) if size & (size - 1) else flip(place, number, size)


def slice_grid(group_count, wide_count):
    wide = group_count // 2
    tall = wide if wide_count % wide == 0 else 1
    return wide_count // tall, tall, wide


def slice_cuts(rows):
    step = -(-rows // (CUTS * 16)) * 16
    return [(start, min(step, rows - start)) for start in range(0, rows, step)]


class Neighbours:
    def __init__(self, grid):
        deep, tall, wide = self.grid = grid
        dp, shard = lax.axis_index("dp"), lax.axis_index("shard")
        z, y = lax.div(dp, tall), lax.rem(dp, tall)
        x, c = lax.div(shard, 2), lax.rem(shard, 2)
        self.z, self.y, self.x, self.c = z, y, x, c
        self.xs = [lax.rem(x + j, wide) for j in range(1, wide)]
        self.ys = [lax.rem(y + j, tall) for j in range(1, tall)]
        self.to_x = [self.place(z, y, p, c) for p in self.xs]
        self.to_y = [self.place(z, p, x, c) for p in self.ys]
        self.out_z = [None] + [self.place(unflip(z, i, deep), y, x, c) for i in range(1, deep)]
        self.partner = self.place(z, y, x, 1 - c)

    def place(self, z, y, x, c):
        return (z * self.grid[1] + y, x * 2 + c)

    def meet(self):
        everyone = [self.partner] + self.to_x + self.to_y + self.out_z[1:]
        barrier = pltpu.get_barrier_semaphore()
        for peer in everyone:
            pl.semaphore_signal(barrier, inc=1, device_id=peer, device_id_type=MESH)
        pl.semaphore_wait(barrier, len(everyone))


def scatter_kernel(grid, cuts, data, out, send_sem, recv_sem, *refs):
    deep, tall, wide = grid
    near = Neighbours(grid)
    z, y, x, c = near.z, near.y, near.x, near.c
    near.meet()
    sent = []

    def push(item, number, src, dst, peer):
        copy = pltpu.make_async_remote_copy(
            src_ref=src,
            dst_ref=dst,
            send_sem=send_sem.at[item, number],
            recv_sem=recv_sem.at[item, number],
            device_id=peer,
            device_id_type=MESH,
        )
        copy.start()
        sent.append(copy)
        return copy

    def total(parts):
        value = parts[0].astype(jnp.float32)
        for part in parts[1:]:
            value = value + part.astype(jnp.float32)
        return value

    first_x, first_y, first_z = 1, wide, wide + tall - 1
    order = [(i, k) for i in list(range(deep - 1, 0, -1)) + [0] for k in range(len(cuts))]
    held = {}
    for item, key in enumerate(order):
        held[key] = refs[item * 7 : item * 7 + 7]
    flights = {}

    def stage_zero(item):
        i, k = order[item]
        start, size = cuts[k]
        src = data.at[unflip(z, i, deep), :, :, 1 - c, start : start + size]
        flights[item] = [push(item, 0, src, held[i, k][0], near.partner)]

    def stage_one(item):
        i, k = order[item]
        start, size = cuts[k]
        got, acc, got_one = held[i, k][:3]
        plane = unflip(z, i, deep)
        for copy in flights[item]:
            copy.wait_recv()

        def add(step, carry):
            yi, xi = lax.div(step, wide), lax.rem(step, wide)
            mine = data[plane, yi, xi, c, start : start + size, :]
            acc[yi, xi] = total([mine, got[yi, xi]]).astype(jnp.bfloat16)
            return carry

        lax.fori_loop(0, tall * wide, add, 0)
        if k % 2 == 0:
            flights[item] = [
                push(item, first_x + j, acc.at[:, p], got_one.at[j], near.to_x[j])
                for j, p in enumerate(near.xs)
            ]
        else:
            flights[item] = [
                push(item, first_y + j, acc.at[p], got_one.at[j], near.to_y[j])
                for j, p in enumerate(near.ys)
            ]

    def stage_two(item):
        i, k = order[item]
        acc, got_one, acc_two, got_two = held[i, k][1:5]
        for copy in flights[item]:
            copy.wait_recv()

        def add(other, carry):
            mine = acc[other, x] if k % 2 == 0 else acc[y, other]
            parts = [mine] + [got_one[j, other] for j in range(got_one.shape[0])]
            acc_two[other] = total(parts).astype(jnp.bfloat16)
            return carry

        lax.fori_loop(0, tall if k % 2 == 0 else wide, add, 0)
        if k % 2 == 0:
            flights[item] = [
                push(item, first_y + j, acc_two.at[p], got_two.at[j], near.to_y[j])
                for j, p in enumerate(near.ys)
            ]
        else:
            flights[item] = [
                push(item, first_x + j, acc_two.at[p], got_two.at[j], near.to_x[j])
                for j, p in enumerate(near.xs)
            ]

    across = {}

    def stage_three(item):
        i, k = order[item]
        start, size = cuts[k]
        acc_two, got_two, acc_three, got_z = held[i, k][3:]
        for copy in flights[item]:
            copy.wait_recv()
        mine = y if k % 2 == 0 else x
        parts = [acc_two[mine]] + [got_two[j] for j in range(got_two.shape[0])]
        if i:
            acc_three[...] = total(parts).astype(jnp.bfloat16)
            across[i, k] = push(item, first_z, acc_three, got_z, near.out_z[i])
        else:
            value = total(parts)
            for j in range(1, deep):
                across[j, k].wait_recv()
                value = value + held[j, k][6][...].astype(jnp.float32)
            out[start : start + size, :] = value

    in_waves((stage_zero, stage_one, stage_two, stage_three), len(order), (0, 2, 5, 8))
    for copy in sent:
        copy.wait_send()


def in_waves(stages, count, lags):
    for wave in range(count + lags[-1]):
        for stage, lag in zip(stages, lags):
            if 0 <= wave - lag < count:
                stage(wave - lag)


def scatter_sum(flat, group_count, wide_count, rows):
    deep, tall, wide = grid = slice_grid(group_count, wide_count)
    cuts = slice_cuts(rows)
    scratch = []
    for _ in range(deep):
        for k, (start, size) in enumerate(cuts):
            lead, other = (wide, tall) if k % 2 == 0 else (tall, wide)
            for shape in (
                (tall, wide),
                (tall, wide),
                (lead - 1, other),
                (other,),
                (other - 1,),
                (),
                (),
            ):
                scratch.append(pltpu.VMEM((*shape, size, LANES), jnp.bfloat16))
    sems = pltpu.SemaphoreType.DMA((deep * len(cuts), wide + tall))
    vmem = pl.BlockSpec(memory_space=pltpu.VMEM)
    return pl.pallas_call(
        functools.partial(scatter_kernel, grid, cuts),
        out_shape=jax.ShapeDtypeStruct((rows, LANES), jnp.float32),
        in_specs=[vmem],
        out_specs=vmem,
        scratch_shapes=[sems, sems] + scratch,
        compiler_params=pltpu.CompilerParams(
            collective_id=0, has_side_effects=True, vmem_limit_bytes=56 * 1024 * 1024
        ),
    )(flat.reshape(deep, tall, wide, 2, rows, LANES))


def gather_kernel(grid, cuts, own, out, send_sem, recv_sem):
    deep, tall, wide = grid
    near = Neighbours(grid)
    z, y, x, c = near.z, near.y, near.x, near.c
    near.meet()
    sent = []

    def push(item, number, src, dst, peers):
        started = []
        for j, peer in enumerate(peers):
            copy = pltpu.make_async_remote_copy(
                src_ref=src,
                dst_ref=dst,
                send_sem=send_sem.at[item, number + j],
                recv_sem=recv_sem.at[item, number + j],
                device_id=peer,
                device_id_type=MESH,
            )
            copy.start()
            started.append(copy)
        sent.extend(started)
        return started

    first_x, first_y, first_z = 1, wide, wide + tall - 1
    order = [(i, k) for i in range(deep) for k in range(len(cuts))]
    flights = {}

    def start_z(item):
        i, k = order[item]
        if i:
            rows = pl.ds(*cuts[k])
            flights[item] = push(item, first_z, own.at[rows], out.at[z, y, x, c, rows], [near.out_z[i]])

    def stage_one(item):
        i, k = order[item]
        rows = pl.ds(*cuts[k])
        for copy in flights.get(item, []):
            copy.wait_recv()
        block = out.at[flip(z, i, deep), y, x, c, rows]
        source = block if i else own.at[rows]
        if k % 2 == 0:
            flights[item] = push(item, first_y, source, block, near.to_y)
        else:
            flights[item] = push(item, first_x, source, block, near.to_x)
        if item == 0:
            out[z, y, x, c] = own[...]

    def stage_two(item):
        i, k = order[item]
        rows = pl.ds(*cuts[k])
        for copy in flights[item]:
            copy.wait_recv()
        plane = flip(z, i, deep)
        if k % 2 == 0:
            line = out.at[plane, :, x, c, rows]
            flights[item] = push(item, first_x, line, line, near.to_x)
        else:
            line = out.at[plane, y, :, c, rows]
            flights[item] = push(item, first_y, line, line, near.to_y)

    def stage_three(item):
        i, k = order[item]
        for copy in flights[item]:
            copy.wait_recv()
        sheet = out.at[flip(z, i, deep), :, :, c, pl.ds(*cuts[k])]
        flights[item] = push(item, 0, sheet, sheet, [near.partner])

    for item in range(min(AHEAD, len(order))):
        start_z(item)

    def next_z(wave):
        if wave + AHEAD < len(order):
            start_z(wave + AHEAD)

    in_waves((next_z, stage_one, stage_two, stage_three), len(order), (0, 0, LAG, 2 * LAG))
    for item in range(len(order)):
        for copy in flights[item]:
            copy.wait_recv()
    for copy in sent:
        copy.wait_send()


def gather_rows(own, group_count, wide_count):
    rows = own.shape[0]
    deep, tall, wide = grid = slice_grid(group_count, wide_count)
    cuts = slice_cuts(rows)
    sems = pltpu.SemaphoreType.DMA((deep * len(cuts), wide + tall))
    vmem = pl.BlockSpec(memory_space=pltpu.VMEM)
    whole = pl.pallas_call(
        functools.partial(gather_kernel, grid, cuts),
        out_shape=jax.ShapeDtypeStruct((deep, tall, wide, 2, rows, LANES), jnp.bfloat16),
        in_specs=[vmem],
        out_specs=vmem,
        scratch_shapes=[sems, sems],
        compiler_params=pltpu.CompilerParams(
            collective_id=1, has_side_effects=True, vmem_limit_bytes=32 * 1024 * 1024
        ),
    )(own)
    return whole.reshape(wide_count * group_count * rows, LANES)


def unpack_kernel(rows_ref, main_ref, out_ref, main, tail):
    edge = START_OUT // 16 * 16

    def widen(place, size):
        main[pl.ds(place, size), :] = rows_ref[pl.ds(place, size), :].astype(jnp.float32)

    in_spans(main.shape[0], widen)

    def widen_tail(place, size):
        block = rows_ref[pl.ds(edge + place, size), :].astype(jnp.float32)
        tail[pl.ds(place, size), :] = pltpu.roll(block, LANES - SHIFT, 1)

    in_spans(tail.shape[0], widen_tail)
    for j in range(WIDE):
        main_ref[:, j * LANES : (j + 1) * LANES] = main[
            pl.ds(ROWS_GAIN + j, D, stride=WIDE), :
        ].astype(jnp.bfloat16)
    early = lax.broadcasted_iota(jnp.int32, (INNER, LANES), 1) < LANES - SHIFT
    base = START_OUT - edge
    for j in range(THIN):
        here = tail[pl.ds(base + j, INNER, stride=THIN), :]
        after = tail[pl.ds(base + j + 1, INNER, stride=THIN), :]
        out_ref[:, j * LANES : (j + 1) * LANES] = jnp.where(early, here, after).astype(
            jnp.bfloat16
        )


def unpack(rows):
    w_main, w_out = unpack_wide(rows)
    gain_in = rows[:ROWS_GAIN].reshape(D)
    flat = rows[START_SMALL : START_SMALL + ROWS_SMALL].reshape(-1)
    shapes = [(D, HEADS), (KERNEL, CHANNELS), (CHANNELS,), (HEADS,), (HEADS,), (HEADS,), (INNER,)]
    pieces = []
    offset = 0
    for shape in shapes:
        length = math.prod(shape)
        pieces.append(flat[offset : offset + length].reshape(shape))
        offset = offset + length
    return [gain_in, w_main] + pieces + [w_out]


def unpack_wide(rows):
    vmem = pl.BlockSpec(memory_space=pltpu.VMEM)
    edge = START_OUT // 16 * 16
    return pl.pallas_call(
        unpack_kernel,
        out_shape=(
            jax.ShapeDtypeStruct((D, INNER + CHANNELS), jnp.bfloat16),
            jax.ShapeDtypeStruct((INNER, D), jnp.bfloat16),
        ),
        in_specs=[vmem],
        out_specs=(vmem, vmem),
        scratch_shapes=[
            pltpu.VMEM((-(-START_SMALL // 32) * 32, LANES), jnp.float32),
            pltpu.VMEM(((rows.shape[0] - edge) // 32 * 32, LANES), jnp.float32),
        ],
        compiler_params=pltpu.CompilerParams(vmem_limit_bytes=48 * 1024 * 1024),
    )(rows)


HIGHEST = lax.Precision.HIGHEST
BLOCKS = INNER // LANES
PER = LANES // HEAD_DIM


def exact(left, right):
    return jnp.dot(left, right, preferred_element_type=jnp.float32, precision=HIGHEST)


def row_sum(value):
    return jnp.sum(value, axis=1, keepdims=True)


def col_sum(value):
    return jnp.sum(value, axis=0, keepdims=True)


def mixer_kernel(
    tokens, cot, seq_col, seq_row, gain_in, w_main, w_dt, conv_wb, heads, gain_out, w_out,
    result, grad_input, normed, grad_proj, hidden, live, grad_dt, g_conv, g_heads, g_gain_out, g_gain_in, g_w_dt,
    proj, slope, active, scanned, gated, grad_hidden, factor, mixed, cols, lag_mask,
):
    rows = tokens.shape[0]
    half = jnp.bfloat16
    seq_t = jnp.broadcast_to(seq_col[...], (rows, LANES))
    place_t = lax.broadcasted_iota(jnp.int32, (rows, LANES), 0)
    for lag in range(1, KERNEL):
        same_run = (pltpu.roll(seq_t, lag, 0) == seq_t) & (place_t >= lag)
        lag_mask[lag - 1] = same_run.astype(jnp.float32)
    first = lax.broadcasted_iota(jnp.int32, (rows, rows), 0)
    second = lax.broadcasted_iota(jnp.int32, (rows, rows), 1)
    lower = first >= second
    same = lower & (seq_col[...] == seq_row[...])
    lanes = lax.broadcasted_iota(jnp.int32, (rows, LANES), 1)
    x = tokens[...].astype(jnp.float32)
    scale_in = lax.rsqrt(row_sum(x * x) * (1.0 / D) + EPS)
    normed[...] = (x * scale_in * gain_in[...]).astype(half)
    live[...] = jnp.where(seq_col[...] >= 0, cot[...].astype(jnp.float32), 0.0).astype(half)

    def project(pair):
        both = matmul(normed[...], w_main[:, pair * 2 * LANES : (pair + 1) * 2 * LANES])
        proj[2 * pair] = both[:, :LANES]
        proj[2 * pair + 1] = both[:, LANES:]

    def back_out(pair):
        both = against(live[...], w_out[pair * 2 * LANES : (pair + 1) * 2 * LANES, :])
        grad_hidden[2 * pair] = both[:, :LANES]
        grad_hidden[2 * pair + 1] = both[:, LANES:]

    raw = matmul(normed[...], w_dt[...]) + heads[0:1, 0:LANES]
    steps = jnp.maximum(raw, 0.0) + jnp.log1p(jnp.exp(-jnp.abs(raw)))
    rate = -jnp.exp(heads[1:2, 0:LANES])
    logs = exact(lower.astype(jnp.float32), steps * rate)
    logs_t = logs.T
    steps_t = steps.T

    def convolve(block):
        span = slice(block * LANES, (block + 1) * LANES)
        inside = proj[BLOCKS + block]
        total = conv_wb[KERNEL : KERNEL + 1, span] + conv_wb[KERNEL - 1 : KERNEL, span] * inside
        for lag in range(1, KERNEL):
            tap = conv_wb[KERNEL - 1 - lag : KERNEL - lag, span]
            total = total + tap * (pltpu.roll(inside, lag, 0) * lag_mask[lag - 1])
        gate = jax.nn.sigmoid(total)
        value = total * gate
        active[block] = value
        slope[block] = gate + value * (1.0 - gate)

    project(BLOCKS)
    convolve(BLOCKS)
    convolve(BLOCKS + 1)
    b_mat, c_mat = active[BLOCKS], active[BLOCKS + 1]
    scores = lax.dot_general(
        c_mat, b_mat, (((1,), (1,)), ((), ())), preferred_element_type=jnp.float32, precision=HIGHEST
    )
    squares = jnp.zeros((rows, LANES), jnp.float32)
    cross = jnp.zeros((rows, LANES), jnp.float32)
    for pair in range(BLOCKS // 2):
        project(BLOCKS // 2 + pair)
        project(pair)
        back_out(pair)
        for block in (2 * pair, 2 * pair + 1):
            span = slice(block * LANES, (block + 1) * LANES)
            convolve(block)
            value = active[block]
            parts = []
            for side in range(PER):
                head = PER * block + side
                gap = logs[:, head : head + 1] - logs_t[head : head + 1, :]
                fall = jnp.exp(jnp.where(same, gap, -1e30))
                factor[head] = fall
                mix = ((fall * scores) * steps_t[head : head + 1, :]).astype(half)
                mixed[head] = mix
                parts.append(mix)
            low = value.astype(half)
            zero = jnp.zeros_like(low)
            left = lanes < HEAD_DIM
            stacked = jnp.concatenate(
                [jnp.where(left, low, zero), jnp.where(left, zero, low)], 0
            )
            inside = matmul(jnp.concatenate(parts, 1), stacked)
            total = inside + heads[8:9, span] * value
            gate = proj[block]
            out = total * (gate * jax.nn.sigmoid(gate))
            scanned[block] = total
            gated[block] = out
            squares = squares + out * out
            cross = cross + out * (grad_hidden[block] * gain_out[0:1, span])
    scale = lax.rsqrt(row_sum(squares) * (1.0 / INNER) + EPS)
    pull = row_sum(cross) * (scale * scale * scale) * (1.0 / INNER)
    scale_w = jnp.broadcast_to(scale, (rows, LANES))
    pull_w = jnp.broadcast_to(pull, (rows, LANES))

    def unconvolve(block, grad_active):
        span = slice(block * LANES, (block + 1) * LANES)
        grad = grad_active * slope[block]
        inside = proj[BLOCKS + block]
        total = conv_wb[KERNEL - 1 : KERNEL, span] * grad
        g_conv[KERNEL : KERNEL + 1, span] = col_sum(grad)
        g_conv[KERNEL - 1 : KERNEL, span] = col_sum(grad * inside)
        for lag in range(1, KERNEL):
            tap = conv_wb[KERNEL - 1 - lag : KERNEL - lag, span]
            kept = grad * lag_mask[lag - 1]
            g_conv[KERNEL - 1 - lag : KERNEL - lag, span] = col_sum(kept * pltpu.roll(inside, lag, 0))
            total = total + tap * pltpu.roll(kept, rows - lag, 0)
        grad_proj[:, INNER + block * LANES : INNER + (block + 1) * LANES] = total.astype(half)

    g_conv[KERNEL + 1 :, :] = jnp.zeros((8 - KERNEL - 1, CHANNELS), jnp.float32)
    grad_scores = jnp.zeros((rows, rows), jnp.float32)
    row_part = jnp.zeros((rows, LANES), jnp.float32)
    cols[...] = jnp.zeros((LANES, rows), jnp.float32)
    for block in range(BLOCKS):
        span = slice(block * LANES, (block + 1) * LANES)
        out, total, gate, value = gated[block], scanned[block], proj[block], active[block]
        down = grad_hidden[block]
        unit = out * scale_w
        gain = gain_out[0:1, span]
        hidden[:, span] = (unit * gain).astype(half)
        g_gain_out[0:1, span] = col_sum(down * unit)
        grad_gated = (down * gain) * scale_w - out * pull_w
        sig = jax.nn.sigmoid(gate)
        silu = gate * sig
        grad_total = grad_gated * silu
        grad_proj[:, span] = (grad_gated * total * (sig + silu * (1.0 - sig))).astype(half)
        g_heads[8:9, span] = col_sum(grad_total * value)
        low = grad_total.astype(half)
        zero = jnp.zeros_like(low)
        left = lanes < HEAD_DIM
        values_low = value.astype(half)
        tops = jnp.concatenate([jnp.where(left, low, zero), jnp.where(left, zero, low)], 0)
        grad_mix = against(tops, values_low)
        for side in range(PER):
            head = PER * block + side
            through = grad_mix[side * rows : (side + 1) * rows] * factor[head]
            scored = through * scores
            step = steps_t[head : head + 1, :]
            cols[head : head + 1, :] = col_sum(scored)
            row_part = jnp.where(lanes == head, row_sum(scored * step), row_part)
            grad_scores = grad_scores + through * step
        both = over_rows(jnp.concatenate([mixed[PER * block], mixed[PER * block + 1]], 0), tops)
        unconvolve(block, both + heads[8:9, span] * grad_total)
    low_scores = grad_scores.astype(half)
    unconvolve(BLOCKS + 1, matmul(low_scores, b_mat.astype(half)))
    unconvolve(BLOCKS, over_rows(low_scores, c_mat.astype(half)))
    col_part = cols[...].T
    upper = (first <= second).astype(jnp.float32)
    grad_decay = exact(upper, row_part - col_part * steps)
    grad_steps = col_part + grad_decay * rate
    grad_raw = grad_steps * jax.nn.sigmoid(raw)
    g_heads[0:1, 0:LANES] = col_sum(grad_raw)
    g_heads[1:2, 0:LANES] = col_sum(grad_decay * steps) * rate
    grad_dt[...] = grad_raw.astype(half)
    g_w_dt[...] = over_rows(normed[...], grad_dt[...])
    result[...] = (x + matmul(hidden[...], w_out[...])).astype(half)
    back = against(grad_proj[...], w_main[...]) + against(grad_dt[...], w_dt[...])
    g_gain_in[0:1, :] = col_sum(back * (x * scale_in))
    pulled = back * gain_in[...]
    push = row_sum(pulled * x) * (scale_in * scale_in * scale_in) * (1.0 / D)
    grad_input[...] = live[...].astype(jnp.float32) + (pulled * scale_in - x * push)


def block_pass(tokens, cotangent, seq_ids, weights, total):
    gain_in, w_main, w_dt, conv_w, conv_b, dt_bias, a_log, d_skip, gain_out, w_out = weights
    rows = tokens.shape[0]
    f32 = jnp.float32
    wide = lambda piece: jnp.pad(piece.astype(f32), (0, LANES - HEADS))
    conv_wb = jnp.concatenate([conv_w, conv_b[None], jnp.zeros((3, CHANNELS), conv_w.dtype)]).astype(f32)
    skip = jnp.repeat(d_skip.astype(f32), HEAD_DIM)
    top = jnp.pad(jnp.stack([wide(dt_bias), wide(a_log)]), ((0, 6), (0, INNER - LANES)))
    heads = jnp.concatenate([top, skip[None], jnp.zeros((7, INNER), f32)])
    w_dt_wide = jnp.pad(w_dt, ((0, 0), (0, LANES - HEADS)))
    vmem = pl.BlockSpec(memory_space=pltpu.VMEM)
    shape = jax.ShapeDtypeStruct
    half = jnp.bfloat16
    block = (rows, LANES)
    result, grad_input, normed, grad_proj, hidden, live, _, g_conv, g_heads, g_gain_out, g_gain_in, g_w_dt = pl.pallas_call(
        mixer_kernel,
        out_shape=(
            shape((rows, D), half), shape((rows, D), f32), shape((rows, D), half),
            shape((rows, INNER + CHANNELS), half), shape((rows, INNER), half), shape((rows, D), half),
            shape((rows, LANES), half), shape((8, CHANNELS), f32), shape((16, INNER), f32),
            shape((1, INNER), f32), shape((1, D), f32), shape((D, LANES), f32),
        ),
        in_specs=[vmem] * 11,
        out_specs=(vmem,) * 12,
        scratch_shapes=[
            pltpu.VMEM((WIDE, *block), f32),
            pltpu.VMEM((BLOCKS + 2, *block), f32),
            pltpu.VMEM((BLOCKS + 2, *block), f32),
            pltpu.VMEM((BLOCKS, *block), f32),
            pltpu.VMEM((BLOCKS, *block), f32),
            pltpu.VMEM((BLOCKS, *block), f32),
            pltpu.VMEM((HEADS, rows, rows), f32),
            pltpu.VMEM((HEADS, rows, rows), half),
            pltpu.VMEM((LANES, rows), f32),
            pltpu.VMEM((KERNEL - 1, *block), f32),
        ],
        compiler_params=pltpu.CompilerParams(vmem_limit_bytes=48 * 1024 * 1024),
    )(
        tokens, cotangent, seq_ids[:, None], seq_ids[None, :], gain_in.astype(f32)[None], w_main, w_dt_wide,
        conv_wb, heads, gain_out.astype(f32)[None], w_out,
    )
    skip_grad = g_heads[8].reshape(HEADS, HEAD_DIM).sum(1)
    small_flat = jnp.concatenate([
        g_w_dt[:, :HEADS].reshape(-1), g_conv[: KERNEL + 1].reshape(-1), g_heads[0, :HEADS],
        g_heads[1, :HEADS], skip_grad, g_gain_out[0],
    ])
    small_flat = jnp.pad(small_flat, (0, ROWS_SMALL * LANES - small_flat.shape[0]))
    flat = pack_all(
        g_gain_in.reshape(ROWS_GAIN, LANES), small_flat.reshape(ROWS_SMALL, LANES),
        normed, grad_proj, hidden, live, total // LANES,
    )
    return (result, grad_input, flat)


def adamw(weight, first, second, grad, step_count):
    steps_done = step_count[0].astype(jnp.float32)
    first_new = BETA_ONE * first + (1.0 - BETA_ONE) * grad
    second_new = BETA_TWO * second + (1.0 - BETA_TWO) * grad * grad
    first_hat = first_new / (1.0 - jnp.power(BETA_ONE, steps_done))
    second_hat = second_new / (1.0 - jnp.power(BETA_TWO, steps_done))
    weight_new = weight - LEARN_RATE * (
        first_hat / (jnp.sqrt(second_hat) + ADAM_EPS) + WEIGHT_DECAY * weight
    )
    return (weight_new, first_new, second_new)


def per_device(tokens, cotangent, seq_ids, params, first_moment, second_moment, step_count):
    width = params.shape[0]
    rounded = params.astype(jnp.bfloat16)
    own = rounded.reshape(width // LANES, LANES)
    whole = gather_rows(own, lax.axis_size("shard"), lax.axis_size("dp"))
    weights = unpack(whole)
    result, grad_input, flat = block_pass(tokens, cotangent, seq_ids, weights, whole.size)
    owned = scatter_sum(flat, lax.axis_size("shard"), lax.axis_size("dp"), width // LANES)
    owned = owned.reshape(width)
    new_weight, new_first, new_second = adamw(
        params, first_moment, second_moment, owned, step_count
    )
    return (result, grad_input, owned, new_weight, new_first, new_second)


def solution(mesh):
    return jax.shard_map(
        per_device,
        mesh=mesh,
        in_specs=(
            P(("dp", "shard"), None),
            P(("dp", "shard"), None),
            P(("dp", "shard")),
            P(("dp", "shard")),
            P(("dp", "shard")),
            P(("dp", "shard")),
            P(),
        ),
        out_specs=(
            P(("dp", "shard"), None),
            P(("dp", "shard"), None),
            P(("dp", "shard")),
            P(("dp", "shard")),
            P(("dp", "shard")),
            P(("dp", "shard")),
        ),
        check_vma=False,
    )
```

```python
import functools
import math

import jax
import jax.numpy as jnp
from jax import lax
from jax.experimental import pallas as pl
from jax.experimental.pallas import tpu as pltpu
from jax.sharding import PartitionSpec as P

D = 768
HEADS = 24
HEAD_DIM = 64
STATE = 128
KERNEL = 4
STRETCH = 128
INNER = 1536
CHANNELS = 1792
LANES = 128
CUTS = 4
LAG = 3
AHEAD = 8
SPAN = 256
MESH = pl.DeviceIdType.MESH
PACKED = D + D * (INNER + CHANNELS) + D * HEADS + (KERNEL + 1) * CHANNELS + 3 * HEADS + INNER + INNER * D


EPS = 1e-05
BETA_ONE = 0.9
BETA_TWO = 0.999
ADAM_EPS = 1e-08
LEARN_RATE = 0.01
WEIGHT_DECAY = 0.1


def matmul(left, right):
    return jnp.dot(left, right, preferred_element_type=jnp.float32)


def over_rows(left, right):
    return lax.dot_general(
        left, right, (((0,), (0,)), ((), ())), preferred_element_type=jnp.float32
    )


def against(left, right):
    return lax.dot_general(
        left, right, (((1,), (1,)), ((), ())), preferred_element_type=jnp.float32
    )


ROWS_GAIN = D // LANES
ROWS_MAIN = D * (INNER + CHANNELS) // LANES
START_SMALL = ROWS_GAIN + ROWS_MAIN
START_OUT = (PACKED - INNER * D) // LANES
SHIFT = (PACKED - INNER * D) % LANES
ROWS_OUT = INNER * D // LANES
ROWS_SMALL = START_OUT + 1 - START_SMALL
WIDE = (INNER + CHANNELS) // LANES
THIN = D // LANES


def in_spans(total, body):
    def step(number, carry):
        body(pl.multiple_of(number * SPAN, SPAN), SPAN)
        return carry

    whole = total // SPAN
    lax.fori_loop(0, whole, step, 0)
    if total % SPAN:
        body(whole * SPAN, total - whole * SPAN)


def flip(place, number, size):
    if size & (size - 1):
        return lax.rem(place + number, size)
    bit = 1
    while bit <= number:
        if number & bit:
            place = place + bit - 2 * bit * lax.rem(lax.div(place, bit), 2)
        bit = 2 * bit
    return place


def unflip(place, number, size):
    return lax.rem(place + size - number, size) if size & (size - 1) else flip(place, number, size)


def slice_grid(group_count, wide_count):
    wide = group_count // 2
    tall = wide if wide_count % wide == 0 else 1
    return wide_count // tall, tall, wide


def slice_cuts(rows):
    step = -(-rows // (CUTS * 16)) * 16
    return [(start, min(step, rows - start)) for start in range(0, rows, step)]


class Neighbours:
    def __init__(self, grid):
        deep, tall, wide = self.grid = grid
        dp, shard = lax.axis_index("dp"), lax.axis_index("shard")
        z, y = lax.div(dp, tall), lax.rem(dp, tall)
        x, c = lax.div(shard, 2), lax.rem(shard, 2)
        self.z, self.y, self.x, self.c = z, y, x, c
        self.xs = [lax.rem(x + j, wide) for j in range(1, wide)]
        self.ys = [lax.rem(y + j, tall) for j in range(1, tall)]
        self.to_x = [self.place(z, y, p, c) for p in self.xs]
        self.to_y = [self.place(z, p, x, c) for p in self.ys]
        self.out_z = [None] + [self.place(unflip(z, i, deep), y, x, c) for i in range(1, deep)]
        self.partner = self.place(z, y, x, 1 - c)

    def place(self, z, y, x, c):
        return (z * self.grid[1] + y, x * 2 + c)

    def meet(self):
        everyone = [self.partner] + self.to_x + self.to_y + self.out_z[1:]
        barrier = pltpu.get_barrier_semaphore()
        for peer in everyone:
            pl.semaphore_signal(barrier, inc=1, device_id=peer, device_id_type=MESH)
        pl.semaphore_wait(barrier, len(everyone))


def scatter_kernel(grid, cuts, data, out, send_sem, recv_sem, *refs):
    deep, tall, wide = grid
    near = Neighbours(grid)
    z, y, x, c = near.z, near.y, near.x, near.c
    near.meet()
    sent = []

    def push(item, number, src, dst, peer):
        copy = pltpu.make_async_remote_copy(
            src_ref=src,
            dst_ref=dst,
            send_sem=send_sem.at[item, number],
            recv_sem=recv_sem.at[item, number],
            device_id=peer,
            device_id_type=MESH,
        )
        copy.start()
        sent.append(copy)
        return copy

    def total(parts):
        value = parts[0].astype(jnp.float32)
        for part in parts[1:]:
            value = value + part.astype(jnp.float32)
        return value

    first_x, first_y, first_z = 1, wide, wide + tall - 1
    order = [(i, k) for i in list(range(deep - 1, 0, -1)) + [0] for k in range(len(cuts))]
    held = {}
    for item, key in enumerate(order):
        held[key] = refs[item * 7 : item * 7 + 7]
    flights = {}

    def stage_zero(item):
        i, k = order[item]
        start, size = cuts[k]
        src = data.at[unflip(z, i, deep), :, :, 1 - c, start : start + size]
        flights[item] = [push(item, 0, src, held[i, k][0], near.partner)]

    def stage_one(item):
        i, k = order[item]
        start, size = cuts[k]
        got, acc, got_one = held[i, k][:3]
        plane = unflip(z, i, deep)
        for copy in flights[item]:
            copy.wait_recv()

        def add(step, carry):
            yi, xi = lax.div(step, wide), lax.rem(step, wide)
            mine = data[plane, yi, xi, c, start : start + size, :]
            acc[yi, xi] = total([mine, got[yi, xi]]).astype(jnp.bfloat16)
            return carry

        lax.fori_loop(0, tall * wide, add, 0)
        if k % 2 == 0:
            flights[item] = [
                push(item, first_x + j, acc.at[:, p], got_one.at[j], near.to_x[j])
                for j, p in enumerate(near.xs)
            ]
        else:
            flights[item] = [
                push(item, first_y + j, acc.at[p], got_one.at[j], near.to_y[j])
                for j, p in enumerate(near.ys)
            ]

    def stage_two(item):
        i, k = order[item]
        acc, got_one, acc_two, got_two = held[i, k][1:5]
        for copy in flights[item]:
            copy.wait_recv()

        def add(other, carry):
            mine = acc[other, x] if k % 2 == 0 else acc[y, other]
            parts = [mine] + [got_one[j, other] for j in range(got_one.shape[0])]
            acc_two[other] = total(parts).astype(jnp.bfloat16)
            return carry

        lax.fori_loop(0, tall if k % 2 == 0 else wide, add, 0)
        if k % 2 == 0:
            flights[item] = [
                push(item, first_y + j, acc_two.at[p], got_two.at[j], near.to_y[j])
                for j, p in enumerate(near.ys)
            ]
        else:
            flights[item] = [
                push(item, first_x + j, acc_two.at[p], got_two.at[j], near.to_x[j])
                for j, p in enumerate(near.xs)
            ]

    across = {}

    def stage_three(item):
        i, k = order[item]
        start, size = cuts[k]
        acc_two, got_two, acc_three, got_z = held[i, k][3:]
        for copy in flights[item]:
            copy.wait_recv()
        mine = y if k % 2 == 0 else x
        parts = [acc_two[mine]] + [got_two[j] for j in range(got_two.shape[0])]
        if i:
            acc_three[...] = total(parts).astype(jnp.bfloat16)
            across[i, k] = push(item, first_z, acc_three, got_z, near.out_z[i])
        else:
            value = total(parts)
            for j in range(1, deep):
                across[j, k].wait_recv()
                value = value + held[j, k][6][...].astype(jnp.float32)
            out[start : start + size, :] = value

    in_waves((stage_zero, stage_one, stage_two, stage_three), len(order), (0, 2, 5, 8))
    for copy in sent:
        copy.wait_send()


def in_waves(stages, count, lags):
    for wave in range(count + lags[-1]):
        for stage, lag in zip(stages, lags):
            if 0 <= wave - lag < count:
                stage(wave - lag)


def scatter_sum(flat, group_count, wide_count, rows):
    deep, tall, wide = grid = slice_grid(group_count, wide_count)
    cuts = slice_cuts(rows)
    scratch = []
    for _ in range(deep):
        for k, (start, size) in enumerate(cuts):
            lead, other = (wide, tall) if k % 2 == 0 else (tall, wide)
            for shape in (
                (tall, wide),
                (tall, wide),
                (lead - 1, other),
                (other,),
                (other - 1,),
                (),
                (),
            ):
                scratch.append(pltpu.VMEM((*shape, size, LANES), jnp.bfloat16))
    sems = pltpu.SemaphoreType.DMA((deep * len(cuts), wide + tall))
    vmem = pl.BlockSpec(memory_space=pltpu.VMEM)
    return pl.pallas_call(
        functools.partial(scatter_kernel, grid, cuts),
        out_shape=jax.ShapeDtypeStruct((rows, LANES), jnp.float32),
        in_specs=[vmem],
        out_specs=vmem,
        scratch_shapes=[sems, sems] + scratch,
        compiler_params=pltpu.CompilerParams(
            collective_id=0, has_side_effects=True, vmem_limit_bytes=56 * 1024 * 1024
        ),
    )(flat.reshape(deep, tall, wide, 2, rows, LANES))


def gather_kernel(grid, cuts, params, w_main, w_out, small, gain, own, out, flat, send_sem, recv_sem):
    deep, tall, wide = grid
    near = Neighbours(grid)
    z, y, x, c = near.z, near.y, near.x, near.c
    near.meet()
    sent = []
    size_own = own.shape[0]
    size_plane = tall * wide * 2 * size_own
    own[...] = params[...].astype(jnp.bfloat16)

    def push(item, number, src, dst, peers):
        started = []
        for j, peer in enumerate(peers):
            copy = pltpu.make_async_remote_copy(
                src_ref=src,
                dst_ref=dst,
                send_sem=send_sem.at[item, number + j],
                recv_sem=recv_sem.at[item, number + j],
                device_id=peer,
                device_id_type=MESH,
            )
            copy.start()
            started.append(copy)
        sent.extend(started)
        return started

    first_x, first_y, first_z = 1, wide, wide + tall - 1
    order = [(i, k) for i in range(deep) for k in range(len(cuts))]
    flights = {}

    def start_z(item):
        i, k = order[item]
        if i:
            rows = pl.ds(*cuts[k])
            flights[item] = push(item, first_z, own.at[rows], out.at[z, y, x, c, rows], [near.out_z[i]])

    def next_z(wave):
        if wave + AHEAD < len(order):
            start_z(wave + AHEAD)

    def stage_one(item):
        i, k = order[item]
        rows = pl.ds(*cuts[k])
        for copy in flights.get(item, []):
            copy.wait_recv()
        block = out.at[flip(z, i, deep), y, x, c, rows]
        source = block if i else own.at[rows]
        if k % 2 == 0:
            flights[item] = push(item, first_y, source, block, near.to_y)
        else:
            flights[item] = push(item, first_x, source, block, near.to_x)
        if item == 0:
            out[z, y, x, c] = own[...]

    def stage_two(item):
        i, k = order[item]
        rows = pl.ds(*cuts[k])
        for copy in flights[item]:
            copy.wait_recv()
        plane = flip(z, i, deep)
        if k % 2 == 0:
            line = out.at[plane, :, x, c, rows]
            flights[item] = push(item, first_x, line, line, near.to_x)
        else:
            line = out.at[plane, y, :, c, rows]
            flights[item] = push(item, first_y, line, line, near.to_y)

    def stage_three(item):
        i, k = order[item]
        for copy in flights[item]:
            copy.wait_recv()
        sheet = out.at[flip(z, i, deep), :, :, c, pl.ds(*cuts[k])]
        flights[item] = push(item, 0, sheet, sheet, [near.partner])

    def main_block(number, carry):
        for j in range(WIDE):
            piece = flat[pl.ds(ROWS_GAIN + number * (16 * WIDE) + j, 16, stride=WIDE), :]
            w_main[pl.ds(pl.multiple_of(number * 16, 16), 16), j * LANES : (j + 1) * LANES] = piece.astype(
                jnp.bfloat16
            )
        return carry

    early = lax.broadcasted_iota(jnp.int32, (16, LANES), 1) < LANES - SHIFT

    def out_block(number, carry):
        turned = [
            pltpu.roll(flat[pl.ds(START_OUT + number * (16 * THIN) + j, 16, stride=THIN), :], LANES - SHIFT, 1)
            for j in range(THIN + 1)
        ]
        for j in range(THIN):
            w_out[pl.ds(pl.multiple_of(number * 16, 16), 16), j * LANES : (j + 1) * LANES] = jnp.where(
                early, turned[j], turned[j + 1]
            ).astype(jnp.bfloat16)
        return carry

    kinds = (
        (main_block, ROWS_GAIN, 16 * WIDE, 16 * WIDE, D // 16),
        (out_block, START_OUT, 16 * THIN, 16 * THIN + 1, INNER // 16),
    )

    def unpack_plane(plane):
        low = plane * size_plane
        for body, base, step, reach, count in kinds:
            begin = jnp.clip(lax.div(low - base + step * (count + 1) - 1, step) - count, 0, count)
            end = jnp.clip(lax.div(low + size_plane - base - reach + step * (count + 1), step) - count, 0, count)
            lax.fori_loop(begin, jnp.maximum(begin, end), body, 0)

    def stage_four(item):
        i, k = order[item]
        start, size = cuts[k]
        for copy in flights[item]:
            copy.wait_recv()
        plane = flip(z, i, deep)

        def widen(step, carry):
            yi, rest = lax.div(step, wide * 2), lax.rem(step, wide * 2)
            xi, ci = lax.div(rest, 2), lax.rem(rest, 2)
            place = plane * size_plane + step * size_own + start
            if size_own % 8 == 0:
                place = pl.multiple_of(place, 8)
            flat[pl.ds(place, size), :] = out[plane, yi, xi, ci, start : start + size, :].astype(jnp.float32)
            return carry

        lax.fori_loop(0, tall * wide * 2, widen, 0)
        if k == len(cuts) - 1:
            unpack_plane(plane)

    for item in range(min(AHEAD, len(order))):
        start_z(item)
    in_waves(
        (next_z, stage_one, stage_two, stage_three, stage_four), len(order), (0, 0, LAG, 2 * LAG, 2 * LAG + 2)
    )
    for body, base, step, reach, count in kinds:
        for number in range(count):
            low = base + number * step
            if low // size_plane != (low + reach - 1) // size_plane:
                body(number, 0)
    gain[0:ROWS_GAIN, :] = flat[0:ROWS_GAIN, :]
    gain[ROWS_GAIN:, :] = jnp.zeros((8 - ROWS_GAIN, LANES), jnp.float32)
    small[...] = flat[START_SMALL : START_SMALL + small.shape[0], :]
    for copy in sent:
        copy.wait_send()


def gather_weights(params, group_count, wide_count):
    rows = params.shape[0]
    deep, tall, wide = grid = slice_grid(group_count, wide_count)
    cuts = slice_cuts(rows)
    sems = pltpu.SemaphoreType.DMA((deep * len(cuts), wide + tall))
    vmem = pl.BlockSpec(memory_space=pltpu.VMEM)
    half, f32 = jnp.bfloat16, jnp.float32
    return pl.pallas_call(
        functools.partial(gather_kernel, grid, cuts),
        out_shape=(
            jax.ShapeDtypeStruct((D, INNER + CHANNELS), half),
            jax.ShapeDtypeStruct((INNER, D), half),
            jax.ShapeDtypeStruct((-(-ROWS_SMALL // 8) * 8, LANES), f32),
            jax.ShapeDtypeStruct((8, LANES), f32),
        ),
        in_specs=[vmem],
        out_specs=(vmem,) * 4,
        scratch_shapes=[
            pltpu.VMEM((rows, LANES), half),
            pltpu.VMEM((deep, tall, wide, 2, rows, LANES), half),
            pltpu.VMEM((wide_count * group_count * rows, LANES), f32),
            sems,
            sems,
        ],
        compiler_params=pltpu.CompilerParams(
            collective_id=1, has_side_effects=True, vmem_limit_bytes=40 * 1024 * 1024
        ),
    )(params)


HIGHEST = lax.Precision.HIGHEST
BLOCKS = INNER // LANES
PER = LANES // HEAD_DIM


def exact(left, right):
    return jnp.dot(left, right, preferred_element_type=jnp.float32, precision=HIGHEST)


def row_sum(value):
    return jnp.sum(value, axis=1, keepdims=True)


def col_sum(value):
    return jnp.sum(value, axis=0, keepdims=True)


def mixer_kernel(
    tokens, cot, seq_row, gain, small, w_main, w_out, result, grad_input, flat,
    normed, grad_proj, hidden, live, w_dt_wide,
    proj, slope, active, scanned, gated, grad_hidden, factor, mixed, cols, lag_mask, turned, main, tail,
):
    rows = tokens.shape[0]
    half = jnp.bfloat16
    seq_wide = jnp.broadcast_to(seq_row[...], (rows, rows)).astype(jnp.float32)
    seq_col = seq_wide.T
    seq_t = jnp.broadcast_to(seq_col[:, 0:1], (rows, LANES))
    place_t = lax.broadcasted_iota(jnp.int32, (rows, LANES), 0)
    for lag in range(1, KERNEL):
        same_run = (pltpu.roll(seq_t, lag, 0) == seq_t) & (place_t >= lag)
        lag_mask[lag - 1] = same_run.astype(jnp.float32)
    first = lax.broadcasted_iota(jnp.int32, (rows, rows), 0)
    second = lax.broadcasted_iota(jnp.int32, (rows, rows), 1)
    lower = first >= second
    same = lower & (seq_col == seq_wide)
    lanes = lax.broadcasted_iota(jnp.int32, (rows, LANES), 1)
    lane = lax.broadcasted_iota(jnp.int32, (1, LANES), 1)
    at_conv = D * HEADS // LANES
    at_heads = at_conv + (KERNEL + 1) * CHANNELS // LANES
    head_row = small[at_heads : at_heads + 1, :]
    own_head = lane < HEADS
    dt_bias = jnp.where(own_head, head_row, 0.0)
    a_log = jnp.where(own_head, pltpu.roll(head_row, LANES - HEADS, 1), 0.0)

    def tap(number, block):
        place = at_conv + number * (CHANNELS // LANES) + block
        return small[place : place + 1, :]

    def gain_row(block):
        here = small[at_heads + block : at_heads + block + 2, :]
        moved = pltpu.roll(here, LANES - SHIFT, 1)
        return jnp.where(lane < LANES - SHIFT, moved[0:1], moved[1:2])

    def skip_row(block):
        first_lane = 2 * HEADS + PER * block
        sides = [head_row[:, first_lane + i : first_lane + i + 1] for i in range(PER)]
        return jnp.where(lane < HEAD_DIM, sides[0], sides[1])

    turn = 16 * HEADS // LANES
    spots = D // 16
    lane_wide = lax.broadcasted_iota(jnp.int32, (spots, LANES), 1)
    for number in range(16):
        place, off = number * HEADS // LANES, number * HEADS % LANES
        piece = pltpu.roll(small[pl.ds(place, spots, stride=turn), :], (LANES - off) % LANES, 1)
        if off + HEADS > LANES:
            after = pltpu.roll(small[pl.ds(place + 1, spots, stride=turn), :], LANES - off, 1)
            piece = jnp.where(lane_wide < LANES - off, piece, after)
        w_dt_wide[pl.ds(number, spots, stride=16), :] = jnp.where(lane_wide < HEADS, piece, 0.0)
    w_dt = w_dt_wide[...].astype(half)
    gain_in = jnp.concatenate([gain[j : j + 1, :] for j in range(ROWS_GAIN)], 1)
    x = tokens[...].astype(jnp.float32)
    scale_in = lax.rsqrt(row_sum(x * x) * (1.0 / D) + EPS)
    normed[...] = (x * scale_in * gain_in).astype(half)
    live[...] = jnp.where(seq_col[:, 0:1] >= 0, cot[...].astype(jnp.float32), 0.0).astype(half)

    def project(pair):
        both = matmul(normed[...], w_main[:, pair * 2 * LANES : (pair + 1) * 2 * LANES])
        proj[2 * pair] = both[:, :LANES]
        proj[2 * pair + 1] = both[:, LANES:]

    def back_out(pair):
        both = against(live[...], w_out[pair * 2 * LANES : (pair + 1) * 2 * LANES, :])
        grad_hidden[2 * pair] = both[:, :LANES]
        grad_hidden[2 * pair + 1] = both[:, LANES:]

    raw = matmul(normed[...], w_dt) + dt_bias
    steps = jnp.maximum(raw, 0.0) + jnp.log1p(jnp.exp(-jnp.abs(raw)))
    rate = -jnp.exp(a_log)
    logs = exact(lower.astype(jnp.float32), steps * rate)
    logs_t = logs.T
    steps_t = steps.T

    def convolve(block):
        inside = proj[BLOCKS + block]
        total = tap(KERNEL, block) + tap(KERNEL - 1, block) * inside
        for lag in range(1, KERNEL):
            total = total + tap(KERNEL - 1 - lag, block) * (pltpu.roll(inside, lag, 0) * lag_mask[lag - 1])
        gate = jax.nn.sigmoid(total)
        value = total * gate
        active[block] = value
        slope[block] = gate + value * (1.0 - gate)

    project(BLOCKS)
    convolve(BLOCKS)
    convolve(BLOCKS + 1)
    b_mat, c_mat = active[BLOCKS], active[BLOCKS + 1]
    scores = lax.dot_general(
        c_mat, b_mat, (((1,), (1,)), ((), ())), preferred_element_type=jnp.float32, precision=HIGHEST
    )
    squares = jnp.zeros((rows, LANES), jnp.float32)
    cross = jnp.zeros((rows, LANES), jnp.float32)
    for pair in range(BLOCKS // 2):
        project(BLOCKS // 2 + pair)
        project(pair)
        back_out(pair)
        for block in (2 * pair, 2 * pair + 1):
            convolve(block)
            value = active[block]
            parts = []
            for side in range(PER):
                head = PER * block + side
                gap = logs[:, head : head + 1] - logs_t[head : head + 1, :]
                fall = jnp.exp(jnp.where(same, gap, -1e30))
                factor[head] = fall
                mix = ((fall * scores) * steps_t[head : head + 1, :]).astype(half)
                mixed[head] = mix
                parts.append(mix)
            low = value.astype(half)
            zero = jnp.zeros_like(low)
            left = lanes < HEAD_DIM
            stacked = jnp.concatenate(
                [jnp.where(left, low, zero), jnp.where(left, zero, low)], 0
            )
            inside = matmul(jnp.concatenate(parts, 1), stacked)
            total = inside + skip_row(block) * value
            gate = proj[block]
            out = total * (gate * jax.nn.sigmoid(gate))
            scanned[block] = total
            gated[block] = out
            squares = squares + out * out
            cross = cross + out * (grad_hidden[block] * gain_row(block))
    scale = lax.rsqrt(row_sum(squares) * (1.0 / INNER) + EPS)
    pull = row_sum(cross) * (scale * scale * scale) * (1.0 / INNER)
    scale_w = jnp.broadcast_to(scale, (rows, LANES))
    pull_w = jnp.broadcast_to(pull, (rows, LANES))

    def unconvolve(block, grad_active):
        grad = grad_active * slope[block]
        inside = proj[BLOCKS + block]
        total = tap(KERNEL - 1, block) * grad

        def keep(number, row):
            place = START_SMALL + at_conv + number * (CHANNELS // LANES) + block
            main[place : place + 1, :] = row

        keep(KERNEL, col_sum(grad))
        keep(KERNEL - 1, col_sum(grad * inside))
        for lag in range(1, KERNEL):
            kept = grad * lag_mask[lag - 1]
            keep(KERNEL - 1 - lag, col_sum(kept * pltpu.roll(inside, lag, 0)))
            total = total + tap(KERNEL - 1 - lag, block) * pltpu.roll(kept, rows - lag, 0)
        grad_proj[:, INNER + block * LANES : INNER + (block + 1) * LANES] = total.astype(half)

    skip_grad = jnp.zeros((1, LANES), jnp.float32)
    grad_scores = jnp.zeros((rows, rows), jnp.float32)
    row_part = jnp.zeros((rows, LANES), jnp.float32)
    cols[...] = jnp.zeros((LANES, rows), jnp.float32)
    for block in range(BLOCKS):
        span = slice(block * LANES, (block + 1) * LANES)
        out, total, gate, value = gated[block], scanned[block], proj[block], active[block]
        down = grad_hidden[block]
        unit = out * scale_w
        row_gain = gain_row(block)
        hidden[:, span] = (unit * row_gain).astype(half)
        turned[block + 1 : block + 2, :] = pltpu.roll(col_sum(down * unit), SHIFT, 1)
        grad_gated = (down * row_gain) * scale_w - out * pull_w
        sig = jax.nn.sigmoid(gate)
        silu = gate * sig
        grad_total = grad_gated * silu
        grad_proj[:, span] = (grad_gated * total * (sig + silu * (1.0 - sig))).astype(half)
        skip_sums = col_sum(grad_total * value)
        for side in range(PER):
            inside_side = (lane >= side * HEAD_DIM) & (lane < (side + 1) * HEAD_DIM)
            amount = row_sum(jnp.where(inside_side, skip_sums, 0.0))
            skip_grad = jnp.where(lane == 2 * HEADS + PER * block + side, amount, skip_grad)
        low = grad_total.astype(half)
        zero = jnp.zeros_like(low)
        left = lanes < HEAD_DIM
        values_low = value.astype(half)
        tops = jnp.concatenate([jnp.where(left, low, zero), jnp.where(left, zero, low)], 0)
        grad_mix = against(tops, values_low)
        for side in range(PER):
            head = PER * block + side
            through = grad_mix[side * rows : (side + 1) * rows] * factor[head]
            scored = through * scores
            step = steps_t[head : head + 1, :]
            cols[head : head + 1, :] = col_sum(scored)
            row_part = jnp.where(lanes == head, row_sum(scored * step), row_part)
            grad_scores = grad_scores + through * step
        both = over_rows(jnp.concatenate([mixed[PER * block], mixed[PER * block + 1]], 0), tops)
        unconvolve(block, both + skip_row(block) * grad_total)
    low_scores = grad_scores.astype(half)
    unconvolve(BLOCKS + 1, matmul(low_scores, b_mat.astype(half)))
    unconvolve(BLOCKS, over_rows(low_scores, c_mat.astype(half)))
    col_part = cols[...].T
    upper = (first <= second).astype(jnp.float32)
    grad_decay = exact(upper, row_part - col_part * steps)
    grad_steps = col_part + grad_decay * rate
    grad_raw = grad_steps * jax.nn.sigmoid(raw)
    bias_grad = jnp.where(own_head, col_sum(grad_raw), 0.0)
    log_grad = jnp.where(own_head, col_sum(grad_decay * steps) * rate, 0.0)
    turned[0:1, :] = bias_grad + pltpu.roll(log_grad, HEADS, 1) + skip_grad
    rims = turned[0 : BLOCKS + 1, :]
    at_rims = START_SMALL + at_heads
    lane_rims = lax.broadcasted_iota(jnp.int32, (BLOCKS, LANES), 1)
    main[at_rims : at_rims + BLOCKS, :] = jnp.where(lane_rims < SHIFT, rims[:BLOCKS], rims[1:])
    tail[7:8, :] = rims[BLOCKS:]
    grad_dt = jnp.where(own_head, grad_raw, 0.0).astype(half)
    w_dt_wide[...] = over_rows(normed[...], grad_dt)
    lines = [jnp.zeros((spots, LANES), jnp.float32) for _ in range(turn)]
    for number in range(16):
        place, off = number * HEADS // LANES, number * HEADS % LANES
        piece = pltpu.roll(w_dt_wide[pl.ds(number, spots, stride=16), :], off, 1)
        lines[place] = jnp.where((lane_wide >= off) & (lane_wide < off + HEADS), piece, lines[place])
        if off + HEADS > LANES:
            lines[place + 1] = jnp.where(lane_wide < off + HEADS - LANES, piece, lines[place + 1])
    for number in range(turn):
        main[pl.ds(START_SMALL + number, spots, stride=turn), :] = lines[number]
    result[...] = (x + matmul(hidden[...], w_out[...])).astype(half)
    back = against(grad_proj[...], w_main[...]) + against(grad_dt, w_dt)
    gain_grad = col_sum(back * (x * scale_in))
    for j in range(ROWS_GAIN):
        main[j : j + 1, :] = gain_grad[:, j * LANES : (j + 1) * LANES]
    pulled = back * gain_in
    push = row_sum(pulled * x) * (scale_in * scale_in * scale_in) * (1.0 / D)
    grad_input[...] = live[...].astype(jnp.float32) + (pulled * scale_in - x * push)
    tail[8 + ROWS_OUT :, :] = jnp.zeros((tail.shape[0] - 8 - ROWS_OUT, LANES), jnp.float32)
    for pair in range(WIDE // 2):
        both = over_rows(normed[...], grad_proj[:, pair * 2 * LANES : (pair + 1) * 2 * LANES])
        for side in range(2):
            main[pl.ds(ROWS_GAIN + 2 * pair + side, D, stride=WIDE), :] = both[
                :, side * LANES : (side + 1) * LANES
            ]
    for pair in range(THIN // 2):
        both = over_rows(hidden[...], live[:, pair * 2 * LANES : (pair + 1) * 2 * LANES])
        for side in range(2):
            part = pltpu.roll(both[:, side * LANES : (side + 1) * LANES], SHIFT, 1)
            tail[pl.ds(8 + 2 * pair + side, INNER, stride=THIN), :] = part
    edge = START_OUT // 16 * 16

    def cast_main(place, size):
        flat[pl.ds(place, size), :] = main[pl.ds(place, size), :].astype(half)

    in_spans(edge, cast_main)
    early = lax.broadcasted_iota(jnp.int32, (8, LANES), 1) < SHIFT
    seam = jnp.where(early, tail[7:15, :], tail[8:16, :])
    flat[edge : edge + 16, :] = jnp.concatenate([main[edge : edge + 8, :], seam], 0).astype(half)

    def cast_tail(place, size):
        block = tail[pl.ds(place + 16, size), :]
        before = tail[pl.ds(place + 8, size), :]
        joined = jnp.concatenate([before[7:8], block[: size - 1]], 0)
        wide_lanes = lax.broadcasted_iota(jnp.int32, (size, LANES), 1)
        flat[pl.ds(edge + 16 + place, size), :] = jnp.where(wide_lanes < SHIFT, joined, block).astype(half)

    in_spans(flat.shape[0] - edge - 16, cast_tail)


def block_pass(tokens, cotangent, seq_ids, weights, total):
    w_main, w_out, small, gain = weights
    rows = tokens.shape[0]
    f32, half = jnp.float32, jnp.bfloat16
    vmem = pl.BlockSpec(memory_space=pltpu.VMEM)
    shape = jax.ShapeDtypeStruct
    block = (rows, LANES)
    flat_rows = total // LANES
    return pl.pallas_call(
        mixer_kernel,
        out_shape=(shape((rows, D), half), shape((rows, D), f32), shape((flat_rows, LANES), half)),
        in_specs=[vmem] * 7,
        out_specs=(vmem,) * 3,
        scratch_shapes=[
            pltpu.VMEM((rows, D), half),
            pltpu.VMEM((rows, INNER + CHANNELS), half),
            pltpu.VMEM((rows, INNER), half),
            pltpu.VMEM((rows, D), half),
            pltpu.VMEM((D, LANES), f32),
            pltpu.VMEM((WIDE, *block), f32),
            pltpu.VMEM((BLOCKS + 2, *block), f32),
            pltpu.VMEM((BLOCKS + 2, *block), f32),
            pltpu.VMEM((BLOCKS, *block), f32),
            pltpu.VMEM((BLOCKS, *block), f32),
            pltpu.VMEM((BLOCKS, *block), f32),
            pltpu.VMEM((HEADS, rows, rows), f32),
            pltpu.VMEM((HEADS, rows, rows), half),
            pltpu.VMEM((LANES, rows), f32),
            pltpu.VMEM((KERNEL - 1, *block), f32),
            pltpu.VMEM((16, LANES), f32),
            pltpu.VMEM((START_OUT, LANES), f32),
            pltpu.VMEM((flat_rows - START_OUT + 16, LANES), f32),
        ],
        compiler_params=pltpu.CompilerParams(vmem_limit_bytes=56 * 1024 * 1024),
    )(tokens, cotangent, seq_ids[None, :], gain, small, w_main, w_out)


def adamw(weight, first, second, grad, step_count):
    steps_done = step_count[0].astype(jnp.float32)
    first_new = BETA_ONE * first + (1.0 - BETA_ONE) * grad
    second_new = BETA_TWO * second + (1.0 - BETA_TWO) * grad * grad
    first_hat = first_new / (1.0 - jnp.power(BETA_ONE, steps_done))
    second_hat = second_new / (1.0 - jnp.power(BETA_TWO, steps_done))
    weight_new = weight - LEARN_RATE * (
        first_hat / (jnp.sqrt(second_hat) + ADAM_EPS) + WEIGHT_DECAY * weight
    )
    return (weight_new, first_new, second_new)


def per_device(tokens, cotangent, seq_ids, params, first_moment, second_moment, step_count):
    width = params.shape[0]
    weights = gather_weights(
        params.reshape(width // LANES, LANES), lax.axis_size("shard"), lax.axis_size("dp")
    )
    total = width * lax.axis_size("shard") * lax.axis_size("dp")
    result, grad_input, flat = block_pass(tokens, cotangent, seq_ids, weights, total)
    owned = scatter_sum(flat, lax.axis_size("shard"), lax.axis_size("dp"), width // LANES)
    owned = owned.reshape(width)
    new_weight, new_first, new_second = adamw(
        params, first_moment, second_moment, owned, step_count
    )
    return (result, grad_input, owned, new_weight, new_first, new_second)


def solution(mesh):
    return jax.shard_map(
        per_device,
        mesh=mesh,
        in_specs=(
            P(("dp", "shard"), None),
            P(("dp", "shard"), None),
            P(("dp", "shard")),
            P(("dp", "shard")),
            P(("dp", "shard")),
            P(("dp", "shard")),
            P(),
        ),
        out_specs=(
            P(("dp", "shard"), None),
            P(("dp", "shard"), None),
            P(("dp", "shard")),
            P(("dp", "shard")),
            P(("dp", "shard")),
            P(("dp", "shard")),
        ),
        check_vma=False,
    )
```

```python
import functools

import jax
import jax.numpy as jnp
from jax import lax
from jax.experimental import pallas as pl
from jax.experimental.pallas import tpu as pltpu
from jax.sharding import PartitionSpec as P

D = 768
HEADS = 24
HEAD_DIM = 64
STATE = 128
KERNEL = 4
INNER = 1536
CHANNELS = 1792
LANES = 128
CUTS = 4
LAG = 3
AHEAD = 8
MESH = pl.DeviceIdType.MESH
PACKED = D + D * (INNER + CHANNELS) + D * HEADS + (KERNEL + 1) * CHANNELS + 3 * HEADS + INNER + INNER * D


EPS = 1e-05
BETA_ONE = 0.9
BETA_TWO = 0.999
ADAM_EPS = 1e-08
LEARN_RATE = 0.01
WEIGHT_DECAY = 0.1


def matmul(left, right):
    return jnp.dot(left, right, preferred_element_type=jnp.float32)


def over_rows(left, right):
    return lax.dot_general(
        left, right, (((0,), (0,)), ((), ())), preferred_element_type=jnp.float32
    )


def against(left, right):
    return lax.dot_general(
        left, right, (((1,), (1,)), ((), ())), preferred_element_type=jnp.float32
    )


ROWS_GAIN = D // LANES
ROWS_MAIN = D * (INNER + CHANNELS) // LANES
START_SMALL = ROWS_GAIN + ROWS_MAIN
START_OUT = (PACKED - INNER * D) // LANES
SHIFT = (PACKED - INNER * D) % LANES
ROWS_OUT = INNER * D // LANES
ROWS_SMALL = START_OUT + 1 - START_SMALL
WIDE = (INNER + CHANNELS) // LANES
THIN = D // LANES


def flip(place, number, size):
    if size & (size - 1):
        return lax.rem(place + number, size)
    bit = 1
    while bit <= number:
        if number & bit:
            place = place + bit - 2 * bit * lax.rem(lax.div(place, bit), 2)
        bit = 2 * bit
    return place


def unflip(place, number, size):
    return lax.rem(place + size - number, size) if size & (size - 1) else flip(place, number, size)


def slice_grid(group_count, wide_count):
    wide = group_count // 2
    tall = wide if wide_count % wide == 0 else 1
    return wide_count // tall, tall, wide


def slice_cuts(rows):
    step = -(-rows // (CUTS * 16)) * 16
    return [(start, min(step, rows - start)) for start in range(0, rows, step)]


class Neighbours:
    def __init__(self, grid):
        deep, tall, wide = self.grid = grid
        dp, shard = lax.axis_index("dp"), lax.axis_index("shard")
        z, y = lax.div(dp, tall), lax.rem(dp, tall)
        x, c = lax.div(shard, 2), lax.rem(shard, 2)
        self.z, self.y, self.x, self.c = z, y, x, c
        self.xs = [lax.rem(x + j, wide) for j in range(1, wide)]
        self.ys = [lax.rem(y + j, tall) for j in range(1, tall)]
        self.to_x = [self.place(z, y, p, c) for p in self.xs]
        self.to_y = [self.place(z, p, x, c) for p in self.ys]
        self.out_z = [None] + [self.place(unflip(z, i, deep), y, x, c) for i in range(1, deep)]
        self.partner = self.place(z, y, x, 1 - c)

    def place(self, z, y, x, c):
        return (z * self.grid[1] + y, x * 2 + c)

    def meet(self):
        everyone = [self.partner] + self.to_x + self.to_y + self.out_z[1:]
        barrier = pltpu.get_barrier_semaphore()
        for peer in everyone:
            pl.semaphore_signal(barrier, inc=1, device_id=peer, device_id_type=MESH)
        pl.semaphore_wait(barrier, len(everyone))


def scatter_part(near, cuts, pack_plane, data, out, last, send_sem, recv_sem, refs):
    deep, tall, wide = near.grid
    z, y, x, c = near.z, near.y, near.x, near.c
    sent = []

    def push(item, number, src, dst, peer):
        copy = pltpu.make_async_remote_copy(
            src_ref=src,
            dst_ref=dst,
            send_sem=send_sem.at[item, number],
            recv_sem=recv_sem.at[item, number],
            device_id=peer,
            device_id_type=MESH,
        )
        copy.start()
        sent.append(copy)
        return copy

    def total(parts):
        value = parts[0].astype(jnp.float32)
        for part in parts[1:]:
            value = value + part.astype(jnp.float32)
        return value

    first_x, first_y, first_z = 1, wide, wide + tall - 1
    order = [(i, k) for i in list(range(deep - 1, 0, -1)) + [0] for k in range(len(cuts))]
    held = {}
    for item, key in enumerate(order):
        held[key] = refs[item * 6 : item * 6 + 1] + refs[item * 6 : item * 6 + 6]
    flights = {}

    def stage_zero(item):
        i, k = order[item]
        start, size = cuts[k]
        if k == 0:
            pack_plane(unflip(z, i, deep))
        src = data.at[unflip(z, i, deep), :, :, 1 - c, start : start + size]
        flights[item] = [push(item, 0, src, held[i, k][0], near.partner)]

    def stage_one(item):
        i, k = order[item]
        start, size = cuts[k]
        got, acc, got_one = held[i, k][:3]
        plane = unflip(z, i, deep)
        for copy in flights[item]:
            copy.wait_recv()

        def add(step, carry):
            yi, xi = lax.div(step, wide), lax.rem(step, wide)
            mine = data[plane, yi, xi, c, start : start + size, :]
            acc[yi, xi] = total([mine, got[yi, xi]]).astype(jnp.bfloat16)
            return carry

        lax.fori_loop(0, tall * wide, add, 0)
        if k % 2 == 0:
            flights[item] = [
                push(item, first_x + j, acc.at[:, p], got_one.at[j], near.to_x[j])
                for j, p in enumerate(near.xs)
            ]
        else:
            flights[item] = [
                push(item, first_y + j, acc.at[p], got_one.at[j], near.to_y[j])
                for j, p in enumerate(near.ys)
            ]

    def stage_two(item):
        i, k = order[item]
        acc, got_one, acc_two, got_two = held[i, k][1:5]
        for copy in flights[item]:
            copy.wait_recv()

        def add(other, carry):
            mine = acc[other, x] if k % 2 == 0 else acc[y, other]
            parts = [mine] + [got_one[j, other] for j in range(got_one.shape[0])]
            acc_two[other] = total(parts).astype(jnp.bfloat16)
            return carry

        lax.fori_loop(0, tall if k % 2 == 0 else wide, add, 0)
        if k % 2 == 0:
            flights[item] = [
                push(item, first_y + j, acc_two.at[p], got_two.at[j], near.to_y[j])
                for j, p in enumerate(near.ys)
            ]
        else:
            flights[item] = [
                push(item, first_x + j, acc_two.at[p], got_two.at[j], near.to_x[j])
                for j, p in enumerate(near.xs)
            ]

    across = {}

    def stage_three(item):
        i, k = order[item]
        start, size = cuts[k]
        acc_two, got_two, acc_three, got_z = held[i, k][3:]
        for copy in flights[item]:
            copy.wait_recv()
        mine = y if k % 2 == 0 else x
        parts = [acc_two[mine]] + [got_two[j] for j in range(got_two.shape[0])]
        if i:
            acc_three[...] = total(parts).astype(jnp.bfloat16)
            across[i, k] = push(item, first_z, acc_three, got_z, near.out_z[i])
        else:
            value = total(parts)
            if deep == 1:
                last[start : start + size, :] = jnp.zeros((size, LANES), jnp.bfloat16)
            for j in range(1, deep):
                across[j, k].wait_recv()
                if j < deep - 1:
                    value = value + held[j, k][6][...].astype(jnp.float32)
                else:
                    last[start : start + size, :] = held[j, k][6][...]
            out[start : start + size, :] = value

    in_waves((stage_zero, stage_one, stage_two, stage_three), len(order), (0, 2, 5, 8))
    for copy in sent:
        copy.wait_send()


def in_waves(stages, count, lags):
    for wave in range(count + lags[-1]):
        for stage, lag in zip(stages, lags):
            if 0 <= wave - lag < count:
                stage(wave - lag)


def scatter_scratch(grid, cuts):
    deep, tall, wide = grid
    scratch = []
    for _ in range(deep):
        for k, (start, size) in enumerate(cuts):
            lead, other = (wide, tall) if k % 2 == 0 else (tall, wide)
            for shape in (
                (tall, wide),
                (lead - 1, other),
                (other,),
                (other - 1,),
                (),
                (),
            ):
                scratch.append(pltpu.VMEM((*shape, size, LANES), jnp.bfloat16))
    return scratch


def gather_part(near, cuts, params, w_main, w_out, small, gain, own, out, flat, send_sem, recv_sem):
    deep, tall, wide = near.grid
    z, y, x, c = near.z, near.y, near.x, near.c
    sent = []
    size_own = own.shape[0]
    size_plane = tall * wide * 2 * size_own
    own[...] = params[...].astype(jnp.bfloat16)

    def push(item, number, src, dst, peers):
        started = []
        for j, peer in enumerate(peers):
            copy = pltpu.make_async_remote_copy(
                src_ref=src,
                dst_ref=dst,
                send_sem=send_sem.at[item, number + j],
                recv_sem=recv_sem.at[item, number + j],
                device_id=peer,
                device_id_type=MESH,
            )
            copy.start()
            started.append(copy)
        sent.extend(started)
        return started

    first_x, first_y, first_z = 1, wide, wide + tall - 1
    order = [(i, k) for i in range(deep) for k in range(len(cuts))]
    flights = {}

    def start_z(item):
        i, k = order[item]
        if i:
            rows = pl.ds(*cuts[k])
            flights[item] = push(item, first_z, own.at[rows], out.at[z, y, x, c, rows], [near.out_z[i]])

    def next_z(wave):
        if wave + AHEAD < len(order):
            start_z(wave + AHEAD)

    def stage_one(item):
        i, k = order[item]
        rows = pl.ds(*cuts[k])
        for copy in flights.get(item, []):
            copy.wait_recv()
        block = out.at[flip(z, i, deep), y, x, c, rows]
        source = block if i else own.at[rows]
        if k % 2 == 0:
            flights[item] = push(item, first_y, source, block, near.to_y)
        else:
            flights[item] = push(item, first_x, source, block, near.to_x)
        if item == 0:
            out[z, y, x, c] = own[...]

    def stage_two(item):
        i, k = order[item]
        rows = pl.ds(*cuts[k])
        for copy in flights[item]:
            copy.wait_recv()
        plane = flip(z, i, deep)
        if k % 2 == 0:
            line = out.at[plane, :, x, c, rows]
            flights[item] = push(item, first_x, line, line, near.to_x)
        else:
            line = out.at[plane, y, :, c, rows]
            flights[item] = push(item, first_y, line, line, near.to_y)

    def stage_three(item):
        i, k = order[item]
        for copy in flights[item]:
            copy.wait_recv()
        sheet = out.at[flip(z, i, deep), :, :, c, pl.ds(*cuts[k])]
        flights[item] = push(item, 0, sheet, sheet, [near.partner])

    def main_block(number, carry):
        for j in range(WIDE):
            piece = flat[pl.ds(ROWS_GAIN + number * (16 * WIDE) + j, 16, stride=WIDE), :]
            w_main[pl.ds(pl.multiple_of(number * 16, 16), 16), j * LANES : (j + 1) * LANES] = piece.astype(
                jnp.bfloat16
            )
        return carry

    early = lax.broadcasted_iota(jnp.int32, (16, LANES), 1) < LANES - SHIFT

    def out_block(number, carry):
        turned = [
            pltpu.roll(flat[pl.ds(START_OUT + number * (16 * THIN) + j, 16, stride=THIN), :], LANES - SHIFT, 1)
            for j in range(THIN + 1)
        ]
        for j in range(THIN):
            w_out[pl.ds(pl.multiple_of(number * 16, 16), 16), j * LANES : (j + 1) * LANES] = jnp.where(
                early, turned[j], turned[j + 1]
            ).astype(jnp.bfloat16)
        return carry

    kinds = (
        (main_block, ROWS_GAIN, 16 * WIDE, 16 * WIDE, D // 16),
        (out_block, START_OUT, 16 * THIN, 16 * THIN + 1, INNER // 16),
    )

    def unpack_plane(plane):
        low = plane * size_plane
        for body, base, step, reach, count in kinds:
            begin = jnp.clip(lax.div(low - base + step * (count + 1) - 1, step) - count, 0, count)
            end = jnp.clip(lax.div(low + size_plane - base - reach + step * (count + 1), step) - count, 0, count)
            lax.fori_loop(begin, jnp.maximum(begin, end), body, 0)

    def stage_four(item):
        i, k = order[item]
        start, size = cuts[k]
        for copy in flights[item]:
            copy.wait_recv()
        plane = flip(z, i, deep)

        def widen(step, carry):
            yi, rest = lax.div(step, wide * 2), lax.rem(step, wide * 2)
            xi, ci = lax.div(rest, 2), lax.rem(rest, 2)
            place = plane * size_plane + step * size_own + start
            if size_own % 8 == 0:
                place = pl.multiple_of(place, 8)
            flat[pl.ds(place, size), :] = out[plane, yi, xi, ci, start : start + size, :].astype(jnp.float32)
            return carry

        lax.fori_loop(0, tall * wide * 2, widen, 0)
        if k == len(cuts) - 1:
            unpack_plane(plane)

    for item in range(min(AHEAD, len(order))):
        start_z(item)
    in_waves(
        (next_z, stage_one, stage_two, stage_three, stage_four), len(order), (0, 0, LAG, 2 * LAG, 2 * LAG + 2)
    )
    for body, base, step, reach, count in kinds:
        for number in range(count):
            low = base + number * step
            if low // size_plane != (low + reach - 1) // size_plane:
                body(number, 0)
    gain[0:ROWS_GAIN, :] = flat[0:ROWS_GAIN, :]
    gain[ROWS_GAIN:, :] = jnp.zeros((8 - ROWS_GAIN, LANES), jnp.float32)
    small[...] = flat[START_SMALL : START_SMALL + small.shape[0], :]
    for copy in sent:
        copy.wait_send()


HIGHEST = lax.Precision.HIGHEST
BLOCKS = INNER // LANES
PER = LANES // HEAD_DIM


def exact(left, right):
    return jnp.dot(left, right, preferred_element_type=jnp.float32, precision=HIGHEST)


def row_sum(value):
    return jnp.sum(value, axis=1, keepdims=True)


def col_sum(value):
    return jnp.sum(value, axis=0, keepdims=True)


def mixer_part(
    tokens, cot, seq_row, gain, small, w_main, w_out, result, grad_input,
    normed, grad_proj, hidden, live, w_dt_wide, normed_t, hidden_t,
    proj, slope, active, scanned, gated, grad_hidden, factor, mixed, cols, lag_mask, turned, main, tail,
):
    rows = tokens.shape[0]
    half = jnp.bfloat16
    seq_wide = jnp.broadcast_to(seq_row[...], (rows, rows)).astype(jnp.float32)
    seq_col = seq_wide.T
    seq_t = jnp.broadcast_to(seq_col[:, 0:1], (rows, LANES))
    place_t = lax.broadcasted_iota(jnp.int32, (rows, LANES), 0)
    for lag in range(1, KERNEL):
        same_run = (pltpu.roll(seq_t, lag, 0) == seq_t) & (place_t >= lag)
        lag_mask[lag - 1] = same_run.astype(jnp.float32)
    first = lax.broadcasted_iota(jnp.int32, (rows, rows), 0)
    second = lax.broadcasted_iota(jnp.int32, (rows, rows), 1)
    lower = first >= second
    same = lower & (seq_col == seq_wide)
    lanes = lax.broadcasted_iota(jnp.int32, (rows, LANES), 1)
    lane = lax.broadcasted_iota(jnp.int32, (1, LANES), 1)
    at_conv = D * HEADS // LANES
    at_heads = at_conv + (KERNEL + 1) * CHANNELS // LANES
    head_row = small[at_heads : at_heads + 1, :]
    own_head = lane < HEADS
    dt_bias = jnp.where(own_head, head_row, 0.0)
    a_log = jnp.where(own_head, pltpu.roll(head_row, LANES - HEADS, 1), 0.0)

    def tap(number, block):
        place = at_conv + number * (CHANNELS // LANES) + block
        return small[place : place + 1, :]

    def gain_row(block):
        here = small[at_heads + block : at_heads + block + 2, :]
        moved = pltpu.roll(here, LANES - SHIFT, 1)
        return jnp.where(lane < LANES - SHIFT, moved[0:1], moved[1:2])

    def skip_row(block):
        first_lane = 2 * HEADS + PER * block
        sides = [head_row[:, first_lane + i : first_lane + i + 1] for i in range(PER)]
        return jnp.where(lane < HEAD_DIM, sides[0], sides[1])

    turn = 16 * HEADS // LANES
    spots = D // 16
    lane_wide = lax.broadcasted_iota(jnp.int32, (spots, LANES), 1)
    for number in range(16):
        place, off = number * HEADS // LANES, number * HEADS % LANES
        piece = pltpu.roll(small[pl.ds(place, spots, stride=turn), :], (LANES - off) % LANES, 1)
        if off + HEADS > LANES:
            after = pltpu.roll(small[pl.ds(place + 1, spots, stride=turn), :], LANES - off, 1)
            piece = jnp.where(lane_wide < LANES - off, piece, after)
        w_dt_wide[pl.ds(number, spots, stride=16), :] = jnp.where(lane_wide < HEADS, piece, 0.0)
    w_dt = w_dt_wide[...].astype(half)
    gain_in = jnp.concatenate([gain[j : j + 1, :] for j in range(ROWS_GAIN)], 1)
    x = tokens[...].astype(jnp.float32)
    scale_in = lax.rsqrt(row_sum(x * x) * (1.0 / D) + EPS)
    normed_full = x * scale_in * gain_in
    normed[...] = normed_full.astype(half)
    for j in range(D // LANES):
        spot = slice(j * LANES, (j + 1) * LANES)
        normed_t[spot, :] = normed_full[:, spot].T.astype(half)
    live[...] = jnp.where(seq_col[:, 0:1] >= 0, cot[...].astype(jnp.float32), 0.0).astype(half)

    def project(pair):
        both = matmul(normed[...], w_main[:, pair * 2 * LANES : (pair + 1) * 2 * LANES])
        proj[2 * pair] = both[:, :LANES]
        proj[2 * pair + 1] = both[:, LANES:]

    def back_out(pair):
        both = against(live[...], w_out[pair * 2 * LANES : (pair + 1) * 2 * LANES, :])
        grad_hidden[2 * pair] = both[:, :LANES]
        grad_hidden[2 * pair + 1] = both[:, LANES:]

    raw = matmul(normed[...], w_dt) + dt_bias
    steps = jnp.maximum(raw, 0.0) + jnp.log1p(jnp.exp(-jnp.abs(raw)))
    rate = -jnp.exp(a_log)
    logs = exact(lower.astype(jnp.float32), steps * rate)
    logs_t = logs.T
    steps_t = steps.T

    def convolve(block):
        inside = proj[BLOCKS + block]
        total = tap(KERNEL, block) + tap(KERNEL - 1, block) * inside
        for lag in range(1, KERNEL):
            total = total + tap(KERNEL - 1 - lag, block) * (pltpu.roll(inside, lag, 0) * lag_mask[lag - 1])
        gate = jax.nn.sigmoid(total)
        value = total * gate
        active[block] = value
        slope[block] = gate + value * (1.0 - gate)

    project(BLOCKS)
    convolve(BLOCKS)
    convolve(BLOCKS + 1)
    b_mat, c_mat = active[BLOCKS], active[BLOCKS + 1]
    scores = lax.dot_general(
        c_mat, b_mat, (((1,), (1,)), ((), ())), preferred_element_type=jnp.float32, precision=HIGHEST
    )
    squares = jnp.zeros((rows, LANES), jnp.float32)
    cross = jnp.zeros((rows, LANES), jnp.float32)
    for pair in range(BLOCKS // 2):
        project(BLOCKS // 2 + pair)
        project(pair)
        back_out(pair)
        for block in (2 * pair, 2 * pair + 1):
            convolve(block)
            value = active[block]
            parts = []
            for side in range(PER):
                head = PER * block + side
                gap = logs[:, head : head + 1] - logs_t[head : head + 1, :]
                fall = jnp.exp(jnp.where(same, gap, -1e30))
                factor[head] = fall
                mix = ((fall * scores) * steps_t[head : head + 1, :]).astype(half)
                mixed[head] = mix
                parts.append(mix)
            low = value.astype(half)
            zero = jnp.zeros_like(low)
            left = lanes < HEAD_DIM
            stacked = jnp.concatenate(
                [jnp.where(left, low, zero), jnp.where(left, zero, low)], 0
            )
            inside = matmul(jnp.concatenate(parts, 1), stacked)
            total = inside + skip_row(block) * value
            gate = proj[block]
            out = total * (gate * jax.nn.sigmoid(gate))
            scanned[block] = total
            gated[block] = out
            squares = squares + out * out
            cross = cross + out * (grad_hidden[block] * gain_row(block))
    scale = lax.rsqrt(row_sum(squares) * (1.0 / INNER) + EPS)
    pull = row_sum(cross) * (scale * scale * scale) * (1.0 / INNER)
    scale_w = jnp.broadcast_to(scale, (rows, LANES))
    pull_w = jnp.broadcast_to(pull, (rows, LANES))

    def unconvolve(block, grad_active):
        grad = grad_active * slope[block]
        inside = proj[BLOCKS + block]
        total = tap(KERNEL - 1, block) * grad

        def keep(number, row):
            place = START_SMALL + at_conv + number * (CHANNELS // LANES) + block
            main[place : place + 1, :] = row

        keep(KERNEL, col_sum(grad))
        keep(KERNEL - 1, col_sum(grad * inside))
        for lag in range(1, KERNEL):
            kept = grad * lag_mask[lag - 1]
            keep(KERNEL - 1 - lag, col_sum(kept * pltpu.roll(inside, lag, 0)))
            total = total + tap(KERNEL - 1 - lag, block) * pltpu.roll(kept, rows - lag, 0)
        grad_proj[:, INNER + block * LANES : INNER + (block + 1) * LANES] = total.astype(half)

    skip_grad = jnp.zeros((1, LANES), jnp.float32)
    grad_scores = jnp.zeros((rows, rows), jnp.float32)
    row_part = jnp.zeros((rows, LANES), jnp.float32)
    cols[...] = jnp.zeros((LANES, rows), jnp.float32)
    for block in range(BLOCKS):
        span = slice(block * LANES, (block + 1) * LANES)
        out, total, gate, value = gated[block], scanned[block], proj[block], active[block]
        down = grad_hidden[block]
        unit = out * scale_w
        row_gain = gain_row(block)
        hidden[:, span] = (unit * row_gain).astype(half)
        hidden_t[span, :] = (unit * row_gain).T.astype(half)
        turned[block + 1 : block + 2, :] = pltpu.roll(col_sum(down * unit), SHIFT, 1)
        grad_gated = (down * row_gain) * scale_w - out * pull_w
        sig = jax.nn.sigmoid(gate)
        silu = gate * sig
        grad_total = grad_gated * silu
        grad_proj[:, span] = (grad_gated * total * (sig + silu * (1.0 - sig))).astype(half)
        skip_sums = col_sum(grad_total * value)
        for side in range(PER):
            inside_side = (lane >= side * HEAD_DIM) & (lane < (side + 1) * HEAD_DIM)
            amount = row_sum(jnp.where(inside_side, skip_sums, 0.0))
            skip_grad = jnp.where(lane == 2 * HEADS + PER * block + side, amount, skip_grad)
        low = grad_total.astype(half)
        zero = jnp.zeros_like(low)
        left = lanes < HEAD_DIM
        values_low = value.astype(half)
        tops = jnp.concatenate([jnp.where(left, low, zero), jnp.where(left, zero, low)], 0)
        grad_mix = against(tops, values_low)
        for side in range(PER):
            head = PER * block + side
            through = grad_mix[side * rows : (side + 1) * rows] * factor[head]
            scored = through * scores
            step = steps_t[head : head + 1, :]
            cols[head : head + 1, :] = col_sum(scored)
            row_part = jnp.where(lanes == head, row_sum(scored * step), row_part)
            grad_scores = grad_scores + through * step
        both = over_rows(jnp.concatenate([mixed[PER * block], mixed[PER * block + 1]], 0), tops)
        unconvolve(block, both + skip_row(block) * grad_total)
    low_scores = grad_scores.astype(half)
    unconvolve(BLOCKS + 1, matmul(low_scores, b_mat.astype(half)))
    unconvolve(BLOCKS, over_rows(low_scores, c_mat.astype(half)))
    col_part = cols[...].T
    upper = (first <= second).astype(jnp.float32)
    grad_decay = exact(upper, row_part - col_part * steps)
    grad_steps = col_part + grad_decay * rate
    grad_raw = grad_steps * jax.nn.sigmoid(raw)
    bias_grad = jnp.where(own_head, col_sum(grad_raw), 0.0)
    log_grad = jnp.where(own_head, col_sum(grad_decay * steps) * rate, 0.0)
    turned[0:1, :] = bias_grad + pltpu.roll(log_grad, HEADS, 1) + skip_grad
    rims = turned[0 : BLOCKS + 1, :]
    at_rims = START_SMALL + at_heads
    lane_rims = lax.broadcasted_iota(jnp.int32, (BLOCKS, LANES), 1)
    main[at_rims : at_rims + BLOCKS, :] = jnp.where(lane_rims < SHIFT, rims[:BLOCKS], rims[1:])
    tail[7:8, :] = rims[BLOCKS:]
    grad_dt = jnp.where(own_head, grad_raw, 0.0).astype(half)
    w_dt_wide[...] = matmul(normed_t[...], grad_dt)
    lines = [jnp.zeros((spots, LANES), jnp.float32) for _ in range(turn)]
    for number in range(16):
        place, off = number * HEADS // LANES, number * HEADS % LANES
        piece = pltpu.roll(w_dt_wide[pl.ds(number, spots, stride=16), :], off, 1)
        lines[place] = jnp.where((lane_wide >= off) & (lane_wide < off + HEADS), piece, lines[place])
        if off + HEADS > LANES:
            lines[place + 1] = jnp.where(lane_wide < off + HEADS - LANES, piece, lines[place + 1])
    for number in range(turn):
        main[pl.ds(START_SMALL + number, spots, stride=turn), :] = lines[number]
    result[...] = (x + matmul(hidden[...], w_out[...])).astype(half)
    back = against(grad_proj[...], w_main[...]) + against(grad_dt, w_dt)
    gain_grad = col_sum(back * (x * scale_in))
    for j in range(ROWS_GAIN):
        main[j : j + 1, :] = gain_grad[:, j * LANES : (j + 1) * LANES]
    pulled = back * gain_in
    push = row_sum(pulled * x) * (scale_in * scale_in * scale_in) * (1.0 / D)
    grad_input[...] = live[...].astype(jnp.float32) + (pulled * scale_in - x * push)


def packer(near, size_own, normed_t, grad_proj, hidden_t, live, main, tail, flat, data):
    deep, tall, wide = near.grid
    size_plane = tall * wide * 2 * size_own
    mixed_owner = START_OUT // size_own

    def main_block(number, carry):
        left = normed_t[pl.ds(pl.multiple_of(number * LANES, LANES), LANES), :]
        for pair in range(WIDE // 2):
            both = matmul(left, grad_proj[:, pair * 2 * LANES : (pair + 1) * 2 * LANES])
            for side in range(2):
                place = ROWS_GAIN + number * (LANES * WIDE) + 2 * pair + side
                main[pl.ds(place, LANES, stride=WIDE), :] = both[:, side * LANES : (side + 1) * LANES]
        return carry

    def out_block(number, carry):
        left = hidden_t[pl.ds(pl.multiple_of(number * LANES, LANES), LANES), :]
        for pair in range(THIN // 2):
            both = matmul(left, live[:, pair * 2 * LANES : (pair + 1) * 2 * LANES])
            for side in range(2):
                place = 8 + number * (LANES * THIN) + 2 * pair + side
                tail[pl.ds(place, LANES, stride=THIN), :] = pltpu.roll(
                    both[:, side * LANES : (side + 1) * LANES], SHIFT, 1
                )
        return carry

    kinds = (
        (main_block, ROWS_GAIN, LANES * WIDE, LANES * WIDE, D // LANES),
        (out_block, START_OUT, LANES * THIN, LANES * THIN + 1, INNER // LANES),
    )

    def joined(rows):
        early = lax.broadcasted_iota(jnp.int32, (rows.shape[0] - 8, LANES), 1) < SHIFT
        return jnp.where(early, rows[7 : rows.shape[0] - 1], rows[8:])

    def cast(step, plane):
        yi, rest = lax.div(step, wide * 2), lax.rem(step, wide * 2)
        xi, ci = lax.div(rest, 2), lax.rem(rest, 2)
        owner = plane * (tall * wide * 2) + step
        base = owner * size_own
        if size_own % 8 == 0:
            base = pl.multiple_of(base, 8)

        @pl.when(owner < mixed_owner)
        def _():
            data[plane, yi, xi, ci] = flat[pl.ds(base, size_own), :].astype(jnp.bfloat16)

        @pl.when(owner > mixed_owner)
        def _():
            data[plane, yi, xi, ci] = joined(flat[pl.ds(base, size_own + 8), :]).astype(jnp.bfloat16)

        @pl.when(owner == mixed_owner)
        def _():
            first = mixed_owner * size_own
            under = START_OUT - first
            after = joined(flat[START_OUT : first + size_own + 8, :])
            both = jnp.concatenate([flat[first:START_OUT, :], after], 0) if under else after
            data[plane, yi, xi, ci] = both.astype(jnp.bfloat16)

        return plane

    def pack_plane(plane):
        low = plane * size_plane
        for body, base, step, reach, count in kinds:
            begin = jnp.clip(lax.div(low - base - reach + step * (count + 1), step) - count, 0, count)
            end = jnp.clip(lax.div(low + size_plane - base + step * (count + 1) - 1, step) - count, 0, count)
            lax.fori_loop(begin, jnp.maximum(begin, end), body, 0)
        lax.fori_loop(0, tall * wide * 2, cast, plane)

    return pack_plane


def whole_kernel(
    grid, cuts, params, tokens, cot, seq_row, result, grad_input, most, last,
    w_main, w_out, small, gain, own, data, flat, gather_send, gather_recv, scatter_send, scatter_recv,
    normed, grad_proj, hidden, live, w_dt_wide, normed_t, hidden_t,
    proj, slope, active, scanned, gated, grad_hidden, factor, mixed, cols, lag_mask, turned, *refs,
):
    near = Neighbours(grid)
    near.meet()
    gather_part(near, cuts, params, w_main, w_out, small, gain, own, data, flat, gather_send, gather_recv)
    main = flat.at[0:START_OUT]
    tail = flat.at[START_OUT : flat.shape[0]]
    mixer_part(
        tokens, cot, seq_row, gain, small, w_main, w_out, result, grad_input,
        normed, grad_proj, hidden, live, w_dt_wide, normed_t, hidden_t,
        proj, slope, active, scanned, gated, grad_hidden, factor, mixed, cols, lag_mask, turned, main, tail,
    )
    rest = flat.shape[0] - START_OUT - 8 - ROWS_OUT
    flat[START_OUT + 8 + ROWS_OUT :, :] = jnp.zeros((rest, LANES), jnp.float32)
    pack_plane = packer(near, own.shape[0], normed_t, grad_proj, hidden_t, live, main, tail, flat, data)
    scatter_part(near, cuts, pack_plane, data, most, last, scatter_send, scatter_recv, refs)


def run_block(tokens, cotangent, seq_ids, params, group_count, wide_count):
    rows, own_rows = tokens.shape[0], params.shape[0]
    deep, tall, wide = grid = slice_grid(group_count, wide_count)
    cuts = slice_cuts(own_rows)
    f32, half = jnp.float32, jnp.bfloat16
    vmem = pl.BlockSpec(memory_space=pltpu.VMEM)
    shape = jax.ShapeDtypeStruct
    block = (rows, LANES)
    flat_rows = wide_count * group_count * own_rows
    sems = pltpu.SemaphoreType.DMA((deep * len(cuts), wide + tall))
    return pl.pallas_call(
        functools.partial(whole_kernel, grid, cuts),
        out_shape=(
            shape((rows, D), half),
            shape((rows, D), f32),
            shape((own_rows, LANES), f32),
            shape((own_rows, LANES), half),
        ),
        in_specs=[vmem] * 4,
        out_specs=(vmem,) * 4,
        scratch_shapes=[
            pltpu.VMEM((D, INNER + CHANNELS), half),
            pltpu.VMEM((INNER, D), half),
            pltpu.VMEM((-(-ROWS_SMALL // 8) * 8, LANES), f32),
            pltpu.VMEM((8, LANES), f32),
            pltpu.VMEM((own_rows, LANES), half),
            pltpu.VMEM((deep, tall, wide, 2, own_rows, LANES), half),
            pltpu.VMEM((flat_rows + 16, LANES), f32),
            sems,
            sems,
            sems,
            sems,
            pltpu.VMEM((rows, D), half),
            pltpu.VMEM((rows, INNER + CHANNELS), half),
            pltpu.VMEM((rows, INNER), half),
            pltpu.VMEM((rows, D), half),
            pltpu.VMEM((D, LANES), f32),
            pltpu.VMEM((D, rows), half),
            pltpu.VMEM((INNER, rows), half),
            pltpu.VMEM((WIDE, *block), f32),
            pltpu.VMEM((BLOCKS + 2, *block), f32),
            pltpu.VMEM((BLOCKS + 2, *block), f32),
            pltpu.VMEM((BLOCKS, *block), f32),
            pltpu.VMEM((BLOCKS, *block), f32),
            pltpu.VMEM((BLOCKS, *block), f32),
            pltpu.VMEM((HEADS, rows, rows), f32),
            pltpu.VMEM((HEADS, rows, rows), half),
            pltpu.VMEM((LANES, rows), f32),
            pltpu.VMEM((KERNEL - 1, *block), f32),
            pltpu.VMEM((16, LANES), f32),
        ]
        + scatter_scratch(grid, cuts),
        compiler_params=pltpu.CompilerParams(
            collective_id=0, has_side_effects=True, vmem_limit_bytes=60 * 1024 * 1024
        ),
    )(params, tokens, cotangent, seq_ids[None, :])


def adamw(weight, first, second, grad, step_count):
    steps_done = step_count[0].astype(jnp.float32)
    first_new = BETA_ONE * first + (1.0 - BETA_ONE) * grad
    second_new = BETA_TWO * second + (1.0 - BETA_TWO) * grad * grad
    first_hat = first_new / (1.0 - jnp.power(BETA_ONE, steps_done))
    second_hat = second_new / (1.0 - jnp.power(BETA_TWO, steps_done))
    weight_new = weight - LEARN_RATE * (
        first_hat / (jnp.sqrt(second_hat) + ADAM_EPS) + WEIGHT_DECAY * weight
    )
    return (weight_new, first_new, second_new)


def per_device(tokens, cotangent, seq_ids, params, first_moment, second_moment, step_count):
    width = params.shape[0]
    result, grad_input, most, last = run_block(
        tokens,
        cotangent,
        seq_ids,
        params.reshape(width // LANES, LANES),
        lax.axis_size("shard"),
        lax.axis_size("dp"),
    )
    owned = (most + last.astype(jnp.float32)).reshape(width)
    new_weight, new_first, new_second = adamw(
        params, first_moment, second_moment, owned, step_count
    )
    return (result, grad_input, owned, new_weight, new_first, new_second)


def solution(mesh):
    return jax.shard_map(
        per_device,
        mesh=mesh,
        in_specs=(
            P(("dp", "shard"), None),
            P(("dp", "shard"), None),
            P(("dp", "shard")),
            P(("dp", "shard")),
            P(("dp", "shard")),
            P(("dp", "shard")),
            P(),
        ),
        out_specs=(
            P(("dp", "shard"), None),
            P(("dp", "shard"), None),
            P(("dp", "shard")),
            P(("dp", "shard")),
            P(("dp", "shard")),
            P(("dp", "shard")),
        ),
        check_vma=False,
    )
```

```python
import functools

import jax
import jax.numpy as jnp
from jax import lax
from jax.experimental import pallas as pl
from jax.experimental.pallas import tpu as pltpu
from jax.sharding import PartitionSpec as P

D = 768
HEADS = 24
HEAD_DIM = 64
STATE = 128
KERNEL = 4
INNER = 1536
CHANNELS = 1792
LANES = 128
CUTS = 4
LAG = 3
AHEAD = 8
MESH = pl.DeviceIdType.MESH
PACKED = D + D * (INNER + CHANNELS) + D * HEADS + (KERNEL + 1) * CHANNELS + 3 * HEADS + INNER + INNER * D


EPS = 1e-05
BETA_ONE = 0.9
BETA_TWO = 0.999
ADAM_EPS = 1e-08
LEARN_RATE = 0.01
WEIGHT_DECAY = 0.1


def matmul(left, right):
    return jnp.dot(left, right, preferred_element_type=jnp.float32)


def over_rows(left, right):
    return lax.dot_general(
        left, right, (((0,), (0,)), ((), ())), preferred_element_type=jnp.float32
    )


def against(left, right):
    return lax.dot_general(
        left, right, (((1,), (1,)), ((), ())), preferred_element_type=jnp.float32
    )


ROWS_GAIN = D // LANES
ROWS_MAIN = D * (INNER + CHANNELS) // LANES
START_SMALL = ROWS_GAIN + ROWS_MAIN
START_OUT = (PACKED - INNER * D) // LANES
SHIFT = (PACKED - INNER * D) % LANES
ROWS_OUT = INNER * D // LANES
ROWS_SMALL = START_OUT + 1 - START_SMALL
WIDE = (INNER + CHANNELS) // LANES
THIN = D // LANES


def flip(place, number, size):
    if size & (size - 1):
        return lax.rem(place + number, size)
    bit = 1
    while bit <= number:
        if number & bit:
            place = place + bit - 2 * bit * lax.rem(lax.div(place, bit), 2)
        bit = 2 * bit
    return place


def unflip(place, number, size):
    return lax.rem(place + size - number, size) if size & (size - 1) else flip(place, number, size)


def slice_grid(group_count, wide_count):
    wide = group_count // 2
    tall = wide if wide_count % wide == 0 else 1
    return wide_count // tall, tall, wide


def slice_cuts(rows):
    step = -(-rows // (CUTS * 16)) * 16
    return [(start, min(step, rows - start)) for start in range(0, rows, step)]


class Neighbours:
    def __init__(self, grid):
        deep, tall, wide = self.grid = grid
        dp, shard = lax.axis_index("dp"), lax.axis_index("shard")
        z, y = lax.div(dp, tall), lax.rem(dp, tall)
        x, c = lax.div(shard, 2), lax.rem(shard, 2)
        self.z, self.y, self.x, self.c = z, y, x, c
        self.xs = [lax.rem(x + j, wide) for j in range(1, wide)]
        self.ys = [lax.rem(y + j, tall) for j in range(1, tall)]
        self.to_x = [self.place(z, y, p, c) for p in self.xs]
        self.to_y = [self.place(z, p, x, c) for p in self.ys]
        self.out_z = [None] + [self.place(unflip(z, i, deep), y, x, c) for i in range(1, deep)]
        self.partner = self.place(z, y, x, 1 - c)

    def place(self, z, y, x, c):
        return (z * self.grid[1] + y, x * 2 + c)

    def meet(self):
        everyone = [self.partner] + self.to_x + self.to_y + self.out_z[1:]
        barrier = pltpu.get_barrier_semaphore()
        for peer in everyone:
            pl.semaphore_signal(barrier, inc=1, device_id=peer, device_id_type=MESH)
        pl.semaphore_wait(barrier, len(everyone))


def scatter_part(near, cuts, pack_plane, data, out, last, send_sem, recv_sem, refs):
    deep, tall, wide = near.grid
    z, y, x, c = near.z, near.y, near.x, near.c
    sent = []

    def push(item, number, src, dst, peer):
        copy = pltpu.make_async_remote_copy(
            src_ref=src,
            dst_ref=dst,
            send_sem=send_sem.at[item, number],
            recv_sem=recv_sem.at[item, number],
            device_id=peer,
            device_id_type=MESH,
        )
        copy.start()
        sent.append(copy)
        return copy

    def total(parts):
        value = parts[0].astype(jnp.float32)
        for part in parts[1:]:
            value = value + part.astype(jnp.float32)
        return value

    first_x, first_y, first_z = 1, wide, wide + tall - 1
    order = [(i, k) for i in list(range(deep - 1, 0, -1)) + [0] for k in range(len(cuts))]
    held = {}
    for item, key in enumerate(order):
        held[key] = refs[item * 6 : item * 6 + 1] + refs[item * 6 : item * 6 + 6]
    flights = {}

    def stage_zero(item):
        i, k = order[item]
        start, size = cuts[k]
        if k == 0:
            pack_plane(unflip(z, i, deep))
        src = data.at[unflip(z, i, deep), :, :, 1 - c, start : start + size]
        flights[item] = [push(item, 0, src, held[i, k][0], near.partner)]

    def stage_one(item):
        i, k = order[item]
        start, size = cuts[k]
        got, acc, got_one = held[i, k][:3]
        plane = unflip(z, i, deep)
        for copy in flights[item]:
            copy.wait_recv()

        def add(step, carry):
            yi, xi = lax.div(step, wide), lax.rem(step, wide)
            mine = data[plane, yi, xi, c, start : start + size, :]
            acc[yi, xi] = total([mine, got[yi, xi]]).astype(jnp.bfloat16)
            return carry

        lax.fori_loop(0, tall * wide, add, 0)
        if k % 2 == 0:
            flights[item] = [
                push(item, first_x + j, acc.at[:, p], got_one.at[j], near.to_x[j])
                for j, p in enumerate(near.xs)
            ]
        else:
            flights[item] = [
                push(item, first_y + j, acc.at[p], got_one.at[j], near.to_y[j])
                for j, p in enumerate(near.ys)
            ]

    def stage_two(item):
        i, k = order[item]
        acc, got_one, acc_two, got_two = held[i, k][1:5]
        for copy in flights[item]:
            copy.wait_recv()

        def add(other, carry):
            mine = acc[other, x] if k % 2 == 0 else acc[y, other]
            parts = [mine] + [got_one[j, other] for j in range(got_one.shape[0])]
            acc_two[other] = total(parts).astype(jnp.bfloat16)
            return carry

        lax.fori_loop(0, tall if k % 2 == 0 else wide, add, 0)
        if k % 2 == 0:
            flights[item] = [
                push(item, first_y + j, acc_two.at[p], got_two.at[j], near.to_y[j])
                for j, p in enumerate(near.ys)
            ]
        else:
            flights[item] = [
                push(item, first_x + j, acc_two.at[p], got_two.at[j], near.to_x[j])
                for j, p in enumerate(near.xs)
            ]

    across = {}

    def stage_three(item):
        i, k = order[item]
        start, size = cuts[k]
        acc_two, got_two, acc_three, got_z = held[i, k][3:]
        for copy in flights[item]:
            copy.wait_recv()
        mine = y if k % 2 == 0 else x
        parts = [acc_two[mine]] + [got_two[j] for j in range(got_two.shape[0])]
        if i:
            acc_three[...] = total(parts).astype(jnp.bfloat16)
            across[i, k] = push(item, first_z, acc_three, got_z, near.out_z[i])
        else:
            value = total(parts)
            if deep == 1:
                last[start : start + size, :] = jnp.zeros((size, LANES), jnp.bfloat16)
            for j in range(1, deep):
                across[j, k].wait_recv()
                if j < deep - 1:
                    value = value + held[j, k][6][...].astype(jnp.float32)
                else:
                    last[start : start + size, :] = held[j, k][6][...]
            out[start : start + size, :] = value

    in_waves((stage_zero, stage_one, stage_two, stage_three), len(order), (0, 2, 6, 10))
    for copy in sent:
        copy.wait_send()


def in_waves(stages, count, lags):
    for wave in range(count + lags[-1]):
        for stage, lag in zip(stages, lags):
            if 0 <= wave - lag < count:
                stage(wave - lag)


def scatter_scratch(grid, cuts):
    deep, tall, wide = grid
    scratch = []
    for _ in range(deep):
        for k, (start, size) in enumerate(cuts):
            lead, other = (wide, tall) if k % 2 == 0 else (tall, wide)
            for shape in (
                (tall, wide),
                (lead - 1, other),
                (other,),
                (other - 1,),
                (),
                (),
            ):
                scratch.append(pltpu.VMEM((*shape, size, LANES), jnp.bfloat16))
    return scratch


def gather_part(near, cuts, params, w_main, w_out, small, gain, own, out, flat, send_sem, recv_sem):
    deep, tall, wide = near.grid
    z, y, x, c = near.z, near.y, near.x, near.c
    sent = []
    size_own = own.shape[0]
    size_plane = tall * wide * 2 * size_own
    own[...] = params[...].astype(jnp.bfloat16)

    def push(item, number, src, dst, peers):
        started = []
        for j, peer in enumerate(peers):
            copy = pltpu.make_async_remote_copy(
                src_ref=src,
                dst_ref=dst,
                send_sem=send_sem.at[item, number + j],
                recv_sem=recv_sem.at[item, number + j],
                device_id=peer,
                device_id_type=MESH,
            )
            copy.start()
            started.append(copy)
        sent.extend(started)
        return started

    first_x, first_y, first_z = 1, wide, wide + tall - 1
    order = [(i, k) for i in range(deep) for k in range(len(cuts))]
    flights = {}

    def start_z(item):
        i, k = order[item]
        if i:
            rows = pl.ds(*cuts[k])
            flights[item] = push(item, first_z, own.at[rows], out.at[z, y, x, c, rows], [near.out_z[i]])

    def next_z(wave):
        if wave + AHEAD < len(order):
            start_z(wave + AHEAD)

    def stage_one(item):
        i, k = order[item]
        rows = pl.ds(*cuts[k])
        for copy in flights.get(item, []):
            copy.wait_recv()
        block = out.at[flip(z, i, deep), y, x, c, rows]
        source = block if i else own.at[rows]
        if k % 2 == 0:
            flights[item] = push(item, first_y, source, block, near.to_y)
        else:
            flights[item] = push(item, first_x, source, block, near.to_x)
        if item == 0:
            out[z, y, x, c] = own[...]

    def stage_two(item):
        i, k = order[item]
        rows = pl.ds(*cuts[k])
        for copy in flights[item]:
            copy.wait_recv()
        plane = flip(z, i, deep)
        if k % 2 == 0:
            line = out.at[plane, :, x, c, rows]
            flights[item] = push(item, first_x, line, line, near.to_x)
        else:
            line = out.at[plane, y, :, c, rows]
            flights[item] = push(item, first_y, line, line, near.to_y)

    def stage_three(item):
        i, k = order[item]
        for copy in flights[item]:
            copy.wait_recv()
        sheet = out.at[flip(z, i, deep), :, :, c, pl.ds(*cuts[k])]
        flights[item] = push(item, 0, sheet, sheet, [near.partner])

    def main_block(number, carry):
        for j in range(WIDE):
            piece = flat[pl.ds(ROWS_GAIN + number * (16 * WIDE) + j, 16, stride=WIDE), :]
            w_main[pl.ds(pl.multiple_of(number * 16, 16), 16), j * LANES : (j + 1) * LANES] = piece.astype(
                jnp.bfloat16
            )
        return carry

    early = lax.broadcasted_iota(jnp.int32, (16, LANES), 1) < LANES - SHIFT

    def out_block(number, carry):
        turned = [
            pltpu.roll(flat[pl.ds(START_OUT + number * (16 * THIN) + j, 16, stride=THIN), :], LANES - SHIFT, 1)
            for j in range(THIN + 1)
        ]
        for j in range(THIN):
            w_out[pl.ds(pl.multiple_of(number * 16, 16), 16), j * LANES : (j + 1) * LANES] = jnp.where(
                early, turned[j], turned[j + 1]
            ).astype(jnp.bfloat16)
        return carry

    kinds = (
        (main_block, ROWS_GAIN, 16 * WIDE, 16 * WIDE, D // 16),
        (out_block, START_OUT, 16 * THIN, 16 * THIN + 1, INNER // 16),
    )

    def unpack_plane(plane):
        low = plane * size_plane
        for body, base, step, reach, count in kinds:
            begin = jnp.clip(lax.div(low - base + step * (count + 1) - 1, step) - count, 0, count)
            end = jnp.clip(lax.div(low + size_plane - base - reach + step * (count + 1), step) - count, 0, count)
            lax.fori_loop(begin, jnp.maximum(begin, end), body, 0)

    def stage_four(item):
        i, k = order[item]
        start, size = cuts[k]
        for copy in flights[item]:
            copy.wait_recv()
        plane = flip(z, i, deep)

        def widen(step, carry):
            yi, rest = lax.div(step, wide * 2), lax.rem(step, wide * 2)
            xi, ci = lax.div(rest, 2), lax.rem(rest, 2)
            place = plane * size_plane + step * size_own + start
            if size_own % 8 == 0:
                place = pl.multiple_of(place, 8)
            flat[pl.ds(place, size), :] = out[plane, yi, xi, ci, start : start + size, :].astype(jnp.float32)
            return carry

        lax.fori_loop(0, tall * wide * 2, widen, 0)
        if k == len(cuts) - 1:
            unpack_plane(plane)

    for item in range(min(AHEAD, len(order))):
        start_z(item)
    in_waves(
        (next_z, stage_one, stage_two, stage_three, stage_four), len(order), (0, 0, LAG, 2 * LAG, 2 * LAG + 2)
    )
    for body, base, step, reach, count in kinds:
        for number in range(count):
            low = base + number * step
            if low // size_plane != (low + reach - 1) // size_plane:
                body(number, 0)
    gain[0:ROWS_GAIN, :] = flat[0:ROWS_GAIN, :]
    gain[ROWS_GAIN:, :] = jnp.zeros((8 - ROWS_GAIN, LANES), jnp.float32)
    small[...] = flat[START_SMALL : START_SMALL + small.shape[0], :]
    for copy in sent:
        copy.wait_send()


HIGHEST = lax.Precision.HIGHEST
BLOCKS = INNER // LANES
PER = LANES // HEAD_DIM


def exact(left, right):
    return jnp.dot(left, right, preferred_element_type=jnp.float32, precision=HIGHEST)


def row_sum(value):
    return jnp.sum(value, axis=1, keepdims=True)


def col_sum(value):
    return jnp.sum(value, axis=0, keepdims=True)


def mixer_part(
    tokens, cot, seq_row, gain, small, w_main, w_out, result, grad_input,
    normed, grad_proj, hidden, live, w_dt_wide, normed_t, hidden_t,
    proj, slope, active, scanned, gated, grad_hidden, factor, mixed, cols, lag_mask, turned, main, tail,
):
    rows = tokens.shape[0]
    half = jnp.bfloat16
    seq_wide = jnp.broadcast_to(seq_row[...], (rows, rows)).astype(jnp.float32)
    seq_col = seq_wide.T
    seq_t = jnp.broadcast_to(seq_col[:, 0:1], (rows, LANES))
    place_t = lax.broadcasted_iota(jnp.int32, (rows, LANES), 0)
    for lag in range(1, KERNEL):
        same_run = (pltpu.roll(seq_t, lag, 0) == seq_t) & (place_t >= lag)
        lag_mask[lag - 1] = same_run.astype(jnp.float32)
    first = lax.broadcasted_iota(jnp.int32, (rows, rows), 0)
    second = lax.broadcasted_iota(jnp.int32, (rows, rows), 1)
    lower = first >= second
    same = lower & (seq_col == seq_wide)
    lanes = lax.broadcasted_iota(jnp.int32, (rows, LANES), 1)
    lane = lax.broadcasted_iota(jnp.int32, (1, LANES), 1)
    at_conv = D * HEADS // LANES
    at_heads = at_conv + (KERNEL + 1) * CHANNELS // LANES
    head_row = small[at_heads : at_heads + 1, :]
    own_head = lane < HEADS
    dt_bias = jnp.where(own_head, head_row, 0.0)
    a_log = jnp.where(own_head, pltpu.roll(head_row, LANES - HEADS, 1), 0.0)

    def tap(number, block):
        place = at_conv + number * (CHANNELS // LANES) + block
        return small[place : place + 1, :]

    def gain_row(block):
        here = small[at_heads + block : at_heads + block + 2, :]
        moved = pltpu.roll(here, LANES - SHIFT, 1)
        return jnp.where(lane < LANES - SHIFT, moved[0:1], moved[1:2])

    def skip_row(block):
        first_lane = 2 * HEADS + PER * block
        sides = [head_row[:, first_lane + i : first_lane + i + 1] for i in range(PER)]
        return jnp.where(lane < HEAD_DIM, sides[0], sides[1])

    turn = 16 * HEADS // LANES
    spots = D // 16
    lane_wide = lax.broadcasted_iota(jnp.int32, (spots, LANES), 1)
    for number in range(16):
        place, off = number * HEADS // LANES, number * HEADS % LANES
        piece = pltpu.roll(small[pl.ds(place, spots, stride=turn), :], (LANES - off) % LANES, 1)
        if off + HEADS > LANES:
            after = pltpu.roll(small[pl.ds(place + 1, spots, stride=turn), :], LANES - off, 1)
            piece = jnp.where(lane_wide < LANES - off, piece, after)
        w_dt_wide[pl.ds(number, spots, stride=16), :] = jnp.where(lane_wide < HEADS, piece, 0.0)
    w_dt = w_dt_wide[...].astype(half)
    gain_in = jnp.concatenate([gain[j : j + 1, :] for j in range(ROWS_GAIN)], 1)
    x = tokens[...].astype(jnp.float32)
    scale_in = lax.rsqrt(row_sum(x * x) * (1.0 / D) + EPS)
    normed_full = x * scale_in * gain_in
    normed[...] = normed_full.astype(half)
    for j in range(D // LANES):
        spot = slice(j * LANES, (j + 1) * LANES)
        normed_t[spot, :] = normed_full[:, spot].T.astype(half)
    live[...] = jnp.where(seq_col[:, 0:1] >= 0, cot[...].astype(jnp.float32), 0.0).astype(half)

    def project(pair):
        both = matmul(normed[...], w_main[:, pair * 2 * LANES : (pair + 1) * 2 * LANES])
        proj[2 * pair] = both[:, :LANES]
        proj[2 * pair + 1] = both[:, LANES:]

    def back_out(pair):
        both = against(live[...], w_out[pair * 2 * LANES : (pair + 1) * 2 * LANES, :])
        grad_hidden[2 * pair] = both[:, :LANES]
        grad_hidden[2 * pair + 1] = both[:, LANES:]

    raw = matmul(normed[...], w_dt) + dt_bias
    steps = jnp.maximum(raw, 0.0) + jnp.log1p(jnp.exp(-jnp.abs(raw)))
    rate = -jnp.exp(a_log)
    logs = exact(lower.astype(jnp.float32), steps * rate)
    logs_t = logs.T
    steps_t = steps.T

    def convolve(block):
        inside = proj[BLOCKS + block]
        total = tap(KERNEL, block) + tap(KERNEL - 1, block) * inside
        for lag in range(1, KERNEL):
            total = total + tap(KERNEL - 1 - lag, block) * (pltpu.roll(inside, lag, 0) * lag_mask[lag - 1])
        gate = jax.nn.sigmoid(total)
        value = total * gate
        active[block] = value
        slope[block] = gate + value * (1.0 - gate)

    project(BLOCKS)
    convolve(BLOCKS)
    convolve(BLOCKS + 1)
    b_mat, c_mat = active[BLOCKS], active[BLOCKS + 1]
    scores = lax.dot_general(
        c_mat, b_mat, (((1,), (1,)), ((), ())), preferred_element_type=jnp.float32, precision=HIGHEST
    )
    squares = jnp.zeros((rows, LANES), jnp.float32)
    cross = jnp.zeros((rows, LANES), jnp.float32)
    for pair in range(BLOCKS // 2):
        project(BLOCKS // 2 + pair)
        project(pair)
        back_out(pair)
        for block in (2 * pair, 2 * pair + 1):
            convolve(block)
            value = active[block]
            parts = []
            for side in range(PER):
                head = PER * block + side
                gap = logs[:, head : head + 1] - logs_t[head : head + 1, :]
                fall = jnp.exp(jnp.where(same, gap, -1e30))
                factor[head] = fall
                mix = ((fall * scores) * steps_t[head : head + 1, :]).astype(half)
                mixed[head] = mix
                parts.append(mix)
            low = value.astype(half)
            zero = jnp.zeros_like(low)
            left = lanes < HEAD_DIM
            stacked = jnp.concatenate(
                [jnp.where(left, low, zero), jnp.where(left, zero, low)], 0
            )
            inside = matmul(jnp.concatenate(parts, 1), stacked)
            total = inside + skip_row(block) * value
            gate = proj[block]
            out = total * (gate * jax.nn.sigmoid(gate))
            scanned[block] = total
            gated[block] = out
            squares = squares + out * out
            cross = cross + out * (grad_hidden[block] * gain_row(block))
    scale = lax.rsqrt(row_sum(squares) * (1.0 / INNER) + EPS)
    pull = row_sum(cross) * (scale * scale * scale) * (1.0 / INNER)
    scale_w = jnp.broadcast_to(scale, (rows, LANES))
    pull_w = jnp.broadcast_to(pull, (rows, LANES))

    def unconvolve(block, grad_active):
        grad = grad_active * slope[block]
        inside = proj[BLOCKS + block]
        total = tap(KERNEL - 1, block) * grad

        def keep(number, row):
            place = START_SMALL + at_conv + number * (CHANNELS // LANES) + block
            main[place : place + 1, :] = row

        keep(KERNEL, col_sum(grad))
        keep(KERNEL - 1, col_sum(grad * inside))
        for lag in range(1, KERNEL):
            kept = grad * lag_mask[lag - 1]
            keep(KERNEL - 1 - lag, col_sum(kept * pltpu.roll(inside, lag, 0)))
            total = total + tap(KERNEL - 1 - lag, block) * pltpu.roll(kept, rows - lag, 0)
        grad_proj[:, INNER + block * LANES : INNER + (block + 1) * LANES] = total.astype(half)

    skip_grad = jnp.zeros((1, LANES), jnp.float32)
    grad_scores = jnp.zeros((rows, rows), jnp.float32)
    row_part = jnp.zeros((rows, LANES), jnp.float32)
    cols[...] = jnp.zeros((LANES, rows), jnp.float32)
    for block in range(BLOCKS):
        span = slice(block * LANES, (block + 1) * LANES)
        out, total, gate, value = gated[block], scanned[block], proj[block], active[block]
        down = grad_hidden[block]
        unit = out * scale_w
        row_gain = gain_row(block)
        hidden[:, span] = (unit * row_gain).astype(half)
        hidden_t[span, :] = (unit * row_gain).T.astype(half)
        turned[block + 1 : block + 2, :] = pltpu.roll(col_sum(down * unit), SHIFT, 1)
        grad_gated = (down * row_gain) * scale_w - out * pull_w
        sig = jax.nn.sigmoid(gate)
        silu = gate * sig
        grad_total = grad_gated * silu
        grad_proj[:, span] = (grad_gated * total * (sig + silu * (1.0 - sig))).astype(half)
        skip_sums = col_sum(grad_total * value)
        for side in range(PER):
            inside_side = (lane >= side * HEAD_DIM) & (lane < (side + 1) * HEAD_DIM)
            amount = row_sum(jnp.where(inside_side, skip_sums, 0.0))
            skip_grad = jnp.where(lane == 2 * HEADS + PER * block + side, amount, skip_grad)
        low = grad_total.astype(half)
        zero = jnp.zeros_like(low)
        left = lanes < HEAD_DIM
        values_low = value.astype(half)
        tops = jnp.concatenate([jnp.where(left, low, zero), jnp.where(left, zero, low)], 0)
        grad_mix = against(tops, values_low)
        for side in range(PER):
            head = PER * block + side
            through = grad_mix[side * rows : (side + 1) * rows] * factor[head]
            scored = through * scores
            step = steps_t[head : head + 1, :]
            cols[head : head + 1, :] = col_sum(scored)
            row_part = jnp.where(lanes == head, row_sum(scored * step), row_part)
            grad_scores = grad_scores + through * step
        both = over_rows(jnp.concatenate([mixed[PER * block], mixed[PER * block + 1]], 0), tops)
        unconvolve(block, both + skip_row(block) * grad_total)
    low_scores = grad_scores.astype(half)
    unconvolve(BLOCKS + 1, matmul(low_scores, b_mat.astype(half)))
    unconvolve(BLOCKS, over_rows(low_scores, c_mat.astype(half)))
    col_part = cols[...].T
    upper = (first <= second).astype(jnp.float32)
    grad_decay = exact(upper, row_part - col_part * steps)
    grad_steps = col_part + grad_decay * rate
    grad_raw = grad_steps * jax.nn.sigmoid(raw)
    bias_grad = jnp.where(own_head, col_sum(grad_raw), 0.0)
    log_grad = jnp.where(own_head, col_sum(grad_decay * steps) * rate, 0.0)
    turned[0:1, :] = bias_grad + pltpu.roll(log_grad, HEADS, 1) + skip_grad
    rims = turned[0 : BLOCKS + 1, :]
    at_rims = START_SMALL + at_heads
    lane_rims = lax.broadcasted_iota(jnp.int32, (BLOCKS, LANES), 1)
    main[at_rims : at_rims + BLOCKS, :] = jnp.where(lane_rims < SHIFT, rims[:BLOCKS], rims[1:])
    tail[7:8, :] = rims[BLOCKS:]
    grad_dt = jnp.where(own_head, grad_raw, 0.0).astype(half)
    w_dt_wide[...] = matmul(normed_t[...], grad_dt)
    lines = [jnp.zeros((spots, LANES), jnp.float32) for _ in range(turn)]
    for number in range(16):
        place, off = number * HEADS // LANES, number * HEADS % LANES
        piece = pltpu.roll(w_dt_wide[pl.ds(number, spots, stride=16), :], off, 1)
        lines[place] = jnp.where((lane_wide >= off) & (lane_wide < off + HEADS), piece, lines[place])
        if off + HEADS > LANES:
            lines[place + 1] = jnp.where(lane_wide < off + HEADS - LANES, piece, lines[place + 1])
    for number in range(turn):
        main[pl.ds(START_SMALL + number, spots, stride=turn), :] = lines[number]
    result[...] = (x + matmul(hidden[...], w_out[...])).astype(half)
    back = against(grad_proj[...], w_main[...]) + against(grad_dt, w_dt)
    gain_grad = col_sum(back * (x * scale_in))
    for j in range(ROWS_GAIN):
        main[j : j + 1, :] = gain_grad[:, j * LANES : (j + 1) * LANES]
    pulled = back * gain_in
    push = row_sum(pulled * x) * (scale_in * scale_in * scale_in) * (1.0 / D)
    grad_input[...] = live[...].astype(jnp.float32) + (pulled * scale_in - x * push)


def packer(near, size_own, normed_t, grad_proj, hidden_t, live, main, tail, flat, data):
    deep, tall, wide = near.grid
    size_plane = tall * wide * 2 * size_own
    mixed_owner = START_OUT // size_own

    def main_block(number, carry):
        left = normed_t[pl.ds(pl.multiple_of(number * LANES, LANES), LANES), :]
        for pair in range(WIDE // 2):
            both = matmul(left, grad_proj[:, pair * 2 * LANES : (pair + 1) * 2 * LANES])
            for side in range(2):
                place = ROWS_GAIN + number * (LANES * WIDE) + 2 * pair + side
                main[pl.ds(place, LANES, stride=WIDE), :] = both[:, side * LANES : (side + 1) * LANES]
        return carry

    def out_block(number, carry):
        left = hidden_t[pl.ds(pl.multiple_of(number * LANES, LANES), LANES), :]
        for pair in range(THIN // 2):
            both = matmul(left, live[:, pair * 2 * LANES : (pair + 1) * 2 * LANES])
            for side in range(2):
                place = 8 + number * (LANES * THIN) + 2 * pair + side
                tail[pl.ds(place, LANES, stride=THIN), :] = pltpu.roll(
                    both[:, side * LANES : (side + 1) * LANES], SHIFT, 1
                )
        return carry

    kinds = (
        (main_block, ROWS_GAIN, LANES * WIDE, LANES * WIDE, D // LANES),
        (out_block, START_OUT, LANES * THIN, LANES * THIN + 1, INNER // LANES),
    )

    def joined(rows):
        early = lax.broadcasted_iota(jnp.int32, (rows.shape[0] - 8, LANES), 1) < SHIFT
        return jnp.where(early, rows[7 : rows.shape[0] - 1], rows[8:])

    def cast(step, plane):
        yi, rest = lax.div(step, wide * 2), lax.rem(step, wide * 2)
        xi, ci = lax.div(rest, 2), lax.rem(rest, 2)
        owner = plane * (tall * wide * 2) + step
        base = owner * size_own
        if size_own % 8 == 0:
            base = pl.multiple_of(base, 8)

        @pl.when(owner < mixed_owner)
        def _():
            data[plane, yi, xi, ci] = flat[pl.ds(base, size_own), :].astype(jnp.bfloat16)

        @pl.when(owner > mixed_owner)
        def _():
            data[plane, yi, xi, ci] = joined(flat[pl.ds(base, size_own + 8), :]).astype(jnp.bfloat16)

        @pl.when(owner == mixed_owner)
        def _():
            first = mixed_owner * size_own
            under = START_OUT - first
            after = joined(flat[START_OUT : first + size_own + 8, :])
            both = jnp.concatenate([flat[first:START_OUT, :], after], 0) if under else after
            data[plane, yi, xi, ci] = both.astype(jnp.bfloat16)

        return plane

    def pack_plane(plane):
        low = plane * size_plane
        for body, base, step, reach, count in kinds:
            begin = jnp.clip(lax.div(low - base - reach + step * (count + 1), step) - count, 0, count)
            end = jnp.clip(lax.div(low + size_plane - base + step * (count + 1) - 1, step) - count, 0, count)
            lax.fori_loop(begin, jnp.maximum(begin, end), body, 0)
        lax.fori_loop(0, tall * wide * 2, cast, plane)

    return pack_plane


def whole_kernel(
    grid, cuts, params_far, tokens_far, cot_far, seq_row, result, grad_input, most, last,
    params, tokens, cot, near_sem, w_main, w_out, small, gain, own, data, flat, gather_send, gather_recv, scatter_send, scatter_recv,
    normed, grad_proj, hidden, live, w_dt_wide, normed_t, hidden_t,
    proj, slope, active, scanned, gated, grad_hidden, factor, mixed, cols, lag_mask, turned, *refs,
):
    near = Neighbours(grid)
    fetches = [
        pltpu.make_async_copy(far, here, near_sem.at[number])
        for number, (far, here) in enumerate(((params_far, params), (tokens_far, tokens), (cot_far, cot)))
    ]
    for fetch in fetches:
        fetch.start()
    near.meet()
    fetches[0].wait()
    gather_part(near, cuts, params, w_main, w_out, small, gain, own, data, flat, gather_send, gather_recv)
    main = flat.at[0:START_OUT]
    tail = flat.at[START_OUT : flat.shape[0]]
    for fetch in fetches[1:]:
        fetch.wait()
    mixer_part(
        tokens, cot, seq_row, gain, small, w_main, w_out, result, grad_input,
        normed, grad_proj, hidden, live, w_dt_wide, normed_t, hidden_t,
        proj, slope, active, scanned, gated, grad_hidden, factor, mixed, cols, lag_mask, turned, main, tail,
    )
    rest = flat.shape[0] - START_OUT - 8 - ROWS_OUT
    flat[START_OUT + 8 + ROWS_OUT :, :] = jnp.zeros((rest, LANES), jnp.float32)
    pack_plane = packer(near, own.shape[0], normed_t, grad_proj, hidden_t, live, main, tail, flat, data)
    scatter_part(near, cuts, pack_plane, data, most, last, scatter_send, scatter_recv, refs)


def run_block(tokens, cotangent, seq_ids, params, group_count, wide_count):
    rows, own_rows = tokens.shape[0], params.shape[0]
    deep, tall, wide = grid = slice_grid(group_count, wide_count)
    cuts = slice_cuts(own_rows)
    f32, half = jnp.float32, jnp.bfloat16
    vmem = pl.BlockSpec(memory_space=pltpu.VMEM)
    shape = jax.ShapeDtypeStruct
    block = (rows, LANES)
    flat_rows = wide_count * group_count * own_rows
    sems = pltpu.SemaphoreType.DMA((deep * len(cuts), wide + tall))
    return pl.pallas_call(
        functools.partial(whole_kernel, grid, cuts),
        out_shape=(
            shape((rows, D), half),
            shape((rows, D), f32),
            shape((own_rows, LANES), f32),
            shape((own_rows, LANES), half),
        ),
        in_specs=[pl.BlockSpec(memory_space=pl.ANY)] * 3 + [vmem],
        out_specs=(vmem,) * 4,
        scratch_shapes=[
            pltpu.VMEM((own_rows, LANES), f32),
            pltpu.VMEM((rows, D), half),
            pltpu.VMEM((rows, D), half),
            pltpu.SemaphoreType.DMA((3,)),
            pltpu.VMEM((D, INNER + CHANNELS), half),
            pltpu.VMEM((INNER, D), half),
            pltpu.VMEM((-(-ROWS_SMALL // 8) * 8, LANES), f32),
            pltpu.VMEM((8, LANES), f32),
            pltpu.VMEM((own_rows, LANES), half),
            pltpu.VMEM((deep, tall, wide, 2, own_rows, LANES), half),
            pltpu.VMEM((flat_rows + 16, LANES), f32),
            sems,
            sems,
            sems,
            sems,
            pltpu.VMEM((rows, D), half),
            pltpu.VMEM((rows, INNER + CHANNELS), half),
            pltpu.VMEM((rows, INNER), half),
            pltpu.VMEM((rows, D), half),
            pltpu.VMEM((D, LANES), f32),
            pltpu.VMEM((D, rows), half),
            pltpu.VMEM((INNER, rows), half),
            pltpu.VMEM((WIDE, *block), f32),
            pltpu.VMEM((BLOCKS + 2, *block), f32),
            pltpu.VMEM((BLOCKS + 2, *block), f32),
            pltpu.VMEM((BLOCKS, *block), f32),
            pltpu.VMEM((BLOCKS, *block), f32),
            pltpu.VMEM((BLOCKS, *block), f32),
            pltpu.VMEM((HEADS, rows, rows), f32),
            pltpu.VMEM((HEADS, rows, rows), half),
            pltpu.VMEM((LANES, rows), f32),
            pltpu.VMEM((KERNEL - 1, *block), f32),
            pltpu.VMEM((16, LANES), f32),
        ]
        + scatter_scratch(grid, cuts),
        compiler_params=pltpu.CompilerParams(
            collective_id=0, has_side_effects=True, vmem_limit_bytes=60 * 1024 * 1024
        ),
    )(params, tokens, cotangent, seq_ids[None, :])


def adamw(weight, first, second, grad, step_count):
    steps_done = step_count[0].astype(jnp.float32)
    first_new = BETA_ONE * first + (1.0 - BETA_ONE) * grad
    second_new = BETA_TWO * second + (1.0 - BETA_TWO) * grad * grad
    first_hat = first_new / (1.0 - jnp.power(BETA_ONE, steps_done))
    second_hat = second_new / (1.0 - jnp.power(BETA_TWO, steps_done))
    weight_new = weight - LEARN_RATE * (
        first_hat / (jnp.sqrt(second_hat) + ADAM_EPS) + WEIGHT_DECAY * weight
    )
    return (weight_new, first_new, second_new)


def per_device(tokens, cotangent, seq_ids, params, first_moment, second_moment, step_count):
    width = params.shape[0]
    result, grad_input, most, last = run_block(
        tokens,
        cotangent,
        seq_ids,
        params.reshape(width // LANES, LANES),
        lax.axis_size("shard"),
        lax.axis_size("dp"),
    )
    owned = (most + last.astype(jnp.float32)).reshape(width)
    new_weight, new_first, new_second = adamw(
        params, first_moment, second_moment, owned, step_count
    )
    return (result, grad_input, owned, new_weight, new_first, new_second)


def solution(mesh):
    return jax.shard_map(
        per_device,
        mesh=mesh,
        in_specs=(
            P(("dp", "shard"), None),
            P(("dp", "shard"), None),
            P(("dp", "shard")),
            P(("dp", "shard")),
            P(("dp", "shard")),
            P(("dp", "shard")),
            P(),
        ),
        out_specs=(
            P(("dp", "shard"), None),
            P(("dp", "shard"), None),
            P(("dp", "shard")),
            P(("dp", "shard")),
            P(("dp", "shard")),
            P(("dp", "shard")),
        ),
        check_vma=False,
    )
```

```python
import functools

import jax
import jax.numpy as jnp
from jax import lax
from jax.experimental import pallas as pl
from jax.experimental.pallas import tpu as pltpu
from jax.sharding import PartitionSpec as P

D = 768
HEADS = 24
HEAD_DIM = 64
STATE = 128
KERNEL = 4
INNER = 1536
CHANNELS = 1792
LANES = 128
CUTS = 4
LAG = 3
AHEAD = 8
MESH = pl.DeviceIdType.MESH
PACKED = D + D * (INNER + CHANNELS) + D * HEADS + (KERNEL + 1) * CHANNELS + 3 * HEADS + INNER + INNER * D


EPS = 1e-05
BETA_ONE = 0.9
BETA_TWO = 0.999
ADAM_EPS = 1e-08
LEARN_RATE = 0.01
WEIGHT_DECAY = 0.1


def matmul(left, right):
    return jnp.dot(left, right, preferred_element_type=jnp.float32)


def over_rows(left, right):
    return lax.dot_general(
        left, right, (((0,), (0,)), ((), ())), preferred_element_type=jnp.float32
    )


def against(left, right):
    return lax.dot_general(
        left, right, (((1,), (1,)), ((), ())), preferred_element_type=jnp.float32
    )


ROWS_GAIN = D // LANES
ROWS_MAIN = D * (INNER + CHANNELS) // LANES
START_SMALL = ROWS_GAIN + ROWS_MAIN
START_OUT = (PACKED - INNER * D) // LANES
SHIFT = (PACKED - INNER * D) % LANES
ROWS_OUT = INNER * D // LANES
ROWS_SMALL = START_OUT + 1 - START_SMALL
WIDE = (INNER + CHANNELS) // LANES
THIN = D // LANES


def flip(place, number, size):
    if size & (size - 1):
        return lax.rem(place + number, size)
    bit = 1
    while bit <= number:
        if number & bit:
            place = place + bit - 2 * bit * lax.rem(lax.div(place, bit), 2)
        bit = 2 * bit
    return place


def unflip(place, number, size):
    return lax.rem(place + size - number, size) if size & (size - 1) else flip(place, number, size)


def slice_grid(group_count, wide_count):
    wide = group_count // 2
    tall = wide if wide_count % wide == 0 else 1
    return wide_count // tall, tall, wide


def slice_cuts(rows):
    step = -(-rows // (CUTS * 16)) * 16
    return [(start, min(step, rows - start)) for start in range(0, rows, step)]


class Neighbours:
    def __init__(self, grid):
        deep, tall, wide = self.grid = grid
        dp, shard = lax.axis_index("dp"), lax.axis_index("shard")
        z, y = lax.div(dp, tall), lax.rem(dp, tall)
        x, c = lax.div(shard, 2), lax.rem(shard, 2)
        self.z, self.y, self.x, self.c = z, y, x, c
        self.xs = [lax.rem(x + j, wide) for j in range(1, wide)]
        self.ys = [lax.rem(y + j, tall) for j in range(1, tall)]
        self.to_x = [self.place(z, y, p, c) for p in self.xs]
        self.to_y = [self.place(z, p, x, c) for p in self.ys]
        self.out_z = [None] + [self.place(unflip(z, i, deep), y, x, c) for i in range(1, deep)]
        self.partner = self.place(z, y, x, 1 - c)

    def place(self, z, y, x, c):
        return (z * self.grid[1] + y, x * 2 + c)

    def meet(self):
        everyone = [self.partner] + self.to_x + self.to_y + self.out_z[1:]
        barrier = pltpu.get_barrier_semaphore()
        for peer in everyone:
            pl.semaphore_signal(barrier, inc=1, device_id=peer, device_id_type=MESH)
        pl.semaphore_wait(barrier, len(everyone))


def scatter_part(near, cuts, pack_plane, data, out, last, send_sem, recv_sem, refs):
    deep, tall, wide = near.grid
    z, y, x, c = near.z, near.y, near.x, near.c
    sent = []

    def push(item, number, src, dst, peer):
        copy = pltpu.make_async_remote_copy(
            src_ref=src,
            dst_ref=dst,
            send_sem=send_sem.at[item, number],
            recv_sem=recv_sem.at[item, number],
            device_id=peer,
            device_id_type=MESH,
        )
        copy.start()
        sent.append(copy)
        return copy

    def total(parts):
        value = parts[0].astype(jnp.float32)
        for part in parts[1:]:
            value = value + part.astype(jnp.float32)
        return value

    first_x, first_y, first_z = 1, wide, wide + tall - 1
    order = [(i, k) for i in list(range(deep - 1, 0, -1)) + [0] for k in range(len(cuts))]
    held = {}
    for item, key in enumerate(order):
        held[key] = refs[item * 6 : item * 6 + 1] + refs[item * 6 : item * 6 + 6]
    flights = {}

    def stage_zero(item):
        i, k = order[item]
        start, size = cuts[k]
        if k == 0:
            pack_plane(unflip(z, i, deep))
        src = data.at[unflip(z, i, deep), :, :, 1 - c, start : start + size]
        flights[item] = [push(item, 0, src, held[i, k][0], near.partner)]

    def stage_one(item):
        i, k = order[item]
        start, size = cuts[k]
        got, acc, got_one = held[i, k][:3]
        plane = unflip(z, i, deep)
        for copy in flights[item]:
            copy.wait_recv()

        def add(step, carry):
            yi, xi = lax.div(step, wide), lax.rem(step, wide)
            mine = data[plane, yi, xi, c, start : start + size, :]
            acc[yi, xi] = total([mine, got[yi, xi]]).astype(jnp.bfloat16)
            return carry

        lax.fori_loop(0, tall * wide, add, 0)
        if k % 2 == 0:
            flights[item] = [
                push(item, first_x + j, acc.at[:, p], got_one.at[j], near.to_x[j])
                for j, p in enumerate(near.xs)
            ]
        else:
            flights[item] = [
                push(item, first_y + j, acc.at[p], got_one.at[j], near.to_y[j])
                for j, p in enumerate(near.ys)
            ]

    def stage_two(item):
        i, k = order[item]
        acc, got_one, acc_two, got_two = held[i, k][1:5]
        for copy in flights[item]:
            copy.wait_recv()

        def add(other, carry):
            mine = acc[other, x] if k % 2 == 0 else acc[y, other]
            parts = [mine] + [got_one[j, other] for j in range(got_one.shape[0])]
            acc_two[other] = total(parts).astype(jnp.bfloat16)
            return carry

        lax.fori_loop(0, tall if k % 2 == 0 else wide, add, 0)
        if k % 2 == 0:
            flights[item] = [
                push(item, first_y + j, acc_two.at[p], got_two.at[j], near.to_y[j])
                for j, p in enumerate(near.ys)
            ]
        else:
            flights[item] = [
                push(item, first_x + j, acc_two.at[p], got_two.at[j], near.to_x[j])
                for j, p in enumerate(near.xs)
            ]

    across = {}

    def stage_three(item):
        i, k = order[item]
        start, size = cuts[k]
        acc_two, got_two, acc_three, got_z = held[i, k][3:]
        for copy in flights[item]:
            copy.wait_recv()
        mine = y if k % 2 == 0 else x
        parts = [acc_two[mine]] + [got_two[j] for j in range(got_two.shape[0])]
        if i:
            acc_three[...] = total(parts).astype(jnp.bfloat16)
            across[i, k] = push(item, first_z, acc_three, got_z, near.out_z[i])
        else:
            value = total(parts)
            if deep == 1:
                last[start : start + size, :] = jnp.zeros((size, LANES), jnp.bfloat16)
            for j in range(1, deep):
                across[j, k].wait_recv()
                if j < deep - 1:
                    value = value + held[j, k][6][...].astype(jnp.float32)
                else:
                    last[start : start + size, :] = held[j, k][6][...]
            out[start : start + size, :] = value

    in_waves((stage_zero, stage_one, stage_two, stage_three), len(order), (0, 2, 6, 10))
    for copy in sent:
        copy.wait_send()


def in_waves(stages, count, lags):
    for wave in range(count + lags[-1]):
        for stage, lag in zip(stages, lags):
            if 0 <= wave - lag < count:
                stage(wave - lag)


def scatter_scratch(grid, cuts):
    deep, tall, wide = grid
    scratch = []
    for _ in range(deep):
        for k, (start, size) in enumerate(cuts):
            lead, other = (wide, tall) if k % 2 == 0 else (tall, wide)
            for shape in (
                (tall, wide),
                (lead - 1, other),
                (other,),
                (other - 1,),
                (),
                (),
            ):
                scratch.append(pltpu.VMEM((*shape, size, LANES), jnp.bfloat16))
    return scratch


def gather_part(near, cuts, params, w_main, w_out, small, gain, own, out, flat, send_sem, recv_sem):
    deep, tall, wide = near.grid
    z, y, x, c = near.z, near.y, near.x, near.c
    sent = []
    size_own = own.shape[0]
    size_plane = tall * wide * 2 * size_own
    own[...] = params[...].astype(jnp.bfloat16)

    def push(item, number, src, dst, peers):
        started = []
        for j, peer in enumerate(peers):
            copy = pltpu.make_async_remote_copy(
                src_ref=src,
                dst_ref=dst,
                send_sem=send_sem.at[item, number + j],
                recv_sem=recv_sem.at[item, number + j],
                device_id=peer,
                device_id_type=MESH,
            )
            copy.start()
            started.append(copy)
        sent.extend(started)
        return started

    first_x, first_y, first_z = 1, wide, wide + tall - 1
    order = [(i, k) for i in range(deep) for k in range(len(cuts))]
    flights = {}

    def start_z(item):
        i, k = order[item]
        if i:
            rows = pl.ds(*cuts[k])
            flights[item] = push(item, first_z, own.at[rows], out.at[z, y, x, c, rows], [near.out_z[i]])

    def next_z(wave):
        if wave + AHEAD < len(order):
            start_z(wave + AHEAD)

    def stage_one(item):
        i, k = order[item]
        rows = pl.ds(*cuts[k])
        for copy in flights.get(item, []):
            copy.wait_recv()
        block = out.at[flip(z, i, deep), y, x, c, rows]
        source = block if i else own.at[rows]
        if k % 2 == 0:
            flights[item] = push(item, first_y, source, block, near.to_y)
        else:
            flights[item] = push(item, first_x, source, block, near.to_x)
        if item == 0:
            out[z, y, x, c] = own[...]

    def stage_two(item):
        i, k = order[item]
        rows = pl.ds(*cuts[k])
        for copy in flights[item]:
            copy.wait_recv()
        plane = flip(z, i, deep)
        if k % 2 == 0:
            line = out.at[plane, :, x, c, rows]
            flights[item] = push(item, first_x, line, line, near.to_x)
        else:
            line = out.at[plane, y, :, c, rows]
            flights[item] = push(item, first_y, line, line, near.to_y)

    def stage_three(item):
        i, k = order[item]
        for copy in flights[item]:
            copy.wait_recv()
        sheet = out.at[flip(z, i, deep), :, :, c, pl.ds(*cuts[k])]
        flights[item] = push(item, 0, sheet, sheet, [near.partner])

    def main_block(number, carry):
        for j in range(WIDE):
            piece = flat[pl.ds(ROWS_GAIN + number * (TALL * WIDE) + j, TALL, stride=WIDE), :]
            w_main[pl.ds(pl.multiple_of(number * TALL, TALL), TALL), j * LANES : (j + 1) * LANES] = piece.astype(
                jnp.bfloat16
            )
        return carry

    early = lax.broadcasted_iota(jnp.int32, (TALL, LANES), 1) < LANES - SHIFT

    def out_block(number, carry):
        turned = [
            pltpu.roll(flat[pl.ds(START_OUT + number * (TALL * THIN) + j, TALL, stride=THIN), :], LANES - SHIFT, 1)
            for j in range(THIN + 1)
        ]
        for j in range(THIN):
            w_out[pl.ds(pl.multiple_of(number * TALL, TALL), TALL), j * LANES : (j + 1) * LANES] = jnp.where(
                early, turned[j], turned[j + 1]
            ).astype(jnp.bfloat16)
        return carry

    kinds = (
        (main_block, ROWS_GAIN, TALL * WIDE, TALL * WIDE, D // TALL),
        (out_block, START_OUT, TALL * THIN, TALL * THIN + 1, INNER // TALL),
    )

    def unpack_plane(plane):
        low = plane * size_plane
        for body, base, step, reach, count in kinds:
            begin = jnp.clip(lax.div(low - base + step * (count + 1) - 1, step) - count, 0, count)
            end = jnp.clip(lax.div(low + size_plane - base - reach + step * (count + 1), step) - count, 0, count)
            lax.fori_loop(begin, jnp.maximum(begin, end), body, 0)

    def stage_four(item):
        i, k = order[item]
        start, size = cuts[k]
        for copy in flights[item]:
            copy.wait_recv()
        plane = flip(z, i, deep)

        def widen(step, carry):
            yi, rest = lax.div(step, wide * 2), lax.rem(step, wide * 2)
            xi, ci = lax.div(rest, 2), lax.rem(rest, 2)
            place = plane * size_plane + step * size_own + start
            if size_own % 8 == 0:
                place = pl.multiple_of(place, 8)
            flat[pl.ds(place, size), :] = out[plane, yi, xi, ci, start : start + size, :].astype(jnp.float32)
            return carry

        lax.fori_loop(0, tall * wide * 2, widen, 0)
        if k == len(cuts) - 1:
            unpack_plane(plane)

    for item in range(min(AHEAD, len(order))):
        start_z(item)
    in_waves(
        (next_z, stage_one, stage_two, stage_three, stage_four), len(order), (0, 0, LAG, 2 * LAG, 2 * LAG + 2)
    )
    for body, base, step, reach, count in kinds:
        for number in range(count):
            low = base + number * step
            if low // size_plane != (low + reach - 1) // size_plane:
                body(number, 0)
    gain[0:ROWS_GAIN, :] = flat[0:ROWS_GAIN, :]
    gain[ROWS_GAIN:, :] = jnp.zeros((8 - ROWS_GAIN, LANES), jnp.float32)
    small[...] = flat[START_SMALL : START_SMALL + small.shape[0], :]
    for copy in sent:
        copy.wait_send()


HIGHEST = lax.Precision.HIGHEST
BLOCKS = INNER // LANES
PER = LANES // HEAD_DIM


def exact(left, right):
    return jnp.dot(left, right, preferred_element_type=jnp.float32, precision=HIGHEST)


def row_sum(value):
    return jnp.sum(value, axis=1, keepdims=True)


def col_sum(value):
    return jnp.sum(value, axis=0, keepdims=True)


def mixer_part(
    tokens, cot, seq_row, gain, small, w_main, w_out, result, grad_input,
    normed, grad_proj, hidden, live, w_dt_wide, normed_t, hidden_t,
    proj, slope, active, scanned, gated, grad_hidden, factor, mixed, cols, lag_mask, turned, main, tail,
):
    rows = tokens.shape[0]
    half = jnp.bfloat16
    seq_wide = jnp.broadcast_to(seq_row[...], (rows, rows)).astype(jnp.float32)
    seq_col = seq_wide.T
    seq_t = jnp.broadcast_to(seq_col[:, 0:1], (rows, LANES))
    place_t = lax.broadcasted_iota(jnp.int32, (rows, LANES), 0)
    for lag in range(1, KERNEL):
        same_run = (pltpu.roll(seq_t, lag, 0) == seq_t) & (place_t >= lag)
        lag_mask[lag - 1] = same_run.astype(jnp.float32)
    first = lax.broadcasted_iota(jnp.int32, (rows, rows), 0)
    second = lax.broadcasted_iota(jnp.int32, (rows, rows), 1)
    lower = first >= second
    same = lower & (seq_col == seq_wide)
    lanes = lax.broadcasted_iota(jnp.int32, (rows, LANES), 1)
    lane = lax.broadcasted_iota(jnp.int32, (1, LANES), 1)
    at_conv = D * HEADS // LANES
    at_heads = at_conv + (KERNEL + 1) * CHANNELS // LANES
    head_row = small[at_heads : at_heads + 1, :]
    own_head = lane < HEADS
    dt_bias = jnp.where(own_head, head_row, 0.0)
    a_log = jnp.where(own_head, pltpu.roll(head_row, LANES - HEADS, 1), 0.0)

    def tap(number, block):
        place = at_conv + number * (CHANNELS // LANES) + block
        return small[place : place + 1, :]

    def gain_row(block):
        here = small[at_heads + block : at_heads + block + 2, :]
        moved = pltpu.roll(here, LANES - SHIFT, 1)
        return jnp.where(lane < LANES - SHIFT, moved[0:1], moved[1:2])

    def skip_row(block):
        first_lane = 2 * HEADS + PER * block
        sides = [head_row[:, first_lane + i : first_lane + i + 1] for i in range(PER)]
        return jnp.where(lane < HEAD_DIM, sides[0], sides[1])

    turn = 16 * HEADS // LANES
    spots = D // 16
    lane_wide = lax.broadcasted_iota(jnp.int32, (spots, LANES), 1)
    for number in range(16):
        place, off = number * HEADS // LANES, number * HEADS % LANES
        piece = pltpu.roll(small[pl.ds(place, spots, stride=turn), :], (LANES - off) % LANES, 1)
        if off + HEADS > LANES:
            after = pltpu.roll(small[pl.ds(place + 1, spots, stride=turn), :], LANES - off, 1)
            piece = jnp.where(lane_wide < LANES - off, piece, after)
        w_dt_wide[pl.ds(number, spots, stride=16), :] = jnp.where(lane_wide < HEADS, piece, 0.0)
    w_dt = w_dt_wide[...].astype(half)
    gain_in = jnp.concatenate([gain[j : j + 1, :] for j in range(ROWS_GAIN)], 1)
    x = tokens[...].astype(jnp.float32)
    scale_in = lax.rsqrt(row_sum(x * x) * (1.0 / D) + EPS)
    normed_full = x * scale_in * gain_in
    normed[...] = normed_full.astype(half)
    for j in range(D // LANES):
        spot = slice(j * LANES, (j + 1) * LANES)
        normed_t[spot, :] = normed_full[:, spot].T.astype(half)
    live[...] = jnp.where(seq_col[:, 0:1] >= 0, cot[...].astype(jnp.float32), 0.0).astype(half)

    def project(pair):
        both = matmul(normed[...], w_main[:, pair * 2 * LANES : (pair + 1) * 2 * LANES])
        proj[2 * pair] = both[:, :LANES]
        proj[2 * pair + 1] = both[:, LANES:]

    def back_out(pair):
        both = against(live[...], w_out[pair * 2 * LANES : (pair + 1) * 2 * LANES, :])
        grad_hidden[2 * pair] = both[:, :LANES]
        grad_hidden[2 * pair + 1] = both[:, LANES:]

    raw = matmul(normed[...], w_dt) + dt_bias
    steps = jnp.maximum(raw, 0.0) + jnp.log1p(jnp.exp(-jnp.abs(raw)))
    rate = -jnp.exp(a_log)
    logs = exact(lower.astype(jnp.float32), steps * rate)
    logs_t = logs.T
    steps_t = steps.T

    def convolve(block):
        inside = proj[BLOCKS + block]
        total = tap(KERNEL, block) + tap(KERNEL - 1, block) * inside
        for lag in range(1, KERNEL):
            total = total + tap(KERNEL - 1 - lag, block) * (pltpu.roll(inside, lag, 0) * lag_mask[lag - 1])
        gate = jax.nn.sigmoid(total)
        value = total * gate
        active[block] = value
        slope[block] = gate + value * (1.0 - gate)

    project(BLOCKS)
    convolve(BLOCKS)
    convolve(BLOCKS + 1)
    b_mat, c_mat = active[BLOCKS], active[BLOCKS + 1]
    scores = lax.dot_general(
        c_mat, b_mat, (((1,), (1,)), ((), ())), preferred_element_type=jnp.float32, precision=HIGHEST
    )
    squares = jnp.zeros((rows, LANES), jnp.float32)
    cross = jnp.zeros((rows, LANES), jnp.float32)
    for pair in range(BLOCKS // 2):
        project(BLOCKS // 2 + pair)
        project(pair)
        back_out(pair)
        for block in (2 * pair, 2 * pair + 1):
            convolve(block)
            value = active[block]
            parts = []
            for side in range(PER):
                head = PER * block + side
                gap = logs[:, head : head + 1] - logs_t[head : head + 1, :]
                fall = jnp.exp(jnp.where(same, gap, -1e30))
                factor[head] = fall
                mix = ((fall * scores) * steps_t[head : head + 1, :]).astype(half)
                mixed[head] = mix
                parts.append(mix)
            low = value.astype(half)
            zero = jnp.zeros_like(low)
            left = lanes < HEAD_DIM
            stacked = jnp.concatenate(
                [jnp.where(left, low, zero), jnp.where(left, zero, low)], 0
            )
            inside = matmul(jnp.concatenate(parts, 1), stacked)
            total = inside + skip_row(block) * value
            gate = proj[block]
            out = total * (gate * jax.nn.sigmoid(gate))
            scanned[block] = total
            gated[block] = out
            squares = squares + out * out
            cross = cross + out * (grad_hidden[block] * gain_row(block))
    scale = lax.rsqrt(row_sum(squares) * (1.0 / INNER) + EPS)
    pull = row_sum(cross) * (scale * scale * scale) * (1.0 / INNER)
    scale_w = jnp.broadcast_to(scale, (rows, LANES))
    pull_w = jnp.broadcast_to(pull, (rows, LANES))

    def unconvolve(block, grad_active):
        grad = grad_active * slope[block]
        inside = proj[BLOCKS + block]
        total = tap(KERNEL - 1, block) * grad

        def keep(number, row):
            place = START_SMALL + at_conv + number * (CHANNELS // LANES) + block
            main[place : place + 1, :] = row

        keep(KERNEL, col_sum(grad))
        keep(KERNEL - 1, col_sum(grad * inside))
        for lag in range(1, KERNEL):
            kept = grad * lag_mask[lag - 1]
            keep(KERNEL - 1 - lag, col_sum(kept * pltpu.roll(inside, lag, 0)))
            total = total + tap(KERNEL - 1 - lag, block) * pltpu.roll(kept, rows - lag, 0)
        grad_proj[:, INNER + block * LANES : INNER + (block + 1) * LANES] = total.astype(half)

    skip_grad = jnp.zeros((1, LANES), jnp.float32)
    grad_scores = jnp.zeros((rows, rows), jnp.float32)
    row_part = jnp.zeros((rows, LANES), jnp.float32)
    cols[...] = jnp.zeros((LANES, rows), jnp.float32)
    for block in range(BLOCKS):
        span = slice(block * LANES, (block + 1) * LANES)
        out, total, gate, value = gated[block], scanned[block], proj[block], active[block]
        down = grad_hidden[block]
        unit = out * scale_w
        row_gain = gain_row(block)
        hidden[:, span] = (unit * row_gain).astype(half)
        hidden_t[span, :] = (unit * row_gain).T.astype(half)
        turned[block + 1 : block + 2, :] = pltpu.roll(col_sum(down * unit), SHIFT, 1)
        grad_gated = (down * row_gain) * scale_w - out * pull_w
        sig = jax.nn.sigmoid(gate)
        silu = gate * sig
        grad_total = grad_gated * silu
        grad_proj[:, span] = (grad_gated * total * (sig + silu * (1.0 - sig))).astype(half)
        skip_sums = col_sum(grad_total * value)
        for side in range(PER):
            inside_side = (lane >= side * HEAD_DIM) & (lane < (side + 1) * HEAD_DIM)
            amount = row_sum(jnp.where(inside_side, skip_sums, 0.0))
            skip_grad = jnp.where(lane == 2 * HEADS + PER * block + side, amount, skip_grad)
        low = grad_total.astype(half)
        zero = jnp.zeros_like(low)
        left = lanes < HEAD_DIM
        values_low = value.astype(half)
        tops = jnp.concatenate([jnp.where(left, low, zero), jnp.where(left, zero, low)], 0)
        grad_mix = against(tops, values_low)
        for side in range(PER):
            head = PER * block + side
            through = grad_mix[side * rows : (side + 1) * rows] * factor[head]
            scored = through * scores
            step = steps_t[head : head + 1, :]
            cols[head : head + 1, :] = col_sum(scored)
            row_part = jnp.where(lanes == head, row_sum(scored * step), row_part)
            grad_scores = grad_scores + through * step
        both = over_rows(jnp.concatenate([mixed[PER * block], mixed[PER * block + 1]], 0), tops)
        unconvolve(block, both + skip_row(block) * grad_total)
    low_scores = grad_scores.astype(half)
    unconvolve(BLOCKS + 1, matmul(low_scores, b_mat.astype(half)))
    unconvolve(BLOCKS, over_rows(low_scores, c_mat.astype(half)))
    col_part = cols[...].T
    upper = (first <= second).astype(jnp.float32)
    grad_decay = exact(upper, row_part - col_part * steps)
    grad_steps = col_part + grad_decay * rate
    grad_raw = grad_steps * jax.nn.sigmoid(raw)
    bias_grad = jnp.where(own_head, col_sum(grad_raw), 0.0)
    log_grad = jnp.where(own_head, col_sum(grad_decay * steps) * rate, 0.0)
    turned[0:1, :] = bias_grad + pltpu.roll(log_grad, HEADS, 1) + skip_grad
    rims = turned[0 : BLOCKS + 1, :]
    at_rims = START_SMALL + at_heads
    lane_rims = lax.broadcasted_iota(jnp.int32, (BLOCKS, LANES), 1)
    main[at_rims : at_rims + BLOCKS, :] = jnp.where(lane_rims < SHIFT, rims[:BLOCKS], rims[1:])
    tail[7:8, :] = rims[BLOCKS:]
    grad_dt = jnp.where(own_head, grad_raw, 0.0).astype(half)
    w_dt_wide[...] = matmul(normed_t[...], grad_dt)
    lines = [jnp.zeros((spots, LANES), jnp.float32) for _ in range(turn)]
    for number in range(16):
        place, off = number * HEADS // LANES, number * HEADS % LANES
        piece = pltpu.roll(w_dt_wide[pl.ds(number, spots, stride=16), :], off, 1)
        lines[place] = jnp.where((lane_wide >= off) & (lane_wide < off + HEADS), piece, lines[place])
        if off + HEADS > LANES:
            lines[place + 1] = jnp.where(lane_wide < off + HEADS - LANES, piece, lines[place + 1])
    for number in range(turn):
        main[pl.ds(START_SMALL + number, spots, stride=turn), :] = lines[number]
    result[...] = (x + matmul(hidden[...], w_out[...])).astype(half)
    back = against(grad_proj[...], w_main[...]) + against(grad_dt, w_dt)
    gain_grad = col_sum(back * (x * scale_in))
    for j in range(ROWS_GAIN):
        main[j : j + 1, :] = gain_grad[:, j * LANES : (j + 1) * LANES]
    pulled = back * gain_in
    push = row_sum(pulled * x) * (scale_in * scale_in * scale_in) * (1.0 / D)
    grad_input[...] = live[...].astype(jnp.float32) + (pulled * scale_in - x * push)


DEPTH = 256
TALL = 64


def packer(near, size_own, normed_t, grad_proj, hidden_t, live, main, tail, flat, data):
    deep, tall, wide = near.grid
    size_plane = tall * wide * 2 * size_own
    mixed_owner = START_OUT // size_own

    def main_block(number, carry):
        left = normed_t[pl.ds(pl.multiple_of(number * DEPTH, DEPTH), DEPTH), :]
        for pair in range(WIDE // 2):
            both = matmul(left, grad_proj[:, pair * 2 * LANES : (pair + 1) * 2 * LANES])
            for side in range(2):
                place = ROWS_GAIN + number * (DEPTH * WIDE) + 2 * pair + side
                main[pl.ds(place, DEPTH, stride=WIDE), :] = both[:, side * LANES : (side + 1) * LANES]
        return carry

    def out_block(number, carry):
        left = hidden_t[pl.ds(pl.multiple_of(number * DEPTH, DEPTH), DEPTH), :]
        for pair in range(THIN // 2):
            both = matmul(left, live[:, pair * 2 * LANES : (pair + 1) * 2 * LANES])
            for side in range(2):
                place = 8 + number * (DEPTH * THIN) + 2 * pair + side
                tail[pl.ds(place, DEPTH, stride=THIN), :] = pltpu.roll(
                    both[:, side * LANES : (side + 1) * LANES], SHIFT, 1
                )
        return carry

    kinds = (
        (main_block, ROWS_GAIN, DEPTH * WIDE, DEPTH * WIDE, D // DEPTH),
        (out_block, START_OUT, DEPTH * THIN, DEPTH * THIN + 1, INNER // DEPTH),
    )

    def joined(rows):
        early = lax.broadcasted_iota(jnp.int32, (rows.shape[0] - 8, LANES), 1) < SHIFT
        return jnp.where(early, rows[7 : rows.shape[0] - 1], rows[8:])

    def cast(step, plane):
        yi, rest = lax.div(step, wide * 2), lax.rem(step, wide * 2)
        xi, ci = lax.div(rest, 2), lax.rem(rest, 2)
        owner = plane * (tall * wide * 2) + step
        base = owner * size_own
        if size_own % 8 == 0:
            base = pl.multiple_of(base, 8)

        @pl.when(owner < mixed_owner)
        def _():
            data[plane, yi, xi, ci] = flat[pl.ds(base, size_own), :].astype(jnp.bfloat16)

        @pl.when(owner > mixed_owner)
        def _():
            data[plane, yi, xi, ci] = joined(flat[pl.ds(base, size_own + 8), :]).astype(jnp.bfloat16)

        @pl.when(owner == mixed_owner)
        def _():
            first = mixed_owner * size_own
            under = START_OUT - first
            after = joined(flat[START_OUT : first + size_own + 8, :])
            both = jnp.concatenate([flat[first:START_OUT, :], after], 0) if under else after
            data[plane, yi, xi, ci] = both.astype(jnp.bfloat16)

        return plane

    def pack_plane(plane):
        low = plane * size_plane
        for body, base, step, reach, count in kinds:
            begin = jnp.clip(lax.div(low - base - reach + step * (count + 1), step) - count, 0, count)
            end = jnp.clip(lax.div(low + size_plane - base + step * (count + 1) - 1, step) - count, 0, count)
            lax.fori_loop(begin, jnp.maximum(begin, end), body, 0)
        lax.fori_loop(0, tall * wide * 2, cast, plane)

    return pack_plane


def whole_kernel(
    grid, cuts, params_far, tokens_far, cot_far, seq_row, result, grad_input, most, last,
    params, tokens, cot, near_sem, w_main, w_out, small, gain, own, data, flat, gather_send, gather_recv, scatter_send, scatter_recv,
    normed, grad_proj, hidden, live, w_dt_wide, normed_t, hidden_t,
    proj, slope, active, scanned, gated, grad_hidden, factor, mixed, cols, lag_mask, turned, *refs,
):
    near = Neighbours(grid)
    fetches = [
        pltpu.make_async_copy(far, here, near_sem.at[number])
        for number, (far, here) in enumerate(((params_far, params), (tokens_far, tokens), (cot_far, cot)))
    ]
    for fetch in fetches:
        fetch.start()
    near.meet()
    fetches[0].wait()
    gather_part(near, cuts, params, w_main, w_out, small, gain, own, data, flat, gather_send, gather_recv)
    main = flat.at[0:START_OUT]
    tail = flat.at[START_OUT : flat.shape[0]]
    for fetch in fetches[1:]:
        fetch.wait()
    mixer_part(
        tokens, cot, seq_row, gain, small, w_main, w_out, result, grad_input,
        normed, grad_proj, hidden, live, w_dt_wide, normed_t, hidden_t,
        proj, slope, active, scanned, gated, grad_hidden, factor, mixed, cols, lag_mask, turned, main, tail,
    )
    rest = flat.shape[0] - START_OUT - 8 - ROWS_OUT
    flat[START_OUT + 8 + ROWS_OUT :, :] = jnp.zeros((rest, LANES), jnp.float32)
    pack_plane = packer(near, own.shape[0], normed_t, grad_proj, hidden_t, live, main, tail, flat, data)
    scatter_part(near, cuts, pack_plane, data, most, last, scatter_send, scatter_recv, refs)


def run_block(tokens, cotangent, seq_ids, params, group_count, wide_count):
    rows, own_rows = tokens.shape[0], params.shape[0]
    deep, tall, wide = grid = slice_grid(group_count, wide_count)
    cuts = slice_cuts(own_rows)
    f32, half = jnp.float32, jnp.bfloat16
    vmem = pl.BlockSpec(memory_space=pltpu.VMEM)
    shape = jax.ShapeDtypeStruct
    block = (rows, LANES)
    flat_rows = wide_count * group_count * own_rows
    sems = pltpu.SemaphoreType.DMA((deep * len(cuts), wide + tall))
    return pl.pallas_call(
        functools.partial(whole_kernel, grid, cuts),
        out_shape=(
            shape((rows, D), half),
            shape((rows, D), f32),
            shape((own_rows, LANES), f32),
            shape((own_rows, LANES), half),
        ),
        in_specs=[pl.BlockSpec(memory_space=pl.ANY)] * 3 + [vmem],
        out_specs=(vmem,) * 4,
        scratch_shapes=[
            pltpu.VMEM((own_rows, LANES), f32),
            pltpu.VMEM((rows, D), half),
            pltpu.VMEM((rows, D), half),
            pltpu.SemaphoreType.DMA((3,)),
            pltpu.VMEM((D, INNER + CHANNELS), half),
            pltpu.VMEM((INNER, D), half),
            pltpu.VMEM((-(-ROWS_SMALL // 8) * 8, LANES), f32),
            pltpu.VMEM((8, LANES), f32),
            pltpu.VMEM((own_rows, LANES), half),
            pltpu.VMEM((deep, tall, wide, 2, own_rows, LANES), half),
            pltpu.VMEM((flat_rows + 16, LANES), f32),
            sems,
            sems,
            sems,
            sems,
            pltpu.VMEM((rows, D), half),
            pltpu.VMEM((rows, INNER + CHANNELS), half),
            pltpu.VMEM((rows, INNER), half),
            pltpu.VMEM((rows, D), half),
            pltpu.VMEM((D, LANES), f32),
            pltpu.VMEM((D, rows), half),
            pltpu.VMEM((INNER, rows), half),
            pltpu.VMEM((WIDE, *block), f32),
            pltpu.VMEM((BLOCKS + 2, *block), f32),
            pltpu.VMEM((BLOCKS + 2, *block), f32),
            pltpu.VMEM((BLOCKS, *block), f32),
            pltpu.VMEM((BLOCKS, *block), f32),
            pltpu.VMEM((BLOCKS, *block), f32),
            pltpu.VMEM((HEADS, rows, rows), f32),
            pltpu.VMEM((HEADS, rows, rows), half),
            pltpu.VMEM((LANES, rows), f32),
            pltpu.VMEM((KERNEL - 1, *block), f32),
            pltpu.VMEM((16, LANES), f32),
        ]
        + scatter_scratch(grid, cuts),
        compiler_params=pltpu.CompilerParams(
            collective_id=0, has_side_effects=True, vmem_limit_bytes=60 * 1024 * 1024
        ),
    )(params, tokens, cotangent, seq_ids[None, :])


def adamw(weight, first, second, grad, step_count):
    steps_done = step_count[0].astype(jnp.float32)
    first_new = BETA_ONE * first + (1.0 - BETA_ONE) * grad
    second_new = BETA_TWO * second + (1.0 - BETA_TWO) * grad * grad
    first_hat = first_new / (1.0 - jnp.power(BETA_ONE, steps_done))
    second_hat = second_new / (1.0 - jnp.power(BETA_TWO, steps_done))
    weight_new = weight - LEARN_RATE * (
        first_hat / (jnp.sqrt(second_hat) + ADAM_EPS) + WEIGHT_DECAY * weight
    )
    return (weight_new, first_new, second_new)


def per_device(tokens, cotangent, seq_ids, params, first_moment, second_moment, step_count):
    width = params.shape[0]
    result, grad_input, most, last = run_block(
        tokens,
        cotangent,
        seq_ids,
        params.reshape(width // LANES, LANES),
        lax.axis_size("shard"),
        lax.axis_size("dp"),
    )
    owned = (most + last.astype(jnp.float32)).reshape(width)
    new_weight, new_first, new_second = adamw(
        params, first_moment, second_moment, owned, step_count
    )
    return (result, grad_input, owned, new_weight, new_first, new_second)


def solution(mesh):
    return jax.shard_map(
        per_device,
        mesh=mesh,
        in_specs=(
            P(("dp", "shard"), None),
            P(("dp", "shard"), None),
            P(("dp", "shard")),
            P(("dp", "shard")),
            P(("dp", "shard")),
            P(("dp", "shard")),
            P(),
        ),
        out_specs=(
            P(("dp", "shard"), None),
            P(("dp", "shard"), None),
            P(("dp", "shard")),
            P(("dp", "shard")),
            P(("dp", "shard")),
            P(("dp", "shard")),
        ),
        check_vma=False,
    )
```

```python
import functools

import jax
import jax.numpy as jnp
from jax import lax
from jax.experimental import pallas as pl
from jax.experimental.pallas import tpu as pltpu
from jax.sharding import PartitionSpec as P

D = 768
HEADS = 24
HEAD_DIM = 64
STATE = 128
KERNEL = 4
INNER = 1536
CHANNELS = 1792
LANES = 128
CUTS = 4
LAG = 3
AHEAD = 8
MESH = pl.DeviceIdType.MESH
PACKED = D + D * (INNER + CHANNELS) + D * HEADS + (KERNEL + 1) * CHANNELS + 3 * HEADS + INNER + INNER * D


EPS = 1e-05
BETA_ONE = 0.9
BETA_TWO = 0.999
ADAM_EPS = 1e-08
LEARN_RATE = 0.01
WEIGHT_DECAY = 0.1


def matmul(left, right):
    return jnp.dot(left, right, preferred_element_type=jnp.float32)


def over_rows(left, right):
    return lax.dot_general(
        left, right, (((0,), (0,)), ((), ())), preferred_element_type=jnp.float32
    )


def against(left, right):
    return lax.dot_general(
        left, right, (((1,), (1,)), ((), ())), preferred_element_type=jnp.float32
    )


ROWS_GAIN = D // LANES
ROWS_MAIN = D * (INNER + CHANNELS) // LANES
START_SMALL = ROWS_GAIN + ROWS_MAIN
START_OUT = (PACKED - INNER * D) // LANES
SHIFT = (PACKED - INNER * D) % LANES
ROWS_OUT = INNER * D // LANES
ROWS_SMALL = START_OUT + 1 - START_SMALL
WIDE = (INNER + CHANNELS) // LANES
THIN = D // LANES


def flip(place, number, size):
    if size & (size - 1):
        return lax.rem(place + number, size)
    bit = 1
    while bit <= number:
        if number & bit:
            place = place + bit - 2 * bit * lax.rem(lax.div(place, bit), 2)
        bit = 2 * bit
    return place


def unflip(place, number, size):
    return lax.rem(place + size - number, size) if size & (size - 1) else flip(place, number, size)


def slice_grid(group_count, wide_count):
    wide = group_count // 2
    tall = wide if wide_count % wide == 0 else 1
    return wide_count // tall, tall, wide


def slice_cuts(rows):
    step = -(-rows // (CUTS * 16)) * 16
    return [(start, min(step, rows - start)) for start in range(0, rows, step)]


class Neighbours:
    def __init__(self, grid):
        deep, tall, wide = self.grid = grid
        dp, shard = lax.axis_index("dp"), lax.axis_index("shard")
        z, y = lax.div(dp, tall), lax.rem(dp, tall)
        x, c = lax.div(shard, 2), lax.rem(shard, 2)
        self.z, self.y, self.x, self.c = z, y, x, c
        self.xs = [lax.rem(x + j, wide) for j in range(1, wide)]
        self.ys = [lax.rem(y + j, tall) for j in range(1, tall)]
        self.to_x = [self.place(z, y, p, c) for p in self.xs]
        self.to_y = [self.place(z, p, x, c) for p in self.ys]
        self.out_z = [None] + [self.place(unflip(z, i, deep), y, x, c) for i in range(1, deep)]
        self.partner = self.place(z, y, x, 1 - c)

    def place(self, z, y, x, c):
        return (z * self.grid[1] + y, x * 2 + c)

    def meet(self):
        everyone = [self.partner] + self.to_x + self.to_y + self.out_z[1:]
        barrier = pltpu.get_barrier_semaphore()
        for peer in everyone:
            pl.semaphore_signal(barrier, inc=1, device_id=peer, device_id_type=MESH)
        pl.semaphore_wait(barrier, len(everyone))


def scatter_part(near, cuts, pack_plane, data, out, last, send_sem, recv_sem, refs):
    deep, tall, wide = near.grid
    z, y, x, c = near.z, near.y, near.x, near.c
    sent = []

    def push(item, number, src, dst, peer):
        copy = pltpu.make_async_remote_copy(
            src_ref=src,
            dst_ref=dst,
            send_sem=send_sem.at[item, number],
            recv_sem=recv_sem.at[item, number],
            device_id=peer,
            device_id_type=MESH,
        )
        copy.start()
        sent.append(copy)
        return copy

    def total(parts):
        value = parts[0].astype(jnp.float32)
        for part in parts[1:]:
            value = value + part.astype(jnp.float32)
        return value

    first_x, first_y, first_z = 1, wide, wide + tall - 1
    order = [(i, k) for i in list(range(deep - 1, 0, -1)) + [0] for k in range(len(cuts))]
    held = {}
    for item, key in enumerate(order):
        held[key] = refs[item * 6 : item * 6 + 1] + refs[item * 6 : item * 6 + 6]
    flights = {}

    def stage_zero(item):
        i, k = order[item]
        start, size = cuts[k]
        if k == 0:
            pack_plane(unflip(z, i, deep))
        src = data.at[unflip(z, i, deep), :, :, 1 - c, start : start + size]
        flights[item] = [push(item, 0, src, held[i, k][0], near.partner)]

    def stage_one(item):
        i, k = order[item]
        start, size = cuts[k]
        got, acc, got_one = held[i, k][:3]
        plane = unflip(z, i, deep)
        for copy in flights[item]:
            copy.wait_recv()

        def add(step, carry):
            yi, xi = lax.div(step, wide), lax.rem(step, wide)
            mine = data[plane, yi, xi, c, start : start + size, :]
            acc[yi, xi] = total([mine, got[yi, xi]]).astype(jnp.bfloat16)
            return carry

        lax.fori_loop(0, tall * wide, add, 0)
        if k % 2 == 0:
            flights[item] = [
                push(item, first_x + j, acc.at[:, p], got_one.at[j], near.to_x[j])
                for j, p in enumerate(near.xs)
            ]
        else:
            flights[item] = [
                push(item, first_y + j, acc.at[p], got_one.at[j], near.to_y[j])
                for j, p in enumerate(near.ys)
            ]

    def stage_two(item):
        i, k = order[item]
        acc, got_one, acc_two, got_two = held[i, k][1:5]
        for copy in flights[item]:
            copy.wait_recv()

        def add(other, carry):
            mine = acc[other, x] if k % 2 == 0 else acc[y, other]
            parts = [mine] + [got_one[j, other] for j in range(got_one.shape[0])]
            acc_two[other] = total(parts).astype(jnp.bfloat16)
            return carry

        lax.fori_loop(0, tall if k % 2 == 0 else wide, add, 0)
        if k % 2 == 0:
            flights[item] = [
                push(item, first_y + j, acc_two.at[p], got_two.at[j], near.to_y[j])
                for j, p in enumerate(near.ys)
            ]
        else:
            flights[item] = [
                push(item, first_x + j, acc_two.at[p], got_two.at[j], near.to_x[j])
                for j, p in enumerate(near.xs)
            ]

    across = {}

    def stage_three(item):
        i, k = order[item]
        start, size = cuts[k]
        acc_two, got_two, acc_three, got_z = held[i, k][3:]
        for copy in flights[item]:
            copy.wait_recv()
        mine = y if k % 2 == 0 else x
        parts = [acc_two[mine]] + [got_two[j] for j in range(got_two.shape[0])]
        if i:
            acc_three[...] = total(parts).astype(jnp.bfloat16)
            across[i, k] = push(item, first_z, acc_three, got_z, near.out_z[i])
        else:
            value = total(parts)
            if deep == 1:
                last[start : start + size, :] = jnp.zeros((size, LANES), jnp.bfloat16)
            for j in range(1, deep):
                across[j, k].wait_recv()
                if j < deep - 1:
                    value = value + held[j, k][6][...].astype(jnp.float32)
                else:
                    last[start : start + size, :] = held[j, k][6][...]
            out[start : start + size, :] = value

    in_waves((stage_zero, stage_one, stage_two, stage_three), len(order), (0, 2, 6, 10))
    for copy in sent:
        copy.wait_send()


def in_waves(stages, count, lags):
    for wave in range(count + lags[-1]):
        for stage, lag in zip(stages, lags):
            if 0 <= wave - lag < count:
                stage(wave - lag)


def scatter_scratch(grid, cuts):
    deep, tall, wide = grid
    scratch = []
    for _ in range(deep):
        for k, (start, size) in enumerate(cuts):
            lead, other = (wide, tall) if k % 2 == 0 else (tall, wide)
            for shape in (
                (tall, wide),
                (lead - 1, other),
                (other,),
                (other - 1,),
                (),
                (),
            ):
                scratch.append(pltpu.VMEM((*shape, size, LANES), jnp.bfloat16))
    return scratch


def gather_part(near, cuts, params, w_main, w_out, small, gain, own, out, flat, send_sem, recv_sem):
    deep, tall, wide = near.grid
    z, y, x, c = near.z, near.y, near.x, near.c
    sent = []
    size_own = own.shape[0]
    size_plane = tall * wide * 2 * size_own
    own[...] = params[...].astype(jnp.bfloat16)

    def push(item, number, src, dst, peers):
        started = []
        for j, peer in enumerate(peers):
            copy = pltpu.make_async_remote_copy(
                src_ref=src,
                dst_ref=dst,
                send_sem=send_sem.at[item, number + j],
                recv_sem=recv_sem.at[item, number + j],
                device_id=peer,
                device_id_type=MESH,
            )
            copy.start()
            started.append(copy)
        sent.extend(started)
        return started

    first_x, first_y, first_z = 1, wide, wide + tall - 1
    order = [(i, k) for i in range(deep) for k in range(len(cuts))]
    flights = {}

    def start_z(item):
        i, k = order[item]
        if i:
            rows = pl.ds(*cuts[k])
            flights[item] = push(item, first_z, own.at[rows], out.at[z, y, x, c, rows], [near.out_z[i]])

    def next_z(wave):
        if wave + AHEAD < len(order):
            start_z(wave + AHEAD)

    def stage_one(item):
        i, k = order[item]
        rows = pl.ds(*cuts[k])
        for copy in flights.get(item, []):
            copy.wait_recv()
        block = out.at[flip(z, i, deep), y, x, c, rows]
        source = block if i else own.at[rows]
        if k % 2 == 0:
            flights[item] = push(item, first_y, source, block, near.to_y)
        else:
            flights[item] = push(item, first_x, source, block, near.to_x)
        if item == 0:
            out[z, y, x, c] = own[...]

    def stage_two(item):
        i, k = order[item]
        rows = pl.ds(*cuts[k])
        for copy in flights[item]:
            copy.wait_recv()
        plane = flip(z, i, deep)
        if k % 2 == 0:
            line = out.at[plane, :, x, c, rows]
            flights[item] = push(item, first_x, line, line, near.to_x)
        else:
            line = out.at[plane, y, :, c, rows]
            flights[item] = push(item, first_y, line, line, near.to_y)

    def stage_three(item):
        i, k = order[item]
        for copy in flights[item]:
            copy.wait_recv()
        sheet = out.at[flip(z, i, deep), :, :, c, pl.ds(*cuts[k])]
        flights[item] = push(item, 0, sheet, sheet, [near.partner])

    def main_block(number, carry):
        for j in range(WIDE):
            piece = flat[pl.ds(ROWS_GAIN + number * (TALL * WIDE) + j, TALL, stride=WIDE), :]
            w_main[pl.ds(pl.multiple_of(number * TALL, TALL), TALL), j * LANES : (j + 1) * LANES] = piece.astype(
                jnp.bfloat16
            )
        return carry

    early = lax.broadcasted_iota(jnp.int32, (TALL, LANES), 1) < LANES - SHIFT

    def out_block(number, carry):
        turned = [
            pltpu.roll(flat[pl.ds(START_OUT + number * (TALL * THIN) + j, TALL, stride=THIN), :], LANES - SHIFT, 1)
            for j in range(THIN + 1)
        ]
        for j in range(THIN):
            w_out[pl.ds(pl.multiple_of(number * TALL, TALL), TALL), j * LANES : (j + 1) * LANES] = jnp.where(
                early, turned[j], turned[j + 1]
            ).astype(jnp.bfloat16)
        return carry

    kinds = (
        (main_block, ROWS_GAIN, TALL * WIDE, TALL * WIDE, D // TALL),
        (out_block, START_OUT, TALL * THIN, TALL * THIN + 1, INNER // TALL),
    )

    def unpack_plane(plane):
        low = plane * size_plane
        for body, base, step, reach, count in kinds:
            begin = jnp.clip(lax.div(low - base + step * (count + 1) - 1, step) - count, 0, count)
            end = jnp.clip(lax.div(low + size_plane - base - reach + step * (count + 1), step) - count, 0, count)
            lax.fori_loop(begin, jnp.maximum(begin, end), body, 0)

    def stage_four(item):
        i, k = order[item]
        start, size = cuts[k]
        for copy in flights[item]:
            copy.wait_recv()
        plane = flip(z, i, deep)

        def widen(step, carry):
            yi, rest = lax.div(step, wide * 2), lax.rem(step, wide * 2)
            xi, ci = lax.div(rest, 2), lax.rem(rest, 2)
            place = plane * size_plane + step * size_own + start
            if size_own % 8 == 0:
                place = pl.multiple_of(place, 8)
            flat[pl.ds(place, size), :] = out[plane, yi, xi, ci, start : start + size, :].astype(jnp.float32)
            return carry

        lax.fori_loop(0, tall * wide * 2, widen, 0, unroll=2)
        if k == len(cuts) - 1:
            unpack_plane(plane)

    for item in range(min(AHEAD, len(order))):
        start_z(item)
    in_waves(
        (next_z, stage_one, stage_two, stage_three, stage_four), len(order), (0, 0, LAG, 2 * LAG, 2 * LAG + 2)
    )
    for body, base, step, reach, count in kinds:
        for number in range(count):
            low = base + number * step
            if low // size_plane != (low + reach - 1) // size_plane:
                body(number, 0)
    gain[0:ROWS_GAIN, :] = flat[0:ROWS_GAIN, :]
    gain[ROWS_GAIN:, :] = jnp.zeros((8 - ROWS_GAIN, LANES), jnp.float32)
    small[...] = flat[START_SMALL : START_SMALL + small.shape[0], :]
    for copy in sent:
        copy.wait_send()


HIGHEST = lax.Precision.HIGHEST
BLOCKS = INNER // LANES
PER = LANES // HEAD_DIM


def exact(left, right):
    return jnp.dot(left, right, preferred_element_type=jnp.float32, precision=HIGHEST)


def row_sum(value):
    return jnp.sum(value, axis=1, keepdims=True)


def col_sum(value):
    return jnp.sum(value, axis=0, keepdims=True)


def mixer_part(
    tokens, cot, seq_row, gain, small, w_main, w_out, result, grad_input,
    normed, grad_proj, hidden, live, w_dt_wide, normed_t, hidden_t,
    proj, slope, active, scanned, gated, grad_hidden, factor, mixed, cols, lag_mask, turned, main, tail,
):
    rows = tokens.shape[0]
    half = jnp.bfloat16
    seq_wide = jnp.broadcast_to(seq_row[...], (rows, rows)).astype(jnp.float32)
    seq_col = seq_wide.T
    seq_t = jnp.broadcast_to(seq_col[:, 0:1], (rows, LANES))
    place_t = lax.broadcasted_iota(jnp.int32, (rows, LANES), 0)
    for lag in range(1, KERNEL):
        same_run = (pltpu.roll(seq_t, lag, 0) == seq_t) & (place_t >= lag)
        lag_mask[lag - 1] = same_run.astype(jnp.float32)
    first = lax.broadcasted_iota(jnp.int32, (rows, rows), 0)
    second = lax.broadcasted_iota(jnp.int32, (rows, rows), 1)
    lower = first >= second
    same = lower & (seq_col == seq_wide)
    lanes = lax.broadcasted_iota(jnp.int32, (rows, LANES), 1)
    lane = lax.broadcasted_iota(jnp.int32, (1, LANES), 1)
    at_conv = D * HEADS // LANES
    at_heads = at_conv + (KERNEL + 1) * CHANNELS // LANES
    head_row = small[at_heads : at_heads + 1, :]
    own_head = lane < HEADS
    dt_bias = jnp.where(own_head, head_row, 0.0)
    a_log = jnp.where(own_head, pltpu.roll(head_row, LANES - HEADS, 1), 0.0)

    def tap(number, block):
        place = at_conv + number * (CHANNELS // LANES) + block
        return small[place : place + 1, :]

    def gain_row(block):
        here = small[at_heads + block : at_heads + block + 2, :]
        moved = pltpu.roll(here, LANES - SHIFT, 1)
        return jnp.where(lane < LANES - SHIFT, moved[0:1], moved[1:2])

    def skip_row(block):
        first_lane = 2 * HEADS + PER * block
        sides = [head_row[:, first_lane + i : first_lane + i + 1] for i in range(PER)]
        return jnp.where(lane < HEAD_DIM, sides[0], sides[1])

    turn = 16 * HEADS // LANES
    spots = D // 16
    lane_wide = lax.broadcasted_iota(jnp.int32, (spots, LANES), 1)
    for number in range(16):
        place, off = number * HEADS // LANES, number * HEADS % LANES
        piece = pltpu.roll(small[pl.ds(place, spots, stride=turn), :], (LANES - off) % LANES, 1)
        if off + HEADS > LANES:
            after = pltpu.roll(small[pl.ds(place + 1, spots, stride=turn), :], LANES - off, 1)
            piece = jnp.where(lane_wide < LANES - off, piece, after)
        w_dt_wide[pl.ds(number, spots, stride=16), :] = jnp.where(lane_wide < HEADS, piece, 0.0)
    w_dt = w_dt_wide[...].astype(half)
    gain_in = jnp.concatenate([gain[j : j + 1, :] for j in range(ROWS_GAIN)], 1)
    x = tokens[...].astype(jnp.float32)
    scale_in = lax.rsqrt(row_sum(x * x) * (1.0 / D) + EPS)
    normed_full = x * scale_in * gain_in
    normed[...] = normed_full.astype(half)
    for j in range(D // LANES):
        spot = slice(j * LANES, (j + 1) * LANES)
        normed_t[spot, :] = normed_full[:, spot].T.astype(half)
    live[...] = jnp.where(seq_col[:, 0:1] >= 0, cot[...].astype(jnp.float32), 0.0).astype(half)

    def project(pair):
        both = matmul(normed[...], w_main[:, pair * 2 * LANES : (pair + 1) * 2 * LANES])
        proj[2 * pair] = both[:, :LANES]
        proj[2 * pair + 1] = both[:, LANES:]

    def back_out(pair):
        both = against(live[...], w_out[pair * 2 * LANES : (pair + 1) * 2 * LANES, :])
        grad_hidden[2 * pair] = both[:, :LANES]
        grad_hidden[2 * pair + 1] = both[:, LANES:]

    raw = matmul(normed[...], w_dt) + dt_bias
    steps = jnp.maximum(raw, 0.0) + jnp.log1p(jnp.exp(-jnp.abs(raw)))
    rate = -jnp.exp(a_log)
    logs = exact(lower.astype(jnp.float32), steps * rate)
    logs_t = logs.T
    steps_t = steps.T

    def convolve(block):
        inside = proj[BLOCKS + block]
        total = tap(KERNEL, block) + tap(KERNEL - 1, block) * inside
        for lag in range(1, KERNEL):
            total = total + tap(KERNEL - 1 - lag, block) * (pltpu.roll(inside, lag, 0) * lag_mask[lag - 1])
        gate = jax.nn.sigmoid(total)
        value = total * gate
        active[block] = value
        slope[block] = gate + value * (1.0 - gate)

    project(BLOCKS)
    convolve(BLOCKS)
    convolve(BLOCKS + 1)
    b_mat, c_mat = active[BLOCKS], active[BLOCKS + 1]
    scores = lax.dot_general(
        c_mat, b_mat, (((1,), (1,)), ((), ())), preferred_element_type=jnp.float32, precision=HIGHEST
    )
    squares = jnp.zeros((rows, LANES), jnp.float32)
    cross = jnp.zeros((rows, LANES), jnp.float32)
    for pair in range(BLOCKS // 2):
        project(BLOCKS // 2 + pair)
        project(pair)
        back_out(pair)
        for block in (2 * pair, 2 * pair + 1):
            convolve(block)
            value = active[block]
            parts = []
            for side in range(PER):
                head = PER * block + side
                gap = logs[:, head : head + 1] - logs_t[head : head + 1, :]
                fall = jnp.exp(jnp.where(same, gap, -1e30))
                factor[head] = fall
                mix = ((fall * scores) * steps_t[head : head + 1, :]).astype(half)
                mixed[head] = mix
                parts.append(mix)
            low = value.astype(half)
            zero = jnp.zeros_like(low)
            left = lanes < HEAD_DIM
            stacked = jnp.concatenate(
                [jnp.where(left, low, zero), jnp.where(left, zero, low)], 0
            )
            inside = matmul(jnp.concatenate(parts, 1), stacked)
            total = inside + skip_row(block) * value
            gate = proj[block]
            out = total * (gate * jax.nn.sigmoid(gate))
            scanned[block] = total
            gated[block] = out
            squares = squares + out * out
            cross = cross + out * (grad_hidden[block] * gain_row(block))
    scale = lax.rsqrt(row_sum(squares) * (1.0 / INNER) + EPS)
    pull = row_sum(cross) * (scale * scale * scale) * (1.0 / INNER)
    scale_w = jnp.broadcast_to(scale, (rows, LANES))
    pull_w = jnp.broadcast_to(pull, (rows, LANES))

    def unconvolve(block, grad_active):
        grad = grad_active * slope[block]
        inside = proj[BLOCKS + block]
        total = tap(KERNEL - 1, block) * grad

        def keep(number, row):
            place = START_SMALL + at_conv + number * (CHANNELS // LANES) + block
            main[place : place + 1, :] = row

        keep(KERNEL, col_sum(grad))
        keep(KERNEL - 1, col_sum(grad * inside))
        for lag in range(1, KERNEL):
            kept = grad * lag_mask[lag - 1]
            keep(KERNEL - 1 - lag, col_sum(kept * pltpu.roll(inside, lag, 0)))
            total = total + tap(KERNEL - 1 - lag, block) * pltpu.roll(kept, rows - lag, 0)
        grad_proj[:, INNER + block * LANES : INNER + (block + 1) * LANES] = total.astype(half)

    skip_grad = jnp.zeros((1, LANES), jnp.float32)
    grad_scores = jnp.zeros((rows, rows), jnp.float32)
    row_part = jnp.zeros((rows, LANES), jnp.float32)
    cols[...] = jnp.zeros((LANES, rows), jnp.float32)
    for block in range(BLOCKS):
        span = slice(block * LANES, (block + 1) * LANES)
        out, total, gate, value = gated[block], scanned[block], proj[block], active[block]
        down = grad_hidden[block]
        unit = out * scale_w
        row_gain = gain_row(block)
        hidden[:, span] = (unit * row_gain).astype(half)
        hidden_t[span, :] = (unit * row_gain).T.astype(half)
        turned[block + 1 : block + 2, :] = pltpu.roll(col_sum(down * unit), SHIFT, 1)
        grad_gated = (down * row_gain) * scale_w - out * pull_w
        sig = jax.nn.sigmoid(gate)
        silu = gate * sig
        grad_total = grad_gated * silu
        grad_proj[:, span] = (grad_gated * total * (sig + silu * (1.0 - sig))).astype(half)
        skip_sums = col_sum(grad_total * value)
        for side in range(PER):
            inside_side = (lane >= side * HEAD_DIM) & (lane < (side + 1) * HEAD_DIM)
            amount = row_sum(jnp.where(inside_side, skip_sums, 0.0))
            skip_grad = jnp.where(lane == 2 * HEADS + PER * block + side, amount, skip_grad)
        low = grad_total.astype(half)
        zero = jnp.zeros_like(low)
        left = lanes < HEAD_DIM
        values_low = value.astype(half)
        tops = jnp.concatenate([jnp.where(left, low, zero), jnp.where(left, zero, low)], 0)
        grad_mix = against(tops, values_low)
        for side in range(PER):
            head = PER * block + side
            through = grad_mix[side * rows : (side + 1) * rows] * factor[head]
            scored = through * scores
            step = steps_t[head : head + 1, :]
            cols[head : head + 1, :] = col_sum(scored)
            row_part = jnp.where(lanes == head, row_sum(scored * step), row_part)
            grad_scores = grad_scores + through * step
        both = over_rows(jnp.concatenate([mixed[PER * block], mixed[PER * block + 1]], 0), tops)
        unconvolve(block, both + skip_row(block) * grad_total)
    low_scores = grad_scores.astype(half)
    unconvolve(BLOCKS + 1, matmul(low_scores, b_mat.astype(half)))
    unconvolve(BLOCKS, over_rows(low_scores, c_mat.astype(half)))
    col_part = cols[...].T
    upper = (first <= second).astype(jnp.float32)
    grad_decay = exact(upper, row_part - col_part * steps)
    grad_steps = col_part + grad_decay * rate
    grad_raw = grad_steps * jax.nn.sigmoid(raw)
    bias_grad = jnp.where(own_head, col_sum(grad_raw), 0.0)
    log_grad = jnp.where(own_head, col_sum(grad_decay * steps) * rate, 0.0)
    turned[0:1, :] = bias_grad + pltpu.roll(log_grad, HEADS, 1) + skip_grad
    rims = turned[0 : BLOCKS + 1, :]
    at_rims = START_SMALL + at_heads
    lane_rims = lax.broadcasted_iota(jnp.int32, (BLOCKS, LANES), 1)
    main[at_rims : at_rims + BLOCKS, :] = jnp.where(lane_rims < SHIFT, rims[:BLOCKS], rims[1:])
    tail[7:8, :] = rims[BLOCKS:]
    grad_dt = jnp.where(own_head, grad_raw, 0.0).astype(half)
    w_dt_wide[...] = matmul(normed_t[...], grad_dt)
    lines = [jnp.zeros((spots, LANES), jnp.float32) for _ in range(turn)]
    for number in range(16):
        place, off = number * HEADS // LANES, number * HEADS % LANES
        piece = pltpu.roll(w_dt_wide[pl.ds(number, spots, stride=16), :], off, 1)
        lines[place] = jnp.where((lane_wide >= off) & (lane_wide < off + HEADS), piece, lines[place])
        if off + HEADS > LANES:
            lines[place + 1] = jnp.where(lane_wide < off + HEADS - LANES, piece, lines[place + 1])
    for number in range(turn):
        main[pl.ds(START_SMALL + number, spots, stride=turn), :] = lines[number]
    result[...] = (x + matmul(hidden[...], w_out[...])).astype(half)
    back = against(grad_proj[...], w_main[...]) + against(grad_dt, w_dt)
    gain_grad = col_sum(back * (x * scale_in))
    for j in range(ROWS_GAIN):
        main[j : j + 1, :] = gain_grad[:, j * LANES : (j + 1) * LANES]
    pulled = back * gain_in
    push = row_sum(pulled * x) * (scale_in * scale_in * scale_in) * (1.0 / D)
    grad_input[...] = live[...].astype(jnp.float32) + (pulled * scale_in - x * push)


DEPTH = 256
TALL = 96


def packer(near, size_own, normed_t, grad_proj, hidden_t, live, main, tail, flat, data):
    deep, tall, wide = near.grid
    size_plane = tall * wide * 2 * size_own
    mixed_owner = START_OUT // size_own

    def main_block(number, carry):
        left = normed_t[pl.ds(pl.multiple_of(number * DEPTH, DEPTH), DEPTH), :]
        for pair in range(WIDE // 2):
            both = matmul(left, grad_proj[:, pair * 2 * LANES : (pair + 1) * 2 * LANES])
            for side in range(2):
                place = ROWS_GAIN + number * (DEPTH * WIDE) + 2 * pair + side
                main[pl.ds(place, DEPTH, stride=WIDE), :] = both[:, side * LANES : (side + 1) * LANES]
        return carry

    def out_block(number, carry):
        left = hidden_t[pl.ds(pl.multiple_of(number * DEPTH, DEPTH), DEPTH), :]
        for pair in range(THIN // 2):
            both = matmul(left, live[:, pair * 2 * LANES : (pair + 1) * 2 * LANES])
            for side in range(2):
                place = 8 + number * (DEPTH * THIN) + 2 * pair + side
                tail[pl.ds(place, DEPTH, stride=THIN), :] = pltpu.roll(
                    both[:, side * LANES : (side + 1) * LANES], SHIFT, 1
                )
        return carry

    kinds = (
        (main_block, ROWS_GAIN, DEPTH * WIDE, DEPTH * WIDE, D // DEPTH),
        (out_block, START_OUT, DEPTH * THIN, DEPTH * THIN + 1, INNER // DEPTH),
    )

    def joined(rows):
        early = lax.broadcasted_iota(jnp.int32, (rows.shape[0] - 8, LANES), 1) < SHIFT
        return jnp.where(early, rows[7 : rows.shape[0] - 1], rows[8:])

    def cast(step, plane):
        yi, rest = lax.div(step, wide * 2), lax.rem(step, wide * 2)
        xi, ci = lax.div(rest, 2), lax.rem(rest, 2)
        owner = plane * (tall * wide * 2) + step
        base = owner * size_own
        if size_own % 8 == 0:
            base = pl.multiple_of(base, 8)

        @pl.when(owner < mixed_owner)
        def _():
            data[plane, yi, xi, ci] = flat[pl.ds(base, size_own), :].astype(jnp.bfloat16)

        @pl.when(owner > mixed_owner)
        def _():
            data[plane, yi, xi, ci] = joined(flat[pl.ds(base, size_own + 8), :]).astype(jnp.bfloat16)

        @pl.when(owner == mixed_owner)
        def _():
            first = mixed_owner * size_own
            under = START_OUT - first
            after = joined(flat[START_OUT : first + size_own + 8, :])
            both = jnp.concatenate([flat[first:START_OUT, :], after], 0) if under else after
            data[plane, yi, xi, ci] = both.astype(jnp.bfloat16)

        return plane

    def pack_plane(plane):
        low = plane * size_plane
        for body, base, step, reach, count in kinds:
            begin = jnp.clip(lax.div(low - base - reach + step * (count + 1), step) - count, 0, count)
            end = jnp.clip(lax.div(low + size_plane - base + step * (count + 1) - 1, step) - count, 0, count)
            lax.fori_loop(begin, jnp.maximum(begin, end), body, 0)
        lax.fori_loop(0, tall * wide * 2, cast, plane)

    return pack_plane


def whole_kernel(
    grid, cuts, params_far, tokens_far, cot_far, seq_row, result, grad_input, most, last,
    params, tokens, cot, near_sem, w_main, w_out, small, gain, own, data, flat, gather_send, gather_recv, scatter_send, scatter_recv,
    normed, grad_proj, hidden, live, w_dt_wide, normed_t, hidden_t,
    proj, slope, active, scanned, gated, grad_hidden, factor, mixed, cols, lag_mask, turned, *refs,
):
    near = Neighbours(grid)
    fetches = [
        pltpu.make_async_copy(far, here, near_sem.at[number])
        for number, (far, here) in enumerate(((params_far, params), (tokens_far, tokens), (cot_far, cot)))
    ]
    for fetch in fetches:
        fetch.start()
    near.meet()
    fetches[0].wait()
    gather_part(near, cuts, params, w_main, w_out, small, gain, own, data, flat, gather_send, gather_recv)
    main = flat.at[0:START_OUT]
    tail = flat.at[START_OUT : flat.shape[0]]
    for fetch in fetches[1:]:
        fetch.wait()
    mixer_part(
        tokens, cot, seq_row, gain, small, w_main, w_out, result, grad_input,
        normed, grad_proj, hidden, live, w_dt_wide, normed_t, hidden_t,
        proj, slope, active, scanned, gated, grad_hidden, factor, mixed, cols, lag_mask, turned, main, tail,
    )
    rest = flat.shape[0] - START_OUT - 8 - ROWS_OUT
    flat[START_OUT + 8 + ROWS_OUT :, :] = jnp.zeros((rest, LANES), jnp.float32)
    pack_plane = packer(near, own.shape[0], normed_t, grad_proj, hidden_t, live, main, tail, flat, data)
    scatter_part(near, cuts, pack_plane, data, most, last, scatter_send, scatter_recv, refs)


def run_block(tokens, cotangent, seq_ids, params, group_count, wide_count):
    rows, own_rows = tokens.shape[0], params.shape[0]
    deep, tall, wide = grid = slice_grid(group_count, wide_count)
    cuts = slice_cuts(own_rows)
    f32, half = jnp.float32, jnp.bfloat16
    vmem = pl.BlockSpec(memory_space=pltpu.VMEM)
    shape = jax.ShapeDtypeStruct
    block = (rows, LANES)
    flat_rows = wide_count * group_count * own_rows
    sems = pltpu.SemaphoreType.DMA((deep * len(cuts), wide + tall))
    return pl.pallas_call(
        functools.partial(whole_kernel, grid, cuts),
        out_shape=(
            shape((rows, D), half),
            shape((rows, D), f32),
            shape((own_rows, LANES), f32),
            shape((own_rows, LANES), half),
        ),
        in_specs=[pl.BlockSpec(memory_space=pl.ANY)] * 3 + [vmem],
        out_specs=(vmem,) * 4,
        scratch_shapes=[
            pltpu.VMEM((own_rows, LANES), f32),
            pltpu.VMEM((rows, D), half),
            pltpu.VMEM((rows, D), half),
            pltpu.SemaphoreType.DMA((3,)),
            pltpu.VMEM((D, INNER + CHANNELS), half),
            pltpu.VMEM((INNER, D), half),
            pltpu.VMEM((-(-ROWS_SMALL // 8) * 8, LANES), f32),
            pltpu.VMEM((8, LANES), f32),
            pltpu.VMEM((own_rows, LANES), half),
            pltpu.VMEM((deep, tall, wide, 2, own_rows, LANES), half),
            pltpu.VMEM((flat_rows + 16, LANES), f32),
            sems,
            sems,
            sems,
            sems,
            pltpu.VMEM((rows, D), half),
            pltpu.VMEM((rows, INNER + CHANNELS), half),
            pltpu.VMEM((rows, INNER), half),
            pltpu.VMEM((rows, D), half),
            pltpu.VMEM((D, LANES), f32),
            pltpu.VMEM((D, rows), half),
            pltpu.VMEM((INNER, rows), half),
            pltpu.VMEM((WIDE, *block), f32),
            pltpu.VMEM((BLOCKS + 2, *block), f32),
            pltpu.VMEM((BLOCKS + 2, *block), f32),
            pltpu.VMEM((BLOCKS, *block), f32),
            pltpu.VMEM((BLOCKS, *block), f32),
            pltpu.VMEM((BLOCKS, *block), f32),
            pltpu.VMEM((HEADS, rows, rows), f32),
            pltpu.VMEM((HEADS, rows, rows), half),
            pltpu.VMEM((LANES, rows), f32),
            pltpu.VMEM((KERNEL - 1, *block), f32),
            pltpu.VMEM((16, LANES), f32),
        ]
        + scatter_scratch(grid, cuts),
        compiler_params=pltpu.CompilerParams(
            collective_id=0, has_side_effects=True, vmem_limit_bytes=60 * 1024 * 1024
        ),
    )(params, tokens, cotangent, seq_ids[None, :])


def adamw(weight, first, second, grad, step_count):
    steps_done = step_count[0].astype(jnp.float32)
    first_new = BETA_ONE * first + (1.0 - BETA_ONE) * grad
    second_new = BETA_TWO * second + (1.0 - BETA_TWO) * grad * grad
    first_hat = first_new / (1.0 - jnp.power(BETA_ONE, steps_done))
    second_hat = second_new / (1.0 - jnp.power(BETA_TWO, steps_done))
    weight_new = weight - LEARN_RATE * (
        first_hat / (jnp.sqrt(second_hat) + ADAM_EPS) + WEIGHT_DECAY * weight
    )
    return (weight_new, first_new, second_new)


def per_device(tokens, cotangent, seq_ids, params, first_moment, second_moment, step_count):
    width = params.shape[0]
    result, grad_input, most, last = run_block(
        tokens,
        cotangent,
        seq_ids,
        params.reshape(width // LANES, LANES),
        lax.axis_size("shard"),
        lax.axis_size("dp"),
    )
    owned = (most + last.astype(jnp.float32)).reshape(width)
    new_weight, new_first, new_second = adamw(
        params, first_moment, second_moment, owned, step_count
    )
    return (result, grad_input, owned, new_weight, new_first, new_second)


def solution(mesh):
    return jax.shard_map(
        per_device,
        mesh=mesh,
        in_specs=(
            P(("dp", "shard"), None),
            P(("dp", "shard"), None),
            P(("dp", "shard")),
            P(("dp", "shard")),
            P(("dp", "shard")),
            P(("dp", "shard")),
            P(),
        ),
        out_specs=(
            P(("dp", "shard"), None),
            P(("dp", "shard"), None),
            P(("dp", "shard")),
            P(("dp", "shard")),
            P(("dp", "shard")),
            P(("dp", "shard")),
        ),
        check_vma=False,
    )
```
